256 devices in a mesh: ctx: 64 (over y_hi, z, x), tp: 4 (over y_lo, core).
Axes of the slice: x: 4, y: 4 (y_hi: 2, y_lo: 2; y = y_hi * 2 + y_lo), z: 8, core: 2. Of those that a mesh axis runs over, the one named last changes fastest.
Arguments:
- ids: int32 [32768], P('ctx'), may hold values from 0 to 511
- embed_table: bfloat16 [512, 4096], P(None, 'tp'), may hold values from -126 to 126
- norm_gain: float32 [4096], replicated, may hold values from 0.1 to 1.9
- in_weight: bfloat16 [3, 4096, 4096], P(None, 'ctx', 'tp'), may hold values from -0.09375 to 0.09375
- in_scale: float32 [3, 4096], P(None, 'tp'), may hold values from 0.1 to 1.9
- short_filter: float32 [3, 7, 4096], P(None, None, 'tp'), may hold values from -2.4 to 2.4
- long_filter: float32 [128, 256], P(None, 'tp'), may hold values from -0.9 to 0.9
- decay: float32 [256], P('tp'), may hold values from 0.003 to 0.1
Outputs:
- mixed: bfloat16 [32768, 4096], P('ctx', 'tp')
The draws below stay inside these ranges and needn't reach their ends.
All inputs are finite; a program needn't handle non-finite values.
Results may differ from the reference program's by a relative error of at most 0.009.
Values may be sent and summed in bfloat16 or wider, within the bound.
No kernel may reach another device: no remote copies, remote signals or barrier semaphores. Data moves between devices by JAX's collectives and lax.ppermute only.
A program may use at most 128 MiB of HBM per device.

```python
import math
import jax
import jax.numpy as jnp
from jax import lax

D = 4096
V = 512
GROUP = 16
SHORT_TAPS = 7
LONG_TAPS = 128
TOKENS = 32768
GROUPS = 256


def draw_embed_table(key, part):
    key = jax.random.fold_in(key, 11)
    kbase, krows, kcols = jax.random.split(key, 3)
    rows = jnp.exp(jax.random.uniform(krows, (V, 1), jnp.float32) * math.log(10.0))
    ramp = jnp.exp(jnp.arange(D, dtype=jnp.float32)[None, :] / (D - 1) * math.log(3.0))
    cols = ramp * jnp.exp(jax.random.uniform(kcols, (1, D), jnp.float32) * math.log(3.5))
    base = jnp.clip(jax.random.normal(kbase, (V, D), jnp.float32), -4.0, 4.0)
    return (0.3 * base * rows * cols).astype(jnp.bfloat16)


def with_ends(values, stream_key, least, high):
    place = [jax.random.randint(jax.random.fold_in(stream_key, axis), (), 0, length) for axis, length in enumerate(values.shape)]
    widest = values.shape.index(max(values.shape))
    next_to = place[:widest] + [(place[widest] + 1) % values.shape[widest]] + place[widest + 1:]
    return values.at[tuple(place)].set(least).at[tuple(next_to)].set(high)


def block_scale(stream_key, extent, cuts, low, largest):
    def one(axis_at, shards_of):
        steps = jax.random.uniform(jax.random.fold_in(jax.random.fold_in(stream_key, 6), axis_at), (shards_of,), jnp.float32, low / len(cuts), largest / len(cuts))
        return jnp.repeat(jnp.exp(steps), extent[axis_at] // shards_of).reshape((-1,) + (1,) * (len(extent) - axis_at - 1))

    factor_of = one(*cuts[0])
    for cut in cuts[1:]:
        factor_of = factor_of * one(*cut)
    return factor_of


def scatter_about(stream_key, dims, width, most, shards=(), held_as=jnp.bfloat16):
    result = jax.random.normal(stream_key, dims, jnp.float32) * width
    if len(shards) > 0:
        result = block_scale(stream_key, dims, shards, -0.22, 0.18) * result
    return jnp.clip(result, min=-most, max=most).astype(held_as)


def setup_inputs(seed: int = 0) -> dict:
    keys = jax.random.split(jax.random.key(seed), 9)
    return {
        "ids": with_ends(jax.random.randint(keys[0], (TOKENS,), 0, V), jax.random.fold_in(keys[0], 1), 0, V - 1).astype(jnp.int32),
        "embed_table": draw_embed_table(jax.random.fold_in(keys[8], 71), 0),
        "norm_gain": jnp.clip(1.0 + 0.18 * jax.random.normal(keys[2], (D,), jnp.float32), 0.1, 1.9),
        "in_weight": scatter_about(keys[3], (3, D, D), D ** -0.5, 0.09375, ((1, 64), (2, 4))),
        "in_scale": jnp.clip(1.0 + 0.18 * jax.random.normal(keys[4], (3, D), jnp.float32), 0.1, 1.9),
        "short_filter": scatter_about(keys[5], (3, SHORT_TAPS, D), 0.4, 2.4, ((2, 4),), jnp.float32),
        "long_filter": scatter_about(keys[6], (LONG_TAPS, GROUPS), 0.15, 0.9, ((1, 4),), jnp.float32),
        "decay": jnp.clip(jnp.exp(math.log(0.1) - 3.506558 * jax.random.uniform(keys[7], (GROUPS,), jnp.float32) ** block_scale(keys[7], (GROUPS,), ((0, 4),), -0.2, 0.2)), 0.003, 0.1),
    }


def toeplitz(long_filter, decay):
    steps = jnp.arange(LONG_TAPS, dtype=jnp.float32)
    taps = (long_filter * jnp.exp(-decay[None, :] * steps[:, None])).astype(jnp.bfloat16).astype(jnp.float32)
    offset = jnp.arange(LONG_TAPS, dtype=jnp.int32)[:, None] - jnp.arange(LONG_TAPS, dtype=jnp.int32)[None, :]
    lower = jnp.take(taps, jnp.clip(offset, 0, LONG_TAPS - 1), axis=0)
    upper = jnp.take(taps, jnp.clip(offset + LONG_TAPS, 0, LONG_TAPS - 1), axis=0)
    toep_near = jnp.where((offset >= 0)[:, :, None], lower, 0.0)
    toep_far = jnp.where((offset < 0)[:, :, None], upper, 0.0)
    return (toep_near, toep_far)

def short_conv(stream, filt):
    values = stream.astype(jnp.float32)
    total = jnp.zeros(values.shape, jnp.float32)
    for k in range(SHORT_TAPS):
        total = total + filt[k][None, :] * jnp.roll(values, k, axis=0)
    return total

def reference(ids, embed_table, norm_gain, in_weight, in_scale, short_filter, long_filter, decay):
    x = embed_table[ids].astype(jnp.float32)
    meansq = lax.optimization_barrier(jnp.mean(x * x, axis=1, keepdims=True))
    normed = (x * lax.rsqrt(meansq + 1e-06) * norm_gain[None, :]).astype(jnp.bfloat16)
    streams = []
    for p in range(3):
        proj = (jnp.dot(normed, in_weight[p], preferred_element_type=jnp.float32) * in_scale[p][None, :]).astype(jnp.bfloat16)
        streams.append(short_conv(proj, short_filter[p]))
    inner = (streams[1] * streams[2]).astype(jnp.bfloat16)
    blocks = inner.astype(jnp.float32).reshape(TOKENS // LONG_TAPS, LONG_TAPS, GROUPS, GROUP)
    before = jnp.roll(blocks, 1, axis=0)
    toep_near, toep_far = toeplitz(long_filter, decay)
    conv = jnp.einsum('tsg,bsgc->btgc', toep_near, blocks, precision=lax.Precision.HIGHEST)
    conv = conv + jnp.einsum('tsg,bsgc->btgc', toep_far, before, precision=lax.Precision.HIGHEST)
    conv = conv.reshape(TOKENS, D)
    return (streams[0] * conv).astype(jnp.bfloat16)
```

```python
import jax
import jax.numpy as jnp
import numpy as np
from jax import lax
from jax.experimental import pallas as pl
from jax.experimental.pallas import tpu as pltpu
from jax.sharding import Mesh, PartitionSpec as P

GROUP = 16
SHORT_TAPS = 7
LONG_TAPS = 128
LANES = 128
HALO = 144
STREAMS = 3
BF = jnp.bfloat16
F32 = jnp.float32


def shifted(value, axis, steps):
    count = lax.axis_size(axis)
    pairs = [(source, (source + steps) % count) for source in range(count)]
    return lax.ppermute(value, axis, pairs)


def partial_kernel(normed_ref, pieces_ref, out_ref, weight_ref):
    rows = weight_ref.shape[0] // pieces_ref.shape[0]
    for source in range(pieces_ref.shape[0]):
        for p in range(STREAMS):
            weight_ref[source * rows : (source + 1) * rows, p * LANES : (p + 1) * LANES] = (
                pieces_ref[source, p * rows : (p + 1) * rows, :]
            )
    out_ref[...] = jnp.dot(
        normed_ref[...], weight_ref[...], preferred_element_type=F32
    ).astype(BF)


def partial_table(normed, pieces, rows):
    vocab, depth = normed.shape
    return pl.pallas_call(
        partial_kernel,
        out_shape=jax.ShapeDtypeStruct((vocab, STREAMS * LANES), BF),
        in_specs=[pl.BlockSpec(memory_space=pltpu.VMEM)] * 2,
        out_specs=pl.BlockSpec(memory_space=pltpu.VMEM),
        scratch_shapes=[pltpu.VMEM((depth, STREAMS * LANES), BF)],
        cost_estimate=pl.CostEstimate(
            flops=2 * vocab * depth * STREAMS * LANES, bytes_accessed=1500000, transcendentals=0
        ),
        name="partial_table",
    )(normed, pieces)


def toeplitz_kernel(taps_ref, out_ref):
    for g in range(taps_ref.shape[0]):
        row = jnp.broadcast_to(taps_ref[g : g + 1, :], (LONG_TAPS, 2 * LONG_TAPS))
        out_ref[g * LONG_TAPS : (g + 1) * LONG_TAPS, :] = pltpu.roll(
            row, 0, 1, stride=1, stride_axis=0
        ).astype(BF)


def toeplitz(taps_row):
    groups = taps_row.shape[0]
    return pl.pallas_call(
        toeplitz_kernel,
        out_shape=jax.ShapeDtypeStruct((groups * LONG_TAPS, 2 * LONG_TAPS), BF),
        in_specs=[pl.BlockSpec(memory_space=pltpu.VMEM)],
        out_specs=pl.BlockSpec(memory_space=pltpu.VMEM),
        cost_estimate=pl.CostEstimate(flops=1000000, bytes_accessed=530000, transcendentals=0),
        name="toeplitz",
    )(taps_row)


def mix_kernel(tile_ref, ids_ref, *refs):
    tables = refs[:8]
    filt_ref, toep_ref, out_ref, table_ref, proj_ref, inner_ref = refs[8:]
    piece = tables[0].shape[0]
    vocab = table_ref.shape[0]
    extent = ids_ref.shape[1]
    tokens = out_ref.shape[1]

    @pl.when(pl.program_id(0) == 0)
    def _():
        for j in range(8):
            table_ref[j * piece : (j + 1) * piece, :] = tables[j][...]

    hot = ids_ref[0] == lax.broadcasted_iota(jnp.int32, (extent, vocab), 1)
    proj = jnp.dot(
        jnp.where(hot, 1.0, 0.0).astype(BF), table_ref[...], preferred_element_type=F32
    )
    for p in range(STREAMS):
        proj_ref[p] = proj[:, p * LANES : (p + 1) * LANES]

    def short(p, start):
        total = jnp.zeros((extent - start, LANES), F32)
        for k in range(SHORT_TAPS):
            total = total + filt_ref[p, k : k + 1, :] * proj_ref[p, start - k : extent - k, :]
        return total

    first = HALO - LONG_TAPS
    inner_ref[...] = (short(1, first) * short(2, first)).astype(BF)
    gate = short(0, HALO)
    lane_group = lax.broadcasted_iota(jnp.int32, (LONG_TAPS, LANES), 1) // GROUP
    for pair in range(tokens // (2 * LONG_TAPS)):
        base = pair * 2 * LONG_TAPS
        window = jnp.concatenate(
            [
                inner_ref[base : base + 2 * LONG_TAPS, :],
                inner_ref[base + LONG_TAPS : base + 3 * LONG_TAPS, :],
            ],
            axis=1,
        )
        full = jnp.dot(toep_ref[...], window, preferred_element_type=F32)
        for half in range(2):
            conv = full[:LONG_TAPS, half * LANES : (half + 1) * LANES]
            for g in range(1, LANES // GROUP):
                conv = jnp.where(
                    lane_group == g,
                    full[g * LONG_TAPS : (g + 1) * LONG_TAPS, half * LANES : (half + 1) * LANES],
                    conv,
                )
            at = base + half * LONG_TAPS
            out_ref[0, at : at + LONG_TAPS, :] = (gate[at : at + LONG_TAPS] * conv).astype(BF)


def mixed_blocks(tile, windows, tables, short_filter, toep):
    blocks, extent, _ = windows.shape
    tokens = extent - HALO
    vocab = 8 * tables[0].shape[0]
    whole = pl.BlockSpec(tables[0].shape, lambda i, t: (0, 0))
    return pl.pallas_call(
        mix_kernel,
        out_shape=jax.ShapeDtypeStruct((blocks, tokens, LANES), BF),
        grid_spec=pltpu.PrefetchScalarGridSpec(
            num_scalar_prefetch=1,
            grid=(blocks,),
            in_specs=[pl.BlockSpec((1, extent, 1), lambda i, t: (i, 0, 0))]
            + [whole] * 8
            + [
                pl.BlockSpec((STREAMS, SHORT_TAPS, LANES), lambda i, t: (0, 0, t[0])),
                pl.BlockSpec(toep.shape, lambda i, t: (0, 0)),
            ],
            out_specs=pl.BlockSpec((1, tokens, LANES), lambda i, t: (i, 0, 0)),
            scratch_shapes=[
                pltpu.VMEM((vocab, STREAMS * LANES), BF),
                pltpu.VMEM((STREAMS, extent, LANES), F32),
                pltpu.VMEM((tokens + LONG_TAPS, LANES), BF),
            ],
        ),
        cost_estimate=pl.CostEstimate(
            flops=5000000000, bytes_accessed=4000000, transcendentals=0
        ),
        name="mixed_blocks",
    )(tile, windows, *tables, short_filter, toep)


def per_device(ids, embed_table, norm_gain, in_weight, in_scale, short_filter, long_filter, decay):
    tokens = ids.shape[0]
    vocab, width_local = embed_table.shape
    rows = in_weight.shape[1]
    spread = ("yh", "x")
    tiles = width_local // LANES
    z = lax.axis_index("z")
    yl = lax.axis_index("yl")
    core = lax.axis_index("core")
    tile = lax.axis_index("yh") * 4 + lax.axis_index("x")
    z_count = lax.axis_size("z")

    chunk = 4 * rows
    own = lax.dynamic_slice_in_dim(embed_table, (z % 4) * chunk, chunk, 1)
    tp = ("z", "yl", "core")

    def spot(zi, yi, ci):
        return (zi * 2 + yi) * 2 + ci

    holders = [(zi, yi, zi // 4) for zi in range(z_count) for yi in range(2)]
    to_core = [(spot(a, b, c), spot(a, b, 1 - c)) for a, b, c in holders]
    to_chip = [(spot(a, b, c), spot(a, 1 - b, c)) for a, b, c in holders]
    to_both = [(spot(a, b, c), spot(a, 1 - b, 1 - c)) for a, b, c in holders]
    got_core = lax.ppermute(own, tp, to_core)
    got_chip = lax.ppermute(own, tp, to_chip)
    got_both = lax.ppermute(own, tp, to_both)
    local_f = embed_table.astype(F32)
    squares = jnp.sum(local_f * local_f, axis=1)
    others = [shifted(squares, ("yl", "core"), s) for s in (1, 2, 3)]

    by_tile = in_weight.reshape(STREAMS * rows, tiles, LANES).transpose(1, 0, 2)
    coded = jnp.concatenate([ids >> 4, ids & 15]).astype(BF).reshape(1, -1, LANES)
    load = jnp.concatenate(
        [by_tile, jnp.broadcast_to(coded, (tiles,) + coded.shape[1:])], axis=1
    )
    pieces = lax.all_to_all(load, spread, 0, 0, tiled=True)

    total = squares + others[0] + others[1] + others[2]
    mine = core == z // 4
    near = jnp.where(mine, own, got_core)
    far = jnp.where(mine, got_chip, got_both)
    low = jnp.where(yl == 0, near, far)
    high = jnp.where(yl == 0, far, near)
    features = jnp.concatenate([low, high], axis=1).astype(F32)
    full_width = norm_gain.shape[0]
    gain = jnp.concatenate(
        [
            lax.dynamic_slice_in_dim(norm_gain, z * chunk, chunk, 0),
            lax.dynamic_slice_in_dim(norm_gain, full_width // 2 + z * chunk, chunk, 0),
        ]
    )
    normed = (features * lax.rsqrt(total[:, None] / full_width + 1e-06) * gain[None, :]).astype(BF)

    partial = partial_table(normed, pieces, rows)
    swapped = lax.all_to_all(
        partial.reshape(z_count, vocab // z_count, STREAMS * LANES), "z", 0, 0, tiled=True
    )
    scale = lax.dynamic_slice_in_dim(in_scale, tile * LANES, LANES, 1).reshape(1, STREAMS * LANES)
    piece = (jnp.sum(swapped.astype(F32), axis=0) * scale).astype(BF)
    ups, downs = [piece], []
    for _ in range(4):
        ups.append(shifted(ups[-1], "z", 1))
    last = piece
    for _ in range(3):
        last = shifted(last, "z", -1)
        downs.append(last)
    tables = ups + downs[::-1]

    got = pieces[:, STREAMS * rows :, :].astype(jnp.int32).reshape(tiles, 2, tokens)
    block_ids = got[:, 0] * 16 + got[:, 1]
    tails = block_ids[:, tokens - HALO :]
    edges = jnp.stack([tails[3], tails[7]])
    before = shifted(edges, "z", 1)
    before = jnp.where(z == 0, before[::-1], before)
    lead = jnp.concatenate([before[:1], tails[0:3], before[1:], tails[4:7]], axis=0)
    windows = jnp.concatenate([lead, block_ids], axis=1)
    share = vocab // z_count
    windows = ((z - windows // share) % z_count) * share + windows % share

    groups = LANES // GROUP
    steps = jnp.arange(LONG_TAPS, dtype=F32)
    filt = lax.dynamic_slice_in_dim(long_filter, tile * groups, groups, 1)
    rate = lax.dynamic_slice_in_dim(decay, tile * groups, groups, 0)
    taps = (filt * jnp.exp(-rate[None, :] * steps[:, None])).astype(BF).astype(F32)
    taps_row = jnp.pad(taps[::-1].T, ((0, 0), (1, LONG_TAPS - 1)))

    blocks = mixed_blocks(
        tile.reshape(1).astype(jnp.int32), windows[:, :, None], tables, short_filter,
        toeplitz(taps_row),
    )
    result = lax.all_to_all(blocks, spread, 0, 0, tiled=True)
    return result.transpose(1, 0, 2).reshape(tokens, width_local)


def solution(mesh):
    fine = Mesh(mesh.devices.reshape(2, 8, 4, 2, 2), ("yh", "z", "x", "yl", "core"))
    ctx = ("yh", "z", "x")
    tp = ("yl", "core")
    placed = (
        P(ctx),
        P(None, tp),
        P(),
        P(None, ctx, tp),
        P(None, tp),
        P(None, None, tp),
        P(None, tp),
        P(tp),
    )
    return jax.shard_map(
        per_device, mesh=fine, in_specs=placed, out_specs=P(ctx, tp), check_vma=False
    )
```

```python
import jax
import jax.numpy as jnp
import numpy as np
from jax import lax
from jax.experimental import pallas as pl
from jax.experimental.pallas import tpu as pltpu
from jax.sharding import Mesh, PartitionSpec as P

GROUP = 16
SHORT_TAPS = 7
LONG_TAPS = 128
LANES = 128
HALO = 144
TAIL = 256
STREAMS = 3
BF = jnp.bfloat16
F32 = jnp.float32


def shifted(value, axis, steps):
    count = lax.axis_size(axis)
    pairs = [(source, (source + steps) % count) for source in range(count)]
    return lax.ppermute(value, axis, pairs)


def payload_kernel(weight_ref, ids_ref, tail_ref, out_ref):
    rows = weight_ref.shape[1]
    values = jnp.concatenate(
        [tail_ref[...], ids_ref[...], jnp.zeros((2, LANES), jnp.int32)], axis=0
    )
    coded = jnp.concatenate([values >> 4, values & 15], axis=0).astype(F32).astype(BF)
    for tile in range(out_ref.shape[0]):
        for p in range(STREAMS):
            out_ref[tile, p * rows : (p + 1) * rows, :] = weight_ref[
                p, :, tile * LANES : (tile + 1) * LANES
            ]
        out_ref[tile, STREAMS * rows :, :] = coded


def in_vmem(count):
    return [pl.BlockSpec(memory_space=pltpu.VMEM)] * count


def cost(flops, moved):
    return pl.CostEstimate(flops=flops, bytes_accessed=moved, transcendentals=0)


def payload(in_weight, ids_rows, tail_rows):
    streams, rows, width = in_weight.shape
    return pl.pallas_call(
        payload_kernel,
        out_shape=jax.ShapeDtypeStruct((width // LANES, streams * rows + 16, LANES), BF),
        in_specs=in_vmem(3),
        out_specs=pl.BlockSpec(memory_space=pltpu.VMEM),
        cost_estimate=cost(0, 800000),
        name="payload",
    )(in_weight, ids_rows, tail_rows)


def partial_kernel(flag_ref, own_ref, core_ref, chip_ref, both_ref, pieces_ref, out_ref):
    rows = (pieces_ref.shape[1] - 16) // STREAMS
    half = own_ref.shape[1]
    weight = jnp.concatenate(
        [
            pieces_ref[:, p * rows : (p + 1) * rows, :].reshape(2 * half, LANES)
            for p in range(STREAMS)
        ],
        axis=1,
    )
    mine = flag_ref[0] == 1
    swap = flag_ref[1] == 1
    near = jnp.where(mine, own_ref[...], core_ref[...])
    far = jnp.where(mine, chip_ref[...], both_ref[...])
    features = jnp.concatenate(
        [jnp.where(swap, far, near), jnp.where(swap, near, far)], axis=1
    )
    out_ref[...] = jnp.dot(features, weight, preferred_element_type=F32).astype(BF)


def partial_table(flags, own, got_core, got_chip, got_both, pieces):
    vocab, half = own.shape
    return pl.pallas_call(
        partial_kernel,
        out_shape=jax.ShapeDtypeStruct((vocab, STREAMS * LANES), BF),
        in_specs=[pl.BlockSpec(memory_space=pltpu.SMEM)] + in_vmem(5),
        out_specs=pl.BlockSpec(memory_space=pltpu.VMEM),
        cost_estimate=cost(4 * vocab * half * STREAMS * LANES, 2000000),
        name="partial_table",
    )(flags, own, got_core, got_chip, got_both, pieces)


def toeplitz_kernel(taps_ref, out_ref):
    for g in range(taps_ref.shape[0]):
        row = jnp.broadcast_to(taps_ref[g : g + 1, :], (LONG_TAPS, 2 * LONG_TAPS))
        out_ref[g * LONG_TAPS : (g + 1) * LONG_TAPS, :] = pltpu.roll(
            row, 0, 1, stride=1, stride_axis=0
        ).astype(BF)


def toeplitz(taps_row):
    groups = taps_row.shape[0]
    return pl.pallas_call(
        toeplitz_kernel,
        out_shape=jax.ShapeDtypeStruct((groups * LONG_TAPS, 2 * LONG_TAPS), BF),
        in_specs=in_vmem(1),
        out_specs=pl.BlockSpec(memory_space=pltpu.VMEM),
        cost_estimate=cost(2000000, 1060000),
        name="toeplitz",
    )(taps_row)


def table_kernel(*refs):
    pieces, out_ref = refs[:-1], refs[-1]
    share = pieces[0].shape[0] // 2
    width = pieces[0].shape[1]
    for j, piece in enumerate(pieces):
        for half in range(2):
            out_ref[j * share : (j + 1) * share, half * width : (half + 1) * width] = piece[
                half * share : (half + 1) * share, :
            ]


def joined_table(pieces):
    rows, width = pieces[0].shape
    return pl.pallas_call(
        table_kernel,
        out_shape=jax.ShapeDtypeStruct((len(pieces) * rows // 2, 2 * width), BF),
        in_specs=in_vmem(len(pieces)),
        out_specs=pl.BlockSpec(memory_space=pltpu.VMEM),
        cost_estimate=cost(0, 1600000),
        name="joined_table",
    )(*pieces)


def mix_kernel(spot_ref, ids_ref, table_ref, filt_ref, toep_ref, out_ref, proj_ref, inner_ref):
    block, z, z_count = spot_ref[0], spot_ref[1], spot_ref[2]
    vocab = table_ref.shape[0]
    share = vocab // 8
    tokens = out_ref.shape[0]
    extent = tokens + HALO
    coded = ids_ref[block].astype(F32)
    known = (coded[:8] * 16.0 + coded[8:]).astype(jnp.int32)
    turned = ((z - known // share + z_count) % z_count) * share + known % share
    column = jnp.transpose(turned.astype(F32))
    parts = [column[LANES - (HALO - LANES) :, 0:1]]
    for j in range(1, tokens // LANES + 2):
        parts.append(column[:, j : j + 1])
    wanted = jnp.concatenate(parts, axis=0).astype(jnp.int32)
    hot = wanted == lax.broadcasted_iota(jnp.int32, (extent, vocab), 1)
    proj = jnp.dot(
        jnp.where(hot, 1.0, 0.0).astype(BF), table_ref[...], preferred_element_type=F32
    )
    for part in range(2 * STREAMS):
        proj_ref[part] = proj[:, part * LANES : (part + 1) * LANES]

    first = HALO - LONG_TAPS
    lane_group = lax.broadcasted_iota(jnp.int32, (LONG_TAPS, LANES), 1) // GROUP
    groups = LANES // GROUP
    for half in range(2):

        def short(p, start):
            total = jnp.zeros((extent - start, LANES), F32)
            for k in range(SHORT_TAPS):
                tap = filt_ref[half, p * SHORT_TAPS + k : p * SHORT_TAPS + k + 1, :]
                total = total + tap * proj_ref[half * STREAMS + p, start - k : extent - k, :]
            return total

        inner_ref[half] = (short(1, first) * short(2, first)).astype(BF)
        gate = short(0, HALO)
        for pair in range(tokens // (2 * LONG_TAPS)):
            base = pair * 2 * LONG_TAPS
            window = jnp.concatenate(
                [
                    inner_ref[half, base : base + 2 * LONG_TAPS, :],
                    inner_ref[half, base + LONG_TAPS : base + 3 * LONG_TAPS, :],
                ],
                axis=1,
            )
            full = jnp.dot(
                toep_ref[half * groups * LONG_TAPS : (half + 1) * groups * LONG_TAPS, :],
                window,
                preferred_element_type=F32,
            )
            for side in range(2):
                lanes = slice(side * LANES, (side + 1) * LANES)
                conv = full[:LONG_TAPS, lanes]
                for g in range(1, groups):
                    conv = jnp.where(
                        lane_group == g, full[g * LONG_TAPS : (g + 1) * LONG_TAPS, lanes], conv
                    )
                at = base + side * LONG_TAPS
                out_ref[at : at + LONG_TAPS, half * LANES : (half + 1) * LANES] = (
                    gate[at : at + LONG_TAPS] * conv
                ).astype(BF)


def mixed_block(spot, coded, table, filt, toep, tokens):
    return pl.pallas_call(
        mix_kernel,
        out_shape=jax.ShapeDtypeStruct((tokens, 2 * LANES), BF),
        in_specs=[pl.BlockSpec(memory_space=pltpu.SMEM)] + in_vmem(4),
        out_specs=pl.BlockSpec(memory_space=pltpu.VMEM),
        scratch_shapes=[
            pltpu.VMEM((2 * STREAMS, tokens + HALO, LANES), F32),
            pltpu.VMEM((2, tokens + LONG_TAPS, LANES), BF),
        ],
        cost_estimate=cost(1500000000, 3000000),
        name="mixed_block",
    )(spot, coded, table, filt, toep)


def place_kernel(x_ref, *refs):
    sources, out_ref = refs[:-1], refs[-1]
    half = out_ref.shape[1] // 2
    for step, source in enumerate(sources):
        at = ((x_ref[0] + 4 - step) % 4) * LANES
        for side in range(2):
            out_ref[:, pl.ds(pl.multiple_of(side * half + at, LANES), LANES)] = source[
                :, side * LANES : (side + 1) * LANES
            ]


def placed_columns(x, sources):
    tokens, width = sources[0].shape
    return pl.pallas_call(
        place_kernel,
        out_shape=jax.ShapeDtypeStruct((tokens, width * len(sources)), BF),
        in_specs=[pl.BlockSpec(memory_space=pltpu.SMEM)] + in_vmem(len(sources)),
        out_specs=pl.BlockSpec(memory_space=pltpu.VMEM),
        cost_estimate=cost(0, 2000000),
        name="placed_columns",
    )(x, *sources)


def per_device(ids, embed_table, norm_gain, in_weight, in_scale, short_filter, long_filter, decay):
    tokens = ids.shape[0]
    vocab, width_local = embed_table.shape
    rows = in_weight.shape[1]
    yh = lax.axis_index("yh")
    z = lax.axis_index("z")
    x = lax.axis_index("x")
    yl = lax.axis_index("yl")
    core = lax.axis_index("core")
    x_count = lax.axis_size("x")
    z_count = lax.axis_size("z")
    tile = yh * x_count + x
    full_width = norm_gain.shape[0]

    ids_rows = ids.reshape(-1, LANES)
    tail_rows = shifted(ids_rows[(tokens - TAIL) // LANES :], ("yh", "z", "x"), 1)
    load = payload(in_weight, ids_rows, tail_rows)
    pieces = lax.all_to_all(load, ("yh", "x"), 0, 0, tiled=True)

    chunk = x_count * rows
    gain = lax.dynamic_slice_in_dim(norm_gain, yl * (full_width // 2) + z * chunk, chunk, 0)
    own = lax.dynamic_slice_in_dim(embed_table, (z % 4) * chunk, chunk, 1)
    own = (own.astype(F32) * gain[None, :]).astype(BF)
    tp = ("z", "yl", "core")

    def spot(zi, yi, ci):
        return (zi * 2 + yi) * 2 + ci

    holders = [(zi, yi, zi // 4) for zi in range(z_count) for yi in range(2)]
    got_core = lax.ppermute(own, tp, [(spot(a, b, c), spot(a, b, 1 - c)) for a, b, c in holders])
    got_chip = lax.ppermute(own, tp, [(spot(a, b, c), spot(a, 1 - b, c)) for a, b, c in holders])
    got_both = lax.ppermute(
        own, tp, [(spot(a, b, c), spot(a, 1 - b, 1 - c)) for a, b, c in holders]
    )
    local_f = embed_table.astype(F32)
    squares = jnp.sum(local_f * local_f, axis=1)
    others = [shifted(squares, ("yl", "core"), s) for s in (1, 2, 3)]
    total = squares + others[0] + others[1] + others[2]

    flags = jnp.stack([core == z // 4, yl == 1]).astype(jnp.int32)
    partial = partial_table(flags, own, got_core, got_chip, got_both, pieces)
    share = vocab // z_count
    swapped = lax.all_to_all(
        partial.reshape(z_count, share, STREAMS * LANES), "z", 0, 0, tiled=True
    )
    scale = lax.dynamic_slice_in_dim(in_scale, tile * LANES, LANES, 1).reshape(1, STREAMS * LANES)
    norm = lax.rsqrt(lax.dynamic_slice_in_dim(total, z * share, share, 0) / full_width + 1e-06)
    piece = (jnp.sum(swapped.astype(F32), axis=0) * norm[:, None] * scale).astype(BF)
    other = shifted(piece, "yh", 1)
    both = jnp.concatenate(
        [jnp.where(yh == 0, piece, other), jnp.where(yh == 0, other, piece)], axis=0
    )
    ups, downs, last = [both], [], both
    for step in range(4):
        ups.append(shifted(ups[-1], "z", 1))
        if step < 3:
            last = shifted(last, "z", -1)
            downs.append(last)
    table = joined_table(ups + downs[::-1])

    groups = LANES // GROUP
    steps = jnp.arange(LONG_TAPS, dtype=F32)
    filt = long_filter.reshape(LONG_TAPS, 2, x_count, groups)
    filt = lax.dynamic_index_in_dim(filt, x, 2, keepdims=False).reshape(LONG_TAPS, 2 * groups)
    rate = lax.dynamic_index_in_dim(decay.reshape(2, x_count, groups), x, 1, keepdims=False)
    taps = (filt * jnp.exp(-rate.reshape(1, -1) * steps[:, None])).astype(BF).astype(F32)
    toep = toeplitz(jnp.pad(taps[::-1].T, ((0, 0), (1, LONG_TAPS - 1))))
    near_filter = short_filter.reshape(STREAMS * SHORT_TAPS, 2, x_count, LANES)
    near_filter = lax.dynamic_index_in_dim(near_filter, x, 2, keepdims=False).transpose(1, 0, 2)

    coded = pieces[:, STREAMS * rows :, :]
    sources = {}
    for step in (2, 1, 3, 0):
        where = jnp.stack([yh * x_count + (x + step) % x_count, z, jnp.int32(z_count)])
        block = mixed_block(where.astype(jnp.int32), coded, table, near_filter, toep, tokens)
        if step:
            table, block = lax.optimization_barrier((table, block))
            sources[step] = shifted(block, "x", step)
        else:
            sources[0] = block
    return placed_columns(
        x.reshape(1).astype(jnp.int32), [sources[step] for step in range(x_count)]
    )


def solution(mesh):
    fine = Mesh(mesh.devices.reshape(2, 8, 4, 2, 2), ("yh", "z", "x", "yl", "core"))
    ctx = ("yh", "z", "x")
    tp = ("yl", "core")
    placed = (
        P(ctx),
        P(None, tp),
        P(),
        P(None, ctx, tp),
        P(None, tp),
        P(None, None, tp),
        P(None, tp),
        P(tp),
    )
    return jax.shard_map(
        per_device, mesh=fine, in_specs=placed, out_specs=P(ctx, tp), check_vma=False
    )
```

```python
import jax
import jax.numpy as jnp
import numpy as np
from jax import lax
from jax.experimental import pallas as pl
from jax.experimental.pallas import tpu as pltpu
from jax.sharding import Mesh, PartitionSpec as P

GROUP = 16
SHORT_TAPS = 7
LONG_TAPS = 128
LANES = 128
HALO = 144
STREAMS = 3
BF = jnp.bfloat16
F32 = jnp.float32


def shifted(value, axis, steps):
    count = lax.axis_size(axis)
    pairs = [(source, (source + steps) % count) for source in range(count)]
    return lax.ppermute(value, axis, pairs)


def payload_kernel(weight_ref, ids_ref, out_ref):
    rows = weight_ref.shape[1]
    values = ids_ref[...]
    coded = jnp.concatenate(
        [values >> 4, values & 15, jnp.zeros((8, LANES), jnp.int32)], axis=0
    ).astype(F32).astype(BF)
    for tile in range(out_ref.shape[0]):
        for p in range(STREAMS):
            out_ref[tile, p * rows : (p + 1) * rows, :] = weight_ref[
                p, :, tile * LANES : (tile + 1) * LANES
            ]
        out_ref[tile, STREAMS * rows :, :] = coded


def in_vmem(count):
    return [pl.BlockSpec(memory_space=pltpu.VMEM)] * count


def cost(flops, moved):
    return pl.CostEstimate(flops=flops, bytes_accessed=moved, transcendentals=0)


def payload(in_weight, ids_rows):
    streams, rows, width = in_weight.shape
    return pl.pallas_call(
        payload_kernel,
        out_shape=jax.ShapeDtypeStruct((width // LANES, streams * rows + 16, LANES), BF),
        in_specs=in_vmem(2),
        out_specs=pl.BlockSpec(memory_space=pltpu.VMEM),
        cost_estimate=cost(0, 800000),
        name="payload",
    )(in_weight, ids_rows)


def partial_kernel(flag_ref, own_ref, core_ref, chip_ref, both_ref, pieces_ref, out_ref):
    rows = (pieces_ref.shape[1] - 16) // STREAMS
    half = own_ref.shape[1]
    weight = jnp.concatenate(
        [
            pieces_ref[:, p * rows : (p + 1) * rows, :].reshape(2 * half, LANES)
            for p in range(STREAMS)
        ],
        axis=1,
    )
    mine = flag_ref[0] == 1
    swap = flag_ref[1] == 1
    near = jnp.where(mine, own_ref[...], core_ref[...])
    far = jnp.where(mine, chip_ref[...], both_ref[...])
    features = jnp.concatenate(
        [jnp.where(swap, far, near), jnp.where(swap, near, far)], axis=1
    )
    out_ref[...] = jnp.dot(features, weight, preferred_element_type=F32).astype(BF)


def partial_table(flags, own, got_core, got_chip, got_both, pieces):
    vocab, half = own.shape
    return pl.pallas_call(
        partial_kernel,
        out_shape=jax.ShapeDtypeStruct((vocab, STREAMS * LANES), BF),
        in_specs=[pl.BlockSpec(memory_space=pltpu.SMEM)] + in_vmem(5),
        out_specs=pl.BlockSpec(memory_space=pltpu.VMEM),
        cost_estimate=cost(4 * vocab * half * STREAMS * LANES, 2000000),
        name="partial_table",
    )(flags, own, got_core, got_chip, got_both, pieces)


def toeplitz_kernel(taps_ref, out_ref):
    for g in range(taps_ref.shape[0]):
        row = jnp.broadcast_to(taps_ref[g : g + 1, :], (LONG_TAPS, 2 * LONG_TAPS))
        out_ref[g * LONG_TAPS : (g + 1) * LONG_TAPS, :] = pltpu.roll(
            row, 0, 1, stride=1, stride_axis=0
        ).astype(BF)


def toeplitz(taps_row):
    groups = taps_row.shape[0]
    return pl.pallas_call(
        toeplitz_kernel,
        out_shape=jax.ShapeDtypeStruct((groups * LONG_TAPS, 2 * LONG_TAPS), BF),
        in_specs=in_vmem(1),
        out_specs=pl.BlockSpec(memory_space=pltpu.VMEM),
        cost_estimate=cost(2000000, 1060000),
        name="toeplitz",
    )(taps_row)


def column_of(coded, z, share, count):
    rows = coded.shape[0] // 2
    known = (coded[:rows] * 16.0 + coded[rows:]).astype(jnp.int32)
    bits = share.bit_length() - 1
    turned = (((z - (known >> bits)) & (count - 1)) << bits) + (known & (share - 1))
    padded = jnp.concatenate([turned.astype(F32), jnp.zeros((8 - rows, LANES), F32)], axis=0)
    return jnp.transpose(padded).astype(jnp.int32)


def one_hot(column, vocab):
    hit = column == lax.broadcasted_iota(jnp.int32, (column.shape[0], vocab), 1)
    return jnp.where(hit, 1.0, 0.0).astype(BF)


def mix_kernel(spot_ref, ids_ref, *refs):
    tables = refs[:8]
    filt_ref, toep_ref, out_ref, table_ref, proj_ref, lead_ref, inner_ref, gate_ref = refs[8:]
    z = spot_ref[0]
    step = pl.program_id(0)
    share, width = tables[0].shape
    vocab = table_ref.shape[0]
    tokens = out_ref.shape[1]
    groups = LANES // GROUP
    margin = proj_ref.shape[1] - tokens
    lead = lead_ref.shape[1]
    chunk = 64

    @pl.when(step == 0)
    def _():
        for j in range(8):
            table_ref[j * share : (j + 1) * share, :] = tables[j][:share, :]

    def short(source, p, start, count):
        total = None
        for k in range(SHORT_TAPS):
            tap = filt_ref[p, k : k + 1, :]
            term = tap * source[p, start - k : start - k + count, :]
            total = term if total is None else total + term
        return total

    @pl.when(step % 4 == 0)
    def _():
        segment = step // 4
        segment = jnp.where(z == 0, 1 - segment, segment)
        coded = tables[1][share:, :LANES].astype(F32)
        coded = jnp.where(segment == 0, coded[:4], coded[4:8])
        column = column_of(coded, z, share, 8)
        column = jnp.concatenate([column[2 * LANES - lead :, 0:1], column[:, 1:2]], axis=0)
        proj = jnp.dot(one_hot(column, vocab), table_ref[...], preferred_element_type=F32)
        for p in range(STREAMS):
            lead_ref[p] = proj[:, p * LANES : (p + 1) * LANES]
            proj_ref[p, :margin, :] = lead_ref[p, lead - margin :, :]
        for at in range(0, LONG_TAPS, chunk):
            left = short(lead_ref, 1, lead - LONG_TAPS + at, chunk)
            right = short(lead_ref, 2, lead - LONG_TAPS + at, chunk)
            inner_ref[at : at + chunk, :] = (left * right).astype(BF)

    @pl.when(step % 4 != 0)
    def _():
        for p in range(STREAMS):
            proj_ref[p, :margin, :] = proj_ref[p, tokens:, :]
        inner_ref[:LONG_TAPS, :] = inner_ref[tokens:, :]

    coded = ids_ref[0].astype(F32)
    column = column_of(coded[: 2 * tokens // LANES], z, share, 8)
    column = jnp.concatenate([column[:, j : j + 1] for j in range(tokens // LANES)], axis=0)
    proj = jnp.dot(one_hot(column, vocab), table_ref[...], preferred_element_type=F32)
    for p in range(STREAMS):
        proj_ref[p, margin:, :] = proj[:, p * LANES : (p + 1) * LANES]
    for at in range(0, tokens, chunk):
        left = short(proj_ref, 1, margin + at, chunk)
        right = short(proj_ref, 2, margin + at, chunk)
        inner_ref[LONG_TAPS + at : LONG_TAPS + at + chunk, :] = (left * right).astype(BF)
        gate_ref[at : at + chunk, :] = short(proj_ref, 0, margin + at, chunk)

    lane_group = lax.broadcasted_iota(jnp.int32, (LONG_TAPS, LANES), 1) // GROUP
    for base in range(0, tokens, 2 * LONG_TAPS):
        window = jnp.concatenate(
            [
                inner_ref[base : base + 2 * LONG_TAPS, :],
                inner_ref[base + LONG_TAPS : base + 3 * LONG_TAPS, :],
            ],
            axis=1,
        )
        full = jnp.dot(toep_ref[...], window, preferred_element_type=F32)
        for side in range(2):
            lanes = slice(side * LANES, (side + 1) * LANES)
            conv = full[:LONG_TAPS, lanes]
            for g in range(1, groups):
                conv = jnp.where(
                    lane_group == g, full[g * LONG_TAPS : (g + 1) * LONG_TAPS, lanes], conv
                )
            at = base + side * LONG_TAPS
            out_ref[0, at : at + LONG_TAPS, :] = (gate_ref[at : at + LONG_TAPS, :] * conv).astype(
                BF
            )


def mixed_blocks(spot, pieces, tables, filt, toep, tokens):
    blocks, held, _ = pieces.shape
    share, width = tables[0].shape

    def whole(value):
        return pl.BlockSpec(value.shape, lambda i: (0,) * value.ndim)

    return pl.pallas_call(
        mix_kernel,
        out_shape=jax.ShapeDtypeStruct((blocks, tokens, LANES), BF),
        grid=(blocks,),
        in_specs=[
            pl.BlockSpec(memory_space=pltpu.SMEM),
            pl.BlockSpec((1, 16, LANES), lambda i: (i, held // 16 - 1, 0)),
        ]
        + [whole(table) for table in tables]
        + [whole(filt), whole(toep)],
        out_specs=pl.BlockSpec((1, tokens, LANES), lambda i: (i, 0, 0)),
        scratch_shapes=[
            pltpu.VMEM((8 * share, width), BF),
            pltpu.VMEM((STREAMS, tokens + 8, LANES), F32),
            pltpu.VMEM((STREAMS, HALO, LANES), F32),
            pltpu.VMEM((tokens + LONG_TAPS, LANES), BF),
            pltpu.VMEM((tokens, LANES), F32),
        ],
        cost_estimate=cost(5000000000, 4000000),
        name="mixed_blocks",
    )(spot, pieces, *tables, filt, toep)


def per_device(ids, embed_table, norm_gain, in_weight, in_scale, short_filter, long_filter, decay):
    tokens = ids.shape[0]
    vocab, width_local = embed_table.shape
    rows = in_weight.shape[1]
    yh = lax.axis_index("yh")
    z = lax.axis_index("z")
    x = lax.axis_index("x")
    yl = lax.axis_index("yl")
    core = lax.axis_index("core")
    x_count = lax.axis_size("x")
    z_count = lax.axis_size("z")
    tile = yh * x_count + x
    full_width = norm_gain.shape[0]

    load = payload(in_weight, ids.reshape(-1, LANES))
    pieces = lax.all_to_all(load, ("yh", "x"), 0, 0, tiled=True)

    chunk = x_count * rows
    gain = lax.dynamic_slice_in_dim(norm_gain, yl * (full_width // 2) + z * chunk, chunk, 0)
    own = lax.dynamic_slice_in_dim(embed_table, (z % 4) * chunk, chunk, 1)
    own = (own.astype(F32) * gain[None, :]).astype(BF)
    around = ("yh", "z", "yl", "core")

    def spot(y, zi, ci):
        return ((y // 2 % 2 * z_count + zi) * 2 + y % 2) * 2 + ci

    holders = [(y, zi, zi // 4) for y in range(4) for zi in range(z_count)]
    got_core = lax.ppermute(
        own, around, [(spot(a, b, c), spot(a, b, 1 - c)) for a, b, c in holders]
    )
    got_chip = lax.ppermute(
        own, around, [(spot(a, b, c), spot((a + 1) % 4, b, c)) for a, b, c in holders]
    )
    got_both = lax.ppermute(
        own, around, [(spot(a, b, c), spot((a + 3) % 4, b, 1 - c)) for a, b, c in holders]
    )
    local_f = embed_table.astype(F32)
    squares = jnp.sum(local_f * local_f, axis=1)
    others = [shifted(squares, ("yl", "core"), s) for s in (1, 2, 3)]
    total = squares + others[0] + others[1] + others[2]

    flags = jnp.stack([core == z // 4, yl == 1]).astype(jnp.int32)
    partial = partial_table(flags, own, got_core, got_chip, got_both, pieces)
    share = vocab // z_count
    swapped = lax.all_to_all(
        partial.reshape(z_count, share, STREAMS * LANES), "z", 0, 0, tiled=True
    )
    scale = lax.dynamic_slice_in_dim(in_scale, tile * LANES, LANES, 1).reshape(1, STREAMS * LANES)
    norm = lax.rsqrt(lax.dynamic_slice_in_dim(total, z * share, share, 0) / full_width + 1e-06)
    piece = (jnp.sum(swapped.astype(F32), axis=0) * norm[:, None] * scale).astype(BF)
    coded = pieces[x_count - 1 :: x_count, STREAMS * rows :, :].reshape(2, 2, 8, LANES)[:, 0]
    edges = jnp.concatenate([coded[:, 2:4], coded[:, 6:8]], axis=1).reshape(8, LANES)
    edges = jnp.pad(edges, ((0, 8), (0, (STREAMS - 1) * LANES)))
    ups = [piece, shifted(jnp.concatenate([piece, edges], axis=0), "z", 1)]
    downs, last = [], piece
    for _ in range(3):
        ups.append(shifted(ups[-1][:share], "z", 1))
        last = shifted(last, "z", -1)
        downs.append(last)
    tables = ups + downs[::-1]

    groups = LANES // GROUP
    steps = jnp.arange(LONG_TAPS, dtype=F32)
    filt = lax.dynamic_slice_in_dim(long_filter, tile * groups, groups, 1)
    rate = lax.dynamic_slice_in_dim(decay, tile * groups, groups, 0)
    taps = (filt * jnp.exp(-rate[None, :] * steps[:, None])).astype(BF).astype(F32)
    toep = toeplitz(jnp.pad(taps[::-1].T, ((0, 0), (1, LONG_TAPS - 1))))
    near_filter = lax.dynamic_slice_in_dim(short_filter, tile * LANES, LANES, 2)

    blocks = mixed_blocks(
        z.reshape(1).astype(jnp.int32), pieces, tables, near_filter, toep, tokens
    )
    result = lax.all_to_all(blocks, ("yh", "x"), 0, 0, tiled=True)
    return result.transpose(1, 0, 2).reshape(tokens, width_local)


def solution(mesh):
    fine = Mesh(mesh.devices.reshape(2, 8, 4, 2, 2), ("yh", "z", "x", "yl", "core"))
    ctx = ("yh", "z", "x")
    tp = ("yl", "core")
    placed = (
        P(ctx),
        P(None, tp),
        P(),
        P(None, ctx, tp),
        P(None, tp),
        P(None, None, tp),
        P(None, tp),
        P(tp),
    )
    return jax.shard_map(
        per_device, mesh=fine, in_specs=placed, out_specs=P(ctx, tp), check_vma=False
    )
```

```python
import jax
import jax.numpy as jnp
import numpy as np
from jax import lax
from jax.experimental import pallas as pl
from jax.experimental.pallas import tpu as pltpu
from jax.sharding import Mesh, PartitionSpec as P

GROUP = 16
SHORT_TAPS = 7
LONG_TAPS = 128
LANES = 128
HALO = 144
STREAMS = 3
BF = jnp.bfloat16
F32 = jnp.float32


def shifted(value, axis, steps):
    count = lax.axis_size(axis)
    pairs = [(source, (source + steps) % count) for source in range(count)]
    return lax.ppermute(value, axis, pairs)


def payload_kernel(weight_ref, ids_ref, out_ref):
    rows = weight_ref.shape[1]
    values = ids_ref[...]
    coded = jnp.concatenate(
        [values >> 4, values & 15, jnp.zeros((8, LANES), jnp.int32)], axis=0
    ).astype(F32).astype(BF)
    for tile in range(out_ref.shape[0]):
        for p in range(STREAMS):
            out_ref[tile, p * rows : (p + 1) * rows, :] = weight_ref[
                p, :, tile * LANES : (tile + 1) * LANES
            ]
        out_ref[tile, STREAMS * rows :, :] = coded


def in_vmem(count):
    return [pl.BlockSpec(memory_space=pltpu.VMEM)] * count


def cost(flops, moved):
    return pl.CostEstimate(flops=flops, bytes_accessed=moved, transcendentals=0)


def payload(in_weight, ids_rows):
    streams, rows, width = in_weight.shape
    return pl.pallas_call(
        payload_kernel,
        out_shape=jax.ShapeDtypeStruct((width // LANES, streams * rows + 16, LANES), BF),
        in_specs=in_vmem(2),
        out_specs=pl.BlockSpec(memory_space=pltpu.VMEM),
        cost_estimate=cost(0, 800000),
        name="payload",
    )(in_weight, ids_rows)


def partial_kernel(flag_ref, own_ref, core_ref, chip_ref, both_ref, pieces_ref, out_ref):
    rows = (pieces_ref.shape[1] - 16) // STREAMS
    half = own_ref.shape[1]
    weight = jnp.concatenate(
        [
            pieces_ref[:, p * rows : (p + 1) * rows, :].reshape(2 * half, LANES)
            for p in range(STREAMS)
        ],
        axis=1,
    )
    mine = flag_ref[0] == 1
    swap = flag_ref[1] == 1
    near = jnp.where(mine, own_ref[...], core_ref[...])
    far = jnp.where(mine, chip_ref[...], both_ref[...])
    features = jnp.concatenate(
        [jnp.where(swap, far, near), jnp.where(swap, near, far)], axis=1
    )
    out_ref[...] = jnp.dot(features, weight, preferred_element_type=F32).astype(BF)


def partial_table(flags, own, got_core, got_chip, got_both, pieces):
    vocab, half = own.shape
    return pl.pallas_call(
        partial_kernel,
        out_shape=jax.ShapeDtypeStruct((vocab, STREAMS * LANES), BF),
        in_specs=[pl.BlockSpec(memory_space=pltpu.SMEM)] + in_vmem(5),
        out_specs=pl.BlockSpec(memory_space=pltpu.VMEM),
        cost_estimate=cost(4 * vocab * half * STREAMS * LANES, 2000000),
        name="partial_table",
    )(flags, own, got_core, got_chip, got_both, pieces)


def toeplitz_kernel(taps_ref, out_ref):
    for g in range(taps_ref.shape[0]):
        row = jnp.broadcast_to(taps_ref[g : g + 1, :], (LONG_TAPS, 2 * LONG_TAPS))
        block = pltpu.roll(row, 0, 1, stride=1, stride_axis=0)
        out_ref[g] = jnp.transpose(block).astype(BF)


def toeplitz(taps_row):
    groups = taps_row.shape[0]
    return pl.pallas_call(
        toeplitz_kernel,
        out_shape=jax.ShapeDtypeStruct((groups, 2 * LONG_TAPS, LONG_TAPS), BF),
        in_specs=in_vmem(1),
        out_specs=pl.BlockSpec(memory_space=pltpu.VMEM),
        cost_estimate=cost(2000000, 1060000),
        name="toeplitz",
    )(taps_row)


def column_of(coded, z, share, count):
    rows = coded.shape[0] // 2
    known = (coded[:rows] * 16.0 + coded[rows:]).astype(jnp.int32)
    bits = share.bit_length() - 1
    turned = (((z - (known >> bits)) & (count - 1)) << bits) + (known & (share - 1))
    padded = jnp.concatenate([turned.astype(F32), jnp.zeros((8 - rows, LANES), F32)], axis=0)
    return jnp.transpose(padded).astype(jnp.int32)


def one_hot(column, vocab):
    hit = column == lax.broadcasted_iota(jnp.int32, (column.shape[0], vocab), 1)
    return jnp.where(hit, 1.0, 0.0).astype(BF)


def hot_kernel(spot_ref, ids_ref, edge_ref, out_ref, lead_ref):
    z = spot_ref[0]
    share = edge_ref.shape[0] - 16
    vocab = out_ref.shape[2]
    tokens = out_ref.shape[1]
    lead = lead_ref.shape[0] // 2

    @pl.when(pl.program_id(0) == 0)
    def _():
        coded = edge_ref[share:, :LANES].astype(F32)
        first, second = coded[:4], coded[4:8]
        wrapped = z == 0
        for segment, rows in enumerate(
            (jnp.where(wrapped, second, first), jnp.where(wrapped, first, second))
        ):
            column = column_of(rows, z, share, 8)
            column = jnp.concatenate([column[2 * LANES - lead :, 0:1], column[:, 1:2]], axis=0)
            lead_ref[segment * lead : (segment + 1) * lead, :] = one_hot(column, vocab)

    coded = ids_ref[0].astype(F32)
    column = column_of(coded[: 2 * tokens // LANES], z, share, 8)
    for j in range(tokens // LANES):
        out_ref[0, j * LANES : (j + 1) * LANES, :] = one_hot(column[:, j : j + 1], vocab)


def hot_rows(spot, pieces, edge_piece, tokens, vocab):
    blocks, held, _ = pieces.shape
    return pl.pallas_call(
        hot_kernel,
        out_shape=(
            jax.ShapeDtypeStruct((blocks, tokens, vocab), BF),
            jax.ShapeDtypeStruct((2 * HALO, vocab), BF),
        ),
        grid=(blocks,),
        in_specs=[
            pl.BlockSpec(memory_space=pltpu.SMEM),
            pl.BlockSpec((1, 16, LANES), lambda i: (i, held // 16 - 1, 0)),
            pl.BlockSpec(edge_piece.shape, lambda i: (0, 0)),
        ],
        out_specs=(
            pl.BlockSpec((1, tokens, vocab), lambda i: (i, 0, 0)),
            pl.BlockSpec((2 * HALO, vocab), lambda i: (0, 0)),
        ),
        cost_estimate=cost(5000000, 4500000),
        name="hot_rows",
    )(spot, pieces, edge_piece)


def mix_kernel(hot_ref, lead_hot_ref, *refs):
    tables = refs[:8]
    filt_ref, toep_ref, out_ref = refs[8:11]
    table_ref, lead_ref, head_ref, edge_ref = refs[11:15]
    next_ref, proj_ref, fresh_ref, inner_ref, fresh_gate_ref, gate_ref, conv_ref = refs[15:]
    step = pl.program_id(0)
    share, width = tables[0].shape
    tokens = out_ref.shape[1]
    groups = LANES // GROUP
    margin = proj_ref.shape[1] - tokens
    lead = lead_hot_ref.shape[0] // 2
    chunk = 64

    def short(source, p, start, count):
        total = None
        for k in range(SHORT_TAPS):
            tap = filt_ref[p, k : k + 1, :]
            term = tap * source[p, start - k : start - k + count, :]
            total = term if total is None else total + term
        return total

    @pl.when(step == 0)
    def _():
        for j in range(8):
            table_ref[j * share : (j + 1) * share, :] = tables[j][:share, :]
        proj = jnp.dot(lead_hot_ref[...], table_ref[...], preferred_element_type=F32)
        for p in range(STREAMS):
            lead_ref[p] = proj[:, p * LANES : (p + 1) * LANES]
        for segment in range(2):
            for p in range(STREAMS):
                head_ref[segment, p] = lead_ref[
                    p, (segment + 1) * lead - margin : (segment + 1) * lead, :
                ]
            for at in range(0, LONG_TAPS, chunk):
                start = (segment + 1) * lead - LONG_TAPS + at
                fresh_ref[at : at + chunk, :] = short(lead_ref, 1, start, chunk) * short(
                    lead_ref, 2, start, chunk
                )
            edge_ref[segment] = jnp.transpose(fresh_ref[:LONG_TAPS, :]).astype(BF)

    count = tokens // LONG_TAPS

    def select(begin, end):
        proj = jnp.dot(hot_ref[0, begin:end, :], table_ref[...], preferred_element_type=F32)
        for p in range(STREAMS):
            next_ref[p, begin:end, :] = proj[:, p * LANES : (p + 1) * LANES]

    def filtered(at):
        left = short(proj_ref, 1, margin + at, chunk)
        right = short(proj_ref, 2, margin + at, chunk)
        fresh_ref[at : at + chunk, :] = left * right
        fresh_gate_ref[at : at + chunk, :] = short(proj_ref, 0, margin + at, chunk)

    def convolved(g):
        rows = slice(g * GROUP, (g + 1) * GROUP)
        windows = jnp.concatenate(
            [inner_ref[rows, j * LONG_TAPS : (j + 2) * LONG_TAPS] for j in range(count)], axis=0
        )
        full = jnp.dot(windows, toep_ref[g], preferred_element_type=F32)
        for j in range(count):
            conv_ref[j, rows, :] = full[j * GROUP : (j + 1) * GROUP]

    select(0, tokens)
    for g in range(groups):
        convolved(g)
        filtered(g * chunk)

    @pl.when(step >= 0)
    def _():
        for j in range(count):
            at = j * LONG_TAPS
            conv = jnp.transpose(conv_ref[j])
            out_ref[0, at : at + LONG_TAPS, :] = (gate_ref[at : at + LONG_TAPS, :] * conv).astype(BF)

        starts = step % 4 == 0
        segment = jnp.minimum(step // 4, 1)
        for p in range(STREAMS):
            proj_ref[p, :margin, :] = jnp.where(
                starts, head_ref[segment, p], proj_ref[p, tokens:, :]
            )
            proj_ref[p, margin:, :] = next_ref[p]
        starts = (step + 3) % 4 == 0
        segment = jnp.minimum((step + 3) // 4 - 1, 1)
        segment = jnp.maximum(segment, 0)
        inner_ref[:, :LONG_TAPS] = jnp.where(starts, edge_ref[segment], inner_ref[:, tokens:])
        for j in range(count):
            at = j * LONG_TAPS
            inner_ref[:, LONG_TAPS + at : 2 * LONG_TAPS + at] = jnp.transpose(
                fresh_ref[at : at + LONG_TAPS, :]
            ).astype(BF)
        gate_ref[...] = fresh_gate_ref[...]


def mixed_blocks(hot, lead_hot, tables, filt, toep):
    blocks, tokens, vocab = hot.shape
    share, width = tables[0].shape

    def whole(value):
        return pl.BlockSpec(value.shape, lambda i: (0,) * value.ndim)

    return pl.pallas_call(
        mix_kernel,
        out_shape=jax.ShapeDtypeStruct((blocks, tokens, LANES), BF),
        grid=(blocks + 2,),
        in_specs=[
            pl.BlockSpec((1, tokens, vocab), lambda i: (jnp.minimum(i, blocks - 1), 0, 0)),
            whole(lead_hot),
        ]
        + [whole(table) for table in tables]
        + [whole(filt), whole(toep)],
        out_specs=pl.BlockSpec((1, tokens, LANES), lambda i: (jnp.maximum(i - 2, 0), 0, 0)),
        scratch_shapes=[
            pltpu.VMEM((8 * share, width), BF),
            pltpu.VMEM((STREAMS, 2 * HALO, LANES), F32),
            pltpu.VMEM((2, STREAMS, 8, LANES), F32),
            pltpu.VMEM((2, LONG_TAPS, LANES), BF),
            pltpu.VMEM((STREAMS, tokens, LANES), F32),
            pltpu.VMEM((STREAMS, tokens + 8, LANES), F32),
            pltpu.VMEM((tokens, LANES), F32),
            pltpu.VMEM((LANES, tokens + LONG_TAPS), BF),
            pltpu.VMEM((tokens, LANES), F32),
            pltpu.VMEM((tokens, LANES), F32),
            pltpu.VMEM((tokens // LONG_TAPS, LANES, LONG_TAPS), F32),
        ],
        cost_estimate=cost(5000000000, 6000000),
        name="mixed_blocks",
    )(hot, lead_hot, *tables, filt, toep)


def per_device(ids, embed_table, norm_gain, in_weight, in_scale, short_filter, long_filter, decay):
    tokens = ids.shape[0]
    vocab, width_local = embed_table.shape
    rows = in_weight.shape[1]
    yh = lax.axis_index("yh")
    z = lax.axis_index("z")
    x = lax.axis_index("x")
    yl = lax.axis_index("yl")
    core = lax.axis_index("core")
    x_count = lax.axis_size("x")
    z_count = lax.axis_size("z")
    tile = yh * x_count + x
    full_width = norm_gain.shape[0]

    load = payload(in_weight, ids.reshape(-1, LANES))
    load, own_table = lax.optimization_barrier((load, embed_table))
    pieces = lax.all_to_all(load, ("yh", "x"), 0, 0, tiled=True)

    groups = LANES // GROUP
    steps = jnp.arange(LONG_TAPS, dtype=F32)
    filt = lax.dynamic_slice_in_dim(long_filter, tile * groups, groups, 1)
    rate = lax.dynamic_slice_in_dim(decay, tile * groups, groups, 0)
    filt, rate, load = lax.optimization_barrier((filt, rate, load))
    taps = (filt * jnp.exp(-rate[None, :] * steps[:, None])).astype(BF).astype(F32)
    toep = toeplitz(jnp.pad(taps[::-1].T, ((0, 0), (1, LONG_TAPS - 1))))
    near_filter = lax.dynamic_slice_in_dim(short_filter, tile * LANES, LANES, 2)
    scale = lax.dynamic_slice_in_dim(in_scale, tile * LANES, LANES, 1).reshape(1, STREAMS * LANES)

    chunk = x_count * rows
    gain = lax.dynamic_slice_in_dim(norm_gain, yl * (full_width // 2) + z * chunk, chunk, 0)
    own = lax.dynamic_slice_in_dim(own_table, (z % 4) * chunk, chunk, 1)
    own = (own.astype(F32) * gain[None, :]).astype(BF)
    around = ("yh", "z", "yl", "core")

    def spot(y, zi, ci):
        return ((y // 2 % 2 * z_count + zi) * 2 + y % 2) * 2 + ci

    holders = [(y, zi, zi // 4) for y in range(4) for zi in range(z_count)]
    got_core = lax.ppermute(
        own, around, [(spot(a, b, c), spot(a, b, 1 - c)) for a, b, c in holders]
    )
    got_chip = lax.ppermute(
        own, around, [(spot(a, b, c), spot((a + 1) % 4, b, c)) for a, b, c in holders]
    )
    got_both = lax.ppermute(
        own, around, [(spot(a, b, c), spot((a + 3) % 4, b, 1 - c)) for a, b, c in holders]
    )
    flags = jnp.stack([core == z // 4, yl == 1]).astype(jnp.int32)
    pieces, toep, near_filter, scale = lax.optimization_barrier(
        (pieces, toep, near_filter, scale)
    )
    partial = partial_table(flags, own, got_core, got_chip, got_both, pieces)
    partial, own_table = lax.optimization_barrier((partial, own_table))
    share = vocab // z_count
    swapped = lax.all_to_all(
        partial.reshape(z_count, share, STREAMS * LANES), "z", 0, 0, tiled=True
    )
    local_f = own_table.astype(F32)
    squares = jnp.sum(local_f * local_f, axis=1)
    others = [shifted(squares, ("yl", "core"), s) for s in (1, 2, 3)]
    total = squares + others[0] + others[1] + others[2]

    norm = lax.rsqrt(lax.dynamic_slice_in_dim(total, z * share, share, 0) / full_width + 1e-06)
    piece = (jnp.sum(swapped.astype(F32), axis=0) * norm[:, None] * scale).astype(BF)
    coded = pieces[x_count - 1 :: x_count, STREAMS * rows :, :].reshape(2, 2, 8, LANES)[:, 0]
    edges = jnp.concatenate([coded[:, 2:4], coded[:, 6:8]], axis=1).reshape(8, LANES)
    edges = jnp.pad(edges, ((0, 8), (0, (STREAMS - 1) * LANES)))
    ups = [piece, shifted(jnp.concatenate([piece, edges], axis=0), "z", 1)]
    downs, last = [], piece
    for _ in range(3):
        ups.append(shifted(ups[-1][:share], "z", 1))
        last = shifted(last, "z", -1)
        downs.append(last)
    tables = ups + downs[::-1]

    hot, lead_hot = hot_rows(z.reshape(1).astype(jnp.int32), pieces, tables[1], tokens, vocab)
    blocks = mixed_blocks(hot, lead_hot, tables, near_filter, toep)
    result = lax.all_to_all(blocks, ("yh", "x"), 0, 0, tiled=True)
    return result.transpose(1, 0, 2).reshape(tokens, width_local)


def solution(mesh):
    fine = Mesh(mesh.devices.reshape(2, 8, 4, 2, 2), ("yh", "z", "x", "yl", "core"))
    ctx = ("yh", "z", "x")
    tp = ("yl", "core")
    placed = (
        P(ctx),
        P(None, tp),
        P(),
        P(None, ctx, tp),
        P(None, tp),
        P(None, None, tp),
        P(None, tp),
        P(tp),
    )
    return jax.shard_map(
        per_device, mesh=fine, in_specs=placed, out_specs=P(ctx, tp), check_vma=False
    )
```

```python
import jax
import jax.numpy as jnp
import numpy as np
from jax import lax
from jax.experimental import pallas as pl
from jax.experimental.pallas import tpu as pltpu
from jax.sharding import Mesh, PartitionSpec as P

GROUP = 16
SHORT_TAPS = 7
LONG_TAPS = 128
LANES = 128
HALO = 144
STREAMS = 3
BF = jnp.bfloat16
F32 = jnp.float32


def shifted(value, axis, steps):
    count = lax.axis_size(axis)
    pairs = [(source, (source + steps) % count) for source in range(count)]
    return lax.ppermute(value, axis, pairs)


def payload_kernel(weight_ref, ids_ref, out_ref):
    streams, rows, width = weight_ref.shape
    tiles = width // LANES
    columns = out_ref.shape[0] // tiles
    values = ids_ref[...]
    coded = jnp.where(values < 256, values, 255 - values).astype(F32)
    coded = jnp.concatenate([coded, jnp.zeros_like(coded)], axis=0)
    for tile in range(tiles):
        lanes = slice(tile * LANES, (tile + 1) * LANES)
        pair = jnp.concatenate([weight_ref[0, :, lanes], weight_ref[1, :, lanes]], axis=0)
        third = weight_ref[2, :, lanes].astype(F32)
        third = jnp.concatenate([third, pltpu.roll(third, LANES - 8, 1)], axis=0)
        pair = jnp.transpose(pair.astype(F32))
        third = jnp.transpose(third)
        for part in range(columns):
            to = (tile // 4 * columns + part) * 4 + tile % 4
            at = part * GROUP
            out_ref[to, :GROUP, :] = pair[at : at + GROUP].astype(BF)
            out_ref[to, GROUP:, :] = jnp.concatenate([third[at : at + 8], coded], axis=0).astype(
                BF
            )


def in_vmem(count):
    return [pl.BlockSpec(memory_space=pltpu.VMEM)] * count


def cost(flops, moved):
    return pl.CostEstimate(flops=flops, bytes_accessed=moved, transcendentals=0)


def payload(in_weight, ids_rows, parts):
    return pl.pallas_call(
        payload_kernel,
        out_shape=jax.ShapeDtypeStruct((parts, 2 * GROUP, LANES), BF),
        in_specs=in_vmem(2),
        out_specs=pl.BlockSpec(memory_space=pltpu.VMEM),
        cost_estimate=cost(0, 900000),
        name="payload",
    )(in_weight, ids_rows)


def norm_kernel(spot_ref, own_ref, core_ref, up_ref, down_ref, far_up_ref, far_down_ref, *refs):
    gain_ref, out_ref = refs
    vocab, width = own_ref.shape
    quarter = [spot_ref[j] for j in range(4)]
    chunk = 32

    def some(read, at):
        parts = [value.astype(F32) for value in read]
        squares = sum(jnp.sum(part * part, axis=1, keepdims=True) for part in parts)
        factor = lax.rsqrt(squares / (4 * width) + 1e-06)
        for j, part in enumerate(parts):
            gain = gain_ref[:, pl.ds(pl.multiple_of(quarter[j] * width, LANES), width)]
            out_ref[quarter[j], pl.ds(at, chunk), :] = (part * factor * gain).astype(BF)

    def step(i, _):
        near = pl.ds(pl.multiple_of(i * chunk, chunk), chunk)
        at = pl.multiple_of(vocab // 2 + i * chunk, chunk)
        far = pl.ds(at, chunk)
        some([own_ref[near, :], core_ref[near, :], up_ref[near, :], far_up_ref[near, :]], near.start)
        some([own_ref[far, :], core_ref[far, :], down_ref[near, :], far_down_ref[near, :]], at)
        return 0

    lax.fori_loop(0, vocab // 2 // chunk, step, 0)


def normed_rows(spot, own, got_core, got_up, got_down, far_up, far_down, gain):
    vocab, width = own.shape
    return pl.pallas_call(
        norm_kernel,
        out_shape=jax.ShapeDtypeStruct((4, vocab, width), BF),
        in_specs=[pl.BlockSpec(memory_space=pltpu.SMEM)] + in_vmem(7),
        out_specs=pl.BlockSpec(memory_space=pltpu.VMEM),
        cost_estimate=cost(20 * vocab * width, 8 * 2 * vocab * width),
        name="normed_rows",
    )(spot, own, got_core, got_up, got_down, far_up, far_down, gain)


def table_kernel(normed_ref, pieces_ref, scale_ref, out_ref, weight_ref):
    quarters, _, width = normed_ref.shape
    low = lax.broadcasted_iota(jnp.int32, (GROUP, LANES), 1) < LANES // 2
    for m in range(pieces_ref.shape[0] // 2):
        lanes = slice(m * LANES, (m + 1) * LANES)
        first = pieces_ref[2 * m, :GROUP, :].astype(F32)
        second = pieces_ref[2 * m + 1, :GROUP, :].astype(F32)
        weight_ref[:GROUP, lanes] = jnp.where(low, first, pltpu.roll(second, 64, 1)).astype(BF)
        weight_ref[GROUP : 2 * GROUP, lanes] = jnp.where(
            low, pltpu.roll(first, 64, 1), second
        ).astype(BF)
        first = pieces_ref[2 * m, GROUP:, :].astype(F32)[:8]
        second = pieces_ref[2 * m + 1, GROUP:, :].astype(F32)[:8]
        third = jnp.concatenate(
            [
                jnp.where(low[:8], first, pltpu.roll(second, 64, 1)),
                jnp.where(low[:8], pltpu.roll(first, 64, 1), second),
            ],
            axis=0,
        )
        weight_ref[2 * GROUP :, lanes] = third.astype(BF)
    total = None
    for q in range(quarters):
        term = lax.dot_general(
            weight_ref[:, q * width : (q + 1) * width],
            normed_ref[q],
            (((1,), (1,)), ((), ())),
            preferred_element_type=F32,
        )
        total = term if total is None else total + term
    out_ref[...] = (total * scale_ref[...]).astype(BF)


def table_piece(normed, pieces, scale):
    quarters, vocab, width = normed.shape
    rows = STREAMS * GROUP
    return pl.pallas_call(
        table_kernel,
        out_shape=jax.ShapeDtypeStruct((rows, vocab), BF),
        in_specs=in_vmem(3),
        out_specs=pl.BlockSpec(memory_space=pltpu.VMEM),
        scratch_shapes=[pltpu.VMEM((rows, quarters * width), BF)],
        cost_estimate=cost(2 * rows * vocab * quarters * width, 5000000),
        name="table_piece",
    )(normed, pieces, scale)


def toeplitz_kernel(taps_ref, out_ref):
    for g in range(taps_ref.shape[0]):
        row = jnp.broadcast_to(taps_ref[g : g + 1, :], (LONG_TAPS, 2 * LONG_TAPS))
        block = pltpu.roll(row, 0, 1, stride=1, stride_axis=0)
        out_ref[g] = jnp.transpose(block).astype(BF)


def toeplitz(taps_row):
    groups = taps_row.shape[0]
    return pl.pallas_call(
        toeplitz_kernel,
        out_shape=jax.ShapeDtypeStruct((groups, 2 * LONG_TAPS, LONG_TAPS), BF),
        in_specs=in_vmem(1),
        out_specs=pl.BlockSpec(memory_space=pltpu.VMEM),
        cost_estimate=cost(2000000, 1060000),
        name="toeplitz",
    )(taps_row)


def column_of(coded):
    known = jnp.where(coded < 0.0, 255.0 - coded, coded)
    rows = known.shape[0]
    padded = jnp.concatenate([known, jnp.zeros((8 - rows, LANES), F32)], axis=0)
    return jnp.transpose(padded).astype(jnp.int32)


def one_hot(column, vocab):
    hit = column == lax.broadcasted_iota(jnp.int32, (column.shape[0], vocab), 1)
    return jnp.where(hit, 1.0, 0.0).astype(BF)


def ids_of(pieces_ref, index):
    return pieces_ref[index, GROUP:, :].astype(F32)[8:12]


def hot_kernel(spot_ref, pieces_ref, out_ref, lead_ref):
    z = spot_ref[0]
    step = pl.program_id(0)
    devices = pieces_ref.shape[0]
    half, tokens, vocab = out_ref.shape
    lead = lead_ref.shape[0] // 2

    @pl.when(step == 0)
    def _():
        for segment in range(2):
            start = segment * (devices // 2) + z * 4
            rows = ids_of(pieces_ref, (start + devices - 1) % devices)
            column = column_of(rows[2:])
            column = jnp.concatenate([column[2 * LANES - lead :, 0:1], column[:, 1:2]], axis=0)
            lead_ref[segment * lead : (segment + 1) * lead, :] = one_hot(column, vocab)

    for block in range(half):
        index = step * half + block
        source = index // 4 * (devices // 2) + z * 4 + index % 4
        column = column_of(ids_of(pieces_ref, source))
        for j in range(tokens // LANES):
            out_ref[block, j * LANES : (j + 1) * LANES, :] = one_hot(column[:, j : j + 1], vocab)


def hot_rows(spot, pieces, blocks, tokens, vocab):
    half = 2
    return pl.pallas_call(
        hot_kernel,
        out_shape=(
            jax.ShapeDtypeStruct((blocks, tokens, vocab), BF),
            jax.ShapeDtypeStruct((2 * HALO, vocab), BF),
        ),
        grid=(blocks // half,),
        in_specs=[
            pl.BlockSpec(memory_space=pltpu.SMEM),
            pl.BlockSpec(pieces.shape, lambda i: (0, 0, 0)),
        ],
        out_specs=(
            pl.BlockSpec((half, tokens, vocab), lambda i: (i, 0, 0)),
            pl.BlockSpec((2 * HALO, vocab), lambda i: (0, 0)),
        ),
        cost_estimate=cost(5000000, 4500000),
        name="hot_rows",
    )(spot, pieces)


def mix_kernel(spot_ref, hot_ref, lead_hot_ref, *refs):
    tables = refs[:8]
    filt_ref, toep_ref, out_ref = refs[8:11]
    table_ref, lead_ref, head_ref, edge_ref = refs[11:15]
    next_ref, proj_ref, fresh_ref, inner_ref, fresh_gate_ref, gate_ref, conv_ref, flat_ref = refs[15:]
    step = pl.program_id(0)
    tokens = out_ref.shape[1]
    groups = LANES // GROUP
    margin = proj_ref.shape[1] - tokens
    lead = lead_hot_ref.shape[0] // 2
    chunk = 64

    def short(source, p, start, count):
        total = None
        for k in range(SHORT_TAPS):
            tap = filt_ref[p, k : k + 1, :]
            term = tap * source[p, start - k : start - k + count, :]
            total = term if total is None else total + term
        return total

    @pl.when(step == 0)
    def _():
        for j, piece in enumerate(tables):
            at = (spot_ref[0] + len(tables) - j) % len(tables) * GROUP
            for p in range(STREAMS):
                flat_ref[p, pl.ds(pl.multiple_of(at, GROUP), GROUP), :] = piece[
                    p * GROUP : (p + 1) * GROUP, :
                ]
        for p in range(STREAMS):
            table_ref[:, p * LANES : (p + 1) * LANES] = jnp.transpose(
                flat_ref[p].astype(F32)
            ).astype(BF)
        proj = jnp.dot(lead_hot_ref[...], table_ref[...], preferred_element_type=F32)
        for p in range(STREAMS):
            lead_ref[p] = proj[:, p * LANES : (p + 1) * LANES]
        for segment in range(2):
            for p in range(STREAMS):
                head_ref[segment, p] = lead_ref[
                    p, (segment + 1) * lead - margin : (segment + 1) * lead, :
                ]
            for at in range(0, LONG_TAPS, chunk):
                start = (segment + 1) * lead - LONG_TAPS + at
                fresh_ref[at : at + chunk, :] = short(lead_ref, 1, start, chunk) * short(
                    lead_ref, 2, start, chunk
                )
            edge_ref[segment] = jnp.transpose(fresh_ref[:LONG_TAPS, :]).astype(BF)

    count = tokens // LONG_TAPS

    def select(begin, end):
        proj = jnp.dot(hot_ref[0, begin:end, :], table_ref[...], preferred_element_type=F32)
        for p in range(STREAMS):
            next_ref[p, begin:end, :] = proj[:, p * LANES : (p + 1) * LANES]

    def filtered(at):
        left = short(proj_ref, 1, margin + at, chunk)
        right = short(proj_ref, 2, margin + at, chunk)
        fresh_ref[at : at + chunk, :] = left * right
        fresh_gate_ref[at : at + chunk, :] = short(proj_ref, 0, margin + at, chunk)

    def convolved(g):
        rows = slice(g * GROUP, (g + 1) * GROUP)
        windows = jnp.concatenate(
            [inner_ref[rows, j * LONG_TAPS : (j + 2) * LONG_TAPS] for j in range(count)], axis=0
        )
        full = jnp.dot(windows, toep_ref[g], preferred_element_type=F32)
        for j in range(count):
            conv_ref[j, rows, :] = full[j * GROUP : (j + 1) * GROUP]

    select(0, tokens)
    for g in range(groups):
        convolved(g)
        filtered(g * chunk)

    @pl.when(step >= 0)
    def _():
        for j in range(count):
            at = j * LONG_TAPS
            conv = jnp.transpose(conv_ref[j])
            out_ref[0, at : at + LONG_TAPS, :] = (gate_ref[at : at + LONG_TAPS, :] * conv).astype(BF)

        starts = step % 4 == 0
        segment = jnp.minimum(step // 4, 1)
        for p in range(STREAMS):
            proj_ref[p, :margin, :] = jnp.where(
                starts, head_ref[segment, p], proj_ref[p, tokens:, :]
            )
            proj_ref[p, margin:, :] = next_ref[p]
        starts = (step + 3) % 4 == 0
        segment = jnp.minimum((step + 3) // 4 - 1, 1)
        segment = jnp.maximum(segment, 0)
        inner_ref[:, :LONG_TAPS] = jnp.where(starts, edge_ref[segment], inner_ref[:, tokens:])
        for j in range(count):
            at = j * LONG_TAPS
            inner_ref[:, LONG_TAPS + at : 2 * LONG_TAPS + at] = jnp.transpose(
                fresh_ref[at : at + LONG_TAPS, :]
            ).astype(BF)
        gate_ref[...] = fresh_gate_ref[...]


def mixed_blocks(spot, hot, lead_hot, tables, filt, toep):
    blocks, tokens, vocab = hot.shape
    width = STREAMS * LANES

    def whole(value):
        return pl.BlockSpec(value.shape, lambda i: (0,) * value.ndim)

    return pl.pallas_call(
        mix_kernel,
        out_shape=jax.ShapeDtypeStruct((blocks, tokens, LANES), BF),
        grid=(blocks + 2,),
        in_specs=[
            pl.BlockSpec(memory_space=pltpu.SMEM),
            pl.BlockSpec((1, tokens, vocab), lambda i: (jnp.minimum(i, blocks - 1), 0, 0)),
            whole(lead_hot),
        ]
        + [whole(table) for table in tables]
        + [whole(filt), whole(toep)],
        out_specs=pl.BlockSpec((1, tokens, LANES), lambda i: (jnp.maximum(i - 2, 0), 0, 0)),
        scratch_shapes=[
            pltpu.VMEM((vocab, width), BF),
            pltpu.VMEM((STREAMS, 2 * HALO, LANES), F32),
            pltpu.VMEM((2, STREAMS, 8, LANES), F32),
            pltpu.VMEM((2, LONG_TAPS, LANES), BF),
            pltpu.VMEM((STREAMS, tokens, LANES), F32),
            pltpu.VMEM((STREAMS, tokens + 8, LANES), F32),
            pltpu.VMEM((tokens, LANES), F32),
            pltpu.VMEM((LANES, tokens + LONG_TAPS), BF),
            pltpu.VMEM((tokens, LANES), F32),
            pltpu.VMEM((tokens, LANES), F32),
            pltpu.VMEM((tokens // LONG_TAPS, LANES, LONG_TAPS), F32),
            pltpu.VMEM((STREAMS, LANES, vocab), BF),
        ],
        cost_estimate=cost(5000000000, 6000000),
        name="mixed_blocks",
    )(spot, hot, lead_hot, *tables, filt, toep)


def per_device(ids, embed_table, norm_gain, in_weight, in_scale, short_filter, long_filter, decay):
    tokens = ids.shape[0]
    vocab, width_local = embed_table.shape
    yh = lax.axis_index("yh")
    z = lax.axis_index("z")
    x = lax.axis_index("x")
    yl = lax.axis_index("yl")
    core = lax.axis_index("core")
    x_count = lax.axis_size("x")
    z_count = lax.axis_size("z")
    ctx = ("yh", "z", "x")
    tile = yh * x_count + x
    tiles = width_local // LANES

    y = ("yh", "yl")
    got_up = shifted(embed_table[: vocab // 2], y, -1)
    got_down = shifted(embed_table[vocab // 2 :], y, 1)
    got_core = shifted(embed_table, "core", 1)

    load = payload(in_weight, ids.reshape(-1, LANES), tiles * z_count)
    pieces = lax.all_to_all(load, ctx, 0, 0, tiled=True)

    groups = LANES // GROUP
    steps = jnp.arange(LONG_TAPS, dtype=F32)
    filt = lax.dynamic_slice_in_dim(long_filter, tile * groups, groups, 1)
    rate = lax.dynamic_slice_in_dim(decay, tile * groups, groups, 0)
    filt, rate, load = lax.optimization_barrier((filt, rate, load))
    taps = (filt * jnp.exp(-rate[None, :] * steps[:, None])).astype(BF).astype(F32)
    toep = toeplitz(jnp.pad(taps[::-1].T, ((0, 0), (1, LONG_TAPS - 1))))
    near_filter = lax.dynamic_slice_in_dim(short_filter, tile * LANES, LANES, 2)
    scale = lax.dynamic_slice_in_dim(in_scale, tile * LANES + z * GROUP, GROUP, 1)
    scale = scale.reshape(STREAMS * GROUP, 1)

    far_up = shifted(got_up, "core", 1)
    far_down = shifted(got_down, "core", 1)
    mine = yl * 2 + core
    order = jnp.stack([mine, mine ^ 1, mine ^ 2, mine ^ 3]).astype(jnp.int32)
    normed = normed_rows(
        order, embed_table, got_core, got_up, got_down, far_up, far_down, norm_gain.reshape(1, -1)
    )
    pieces, toep, near_filter, normed = lax.optimization_barrier(
        (pieces, toep, near_filter, normed)
    )
    piece = table_piece(normed, pieces, scale)
    ups, downs, last = [piece], [], piece
    for step in range(4):
        ups.append(shifted(ups[-1], "z", 1))
        if step < 3:
            last = shifted(last, "z", -1)
            downs.append(last)

    spot = z.reshape(1).astype(jnp.int32)
    hot, lead_hot = hot_rows(spot, pieces, tiles, tokens, vocab)
    blocks = mixed_blocks(spot, hot, lead_hot, ups + downs[::-1], near_filter, toep)
    result = lax.all_to_all(blocks, ("yh", "x"), 0, 0, tiled=True)
    return result.transpose(1, 0, 2).reshape(tokens, width_local)


def solution(mesh):
    fine = Mesh(mesh.devices.reshape(2, 8, 4, 2, 2), ("yh", "z", "x", "yl", "core"))
    ctx = ("yh", "z", "x")
    tp = ("yl", "core")
    placed = (
        P(ctx),
        P(None, tp),
        P(),
        P(None, ctx, tp),
        P(None, tp),
        P(None, None, tp),
        P(None, tp),
        P(tp),
    )
    return jax.shard_map(
        per_device, mesh=fine, in_specs=placed, out_specs=P(ctx, tp), check_vma=False
    )
```

```python
import jax
import jax.numpy as jnp
import numpy as np
from jax import lax
from jax.experimental import pallas as pl
from jax.experimental.pallas import tpu as pltpu
from jax.sharding import Mesh, PartitionSpec as P

GROUP = 16
SHORT_TAPS = 7
LONG_TAPS = 128
LANES = 128
HALO = 144
GRANT = 24 * 1024 * 1024
STREAMS = 3
BF = jnp.bfloat16
F32 = jnp.float32


def shifted(value, axis, steps):
    count = lax.axis_size(axis)
    pairs = [(source, (source + steps) % count) for source in range(count)]
    return lax.ppermute(value, axis, pairs)


def payload_kernel(weight_ref, ids_ref, table_ref, out_ref, upper_ref, lower_ref, sems):
    half = upper_ref.shape[0]
    copies = [
        pltpu.make_async_copy(table_ref.at[pl.ds(0, half), :], upper_ref, sems.at[0]),
        pltpu.make_async_copy(table_ref.at[pl.ds(half, half), :], lower_ref, sems.at[1]),
    ]
    for copy in copies:
        copy.start()
    streams, rows, width = weight_ref.shape
    tiles = width // LANES
    columns = out_ref.shape[0] // tiles
    values = ids_ref[...]
    coded = jnp.where(values < 256, values, 255 - values).astype(F32)
    coded = jnp.concatenate([coded, jnp.zeros_like(coded)], axis=0)
    for tile in range(tiles):
        lanes = slice(tile * LANES, (tile + 1) * LANES)
        pair = jnp.concatenate([weight_ref[0, :, lanes], weight_ref[1, :, lanes]], axis=0)
        third = weight_ref[2, :, lanes].astype(F32)
        third = jnp.concatenate([third, pltpu.roll(third, LANES - 8, 1)], axis=0)
        pair = jnp.transpose(pair.astype(F32))
        third = jnp.transpose(third)
        for part in range(columns):
            to = (tile // 4 * columns + part) * 4 + tile % 4
            at = part * GROUP
            out_ref[to, :GROUP, :] = pair[at : at + GROUP].astype(BF)
            out_ref[to, GROUP:, :] = jnp.concatenate([third[at : at + 8], coded], axis=0).astype(
                BF
            )
    for copy in copies:
        copy.wait()


def in_vmem(count):
    return [pl.BlockSpec(memory_space=pltpu.VMEM)] * count


def cost(flops, moved):
    return pl.CostEstimate(flops=flops, bytes_accessed=moved, transcendentals=0)


def payload(in_weight, ids_rows, embed_table, parts):
    vocab, width = embed_table.shape
    half = jax.ShapeDtypeStruct((vocab // 2, width), BF)
    return pl.pallas_call(
        payload_kernel,
        out_shape=(jax.ShapeDtypeStruct((parts, 2 * GROUP, LANES), BF), half, half),
        in_specs=in_vmem(3),
        out_specs=(pl.BlockSpec(memory_space=pltpu.VMEM),)
        + (pl.BlockSpec(memory_space=pl.ANY),) * 2,
        scratch_shapes=[pltpu.SemaphoreType.DMA((2,))],
        compiler_params=pltpu.CompilerParams(vmem_limit_bytes=GRANT),
        cost_estimate=cost(0, 2900000),
        name="payload",
    )(in_weight, ids_rows, embed_table)


def norm_kernel(spot_ref, *refs):
    shards, gain_ref, out_ref, token_ref = refs[:6], refs[6], refs[7], refs[8]
    token_ref[...] = jnp.zeros_like(token_ref)
    vocab, width = shards[0].shape
    quarter = [spot_ref[j] for j in range(4)]
    chunk = 16

    for half in range(2):
        read = (shards[0], shards[1], shards[2 + half], shards[4 + half])

        def step(i, _, half=half, read=read):
            near = pl.ds(pl.multiple_of(i * chunk, chunk), chunk)
            at = pl.ds(pl.multiple_of(half * (vocab // 2) + i * chunk, chunk), chunk)
            rows = (at, at, near, near)
            squares = 0.0
            for shard, row in zip(read, rows):
                part = shard[row, :].astype(F32)
                squares = squares + jnp.sum(part * part, axis=1, keepdims=True)
            factor = lax.rsqrt(squares / (4 * width) + 1e-06)
            for j, (shard, row) in enumerate(zip(read, rows)):
                gain = gain_ref[:, pl.ds(pl.multiple_of(quarter[j] * width, LANES), width)]
                out_ref[quarter[j], at, :] = (shard[row, :].astype(F32) * factor * gain).astype(BF)
            return 0

        lax.fori_loop(0, vocab // 2 // chunk, step, 0, unroll=2)


def normed_rows(spot, shards, gain):
    vocab, width = shards[0].shape
    return pl.pallas_call(
        norm_kernel,
        out_shape=(
            jax.ShapeDtypeStruct((4, vocab, width), BF),
            jax.ShapeDtypeStruct((8, LANES), F32),
        ),
        in_specs=[pl.BlockSpec(memory_space=pltpu.SMEM)] + in_vmem(7),
        out_specs=tuple(in_vmem(2)),
        compiler_params=pltpu.CompilerParams(vmem_limit_bytes=GRANT),
        cost_estimate=cost(20 * vocab * width, 8 * 2 * vocab * width),
        name="normed_rows",
    )(spot, *shards, gain)


def table_kernel(far_ref, pieces_ref, scale_ref, _, out_ref, weight_ref, normed_ref, sems):
    quarters, _, width = normed_ref.shape
    copies = [
        pltpu.make_async_copy(far_ref.at[q], normed_ref.at[q], sems.at[q]) for q in range(quarters)
    ]
    for copy in copies:
        copy.start()
    low = lax.broadcasted_iota(jnp.int32, (GROUP, LANES), 1) < LANES // 2
    for m in range(pieces_ref.shape[0] // 2):
        lanes = slice(m * LANES, (m + 1) * LANES)
        first = pieces_ref[2 * m, :GROUP, :].astype(F32)
        second = pieces_ref[2 * m + 1, :GROUP, :].astype(F32)
        weight_ref[:GROUP, lanes] = jnp.where(low, first, pltpu.roll(second, 64, 1)).astype(BF)
        weight_ref[GROUP : 2 * GROUP, lanes] = jnp.where(
            low, pltpu.roll(first, 64, 1), second
        ).astype(BF)
        first = pieces_ref[2 * m, GROUP:, :].astype(F32)[:8]
        second = pieces_ref[2 * m + 1, GROUP:, :].astype(F32)[:8]
        third = jnp.concatenate(
            [
                jnp.where(low[:8], first, pltpu.roll(second, 64, 1)),
                jnp.where(low[:8], pltpu.roll(first, 64, 1), second),
            ],
            axis=0,
        )
        weight_ref[2 * GROUP :, lanes] = third.astype(BF)
    total = None
    for q in range(quarters):
        copies[q].wait()
        term = lax.dot_general(
            weight_ref[:, q * width : (q + 1) * width],
            normed_ref[q],
            (((1,), (1,)), ((), ())),
            preferred_element_type=F32,
        )
        total = term if total is None else total + term
    out_ref[...] = (total * scale_ref[...]).astype(BF)


def table_piece(normed, pieces, scale, token):
    quarters, vocab, width = normed.shape
    rows = STREAMS * GROUP
    return pl.pallas_call(
        table_kernel,
        out_shape=jax.ShapeDtypeStruct((rows, vocab), BF),
        in_specs=[pl.BlockSpec(memory_space=pltpu.HBM)] + in_vmem(3),
        out_specs=pl.BlockSpec(memory_space=pltpu.VMEM),
        scratch_shapes=[
            pltpu.VMEM((rows, quarters * width), BF),
            pltpu.VMEM(normed.shape, BF),
            pltpu.SemaphoreType.DMA((quarters,)),
        ],
        compiler_params=pltpu.CompilerParams(vmem_limit_bytes=GRANT),
        cost_estimate=cost(2 * rows * vocab * quarters * width, 5000000),
        name="table_piece",
    )(normed, pieces, scale, token)


def toeplitz_kernel(taps_ref, out_ref):
    for g in range(taps_ref.shape[0]):
        row = jnp.broadcast_to(taps_ref[g : g + 1, :], (LONG_TAPS, 2 * LONG_TAPS))
        block = pltpu.roll(row, 0, 1, stride=1, stride_axis=0)
        out_ref[g] = jnp.transpose(block).astype(BF)


def toeplitz(taps_row):
    groups = taps_row.shape[0]
    return pl.pallas_call(
        toeplitz_kernel,
        out_shape=jax.ShapeDtypeStruct((groups, 2 * LONG_TAPS, LONG_TAPS), BF),
        in_specs=in_vmem(1),
        out_specs=pl.BlockSpec(memory_space=pltpu.VMEM),
        compiler_params=pltpu.CompilerParams(vmem_limit_bytes=GRANT),
        cost_estimate=cost(2000000, 1060000),
        name="toeplitz",
    )(taps_row)


def column_of(coded):
    known = jnp.where(coded < 0.0, 255.0 - coded, coded)
    rows = known.shape[0]
    padded = jnp.concatenate([known, jnp.zeros((8 - rows, LANES), F32)], axis=0)
    return jnp.transpose(padded).astype(jnp.int32)


def one_hot(column, vocab):
    hit = column == lax.broadcasted_iota(jnp.int32, (column.shape[0], vocab), 1)
    return jnp.where(hit, 1.0, 0.0).astype(BF)


def ids_of(pieces_ref, index):
    return pieces_ref[index, GROUP:, :].astype(F32)[8:12]


def hot_kernel(spot_ref, pieces_ref, out_ref, lead_ref):
    z = spot_ref[0]
    step = pl.program_id(0)
    devices = pieces_ref.shape[0]
    half, tokens, vocab = out_ref.shape
    lead = lead_ref.shape[0] // 2

    @pl.when(step == 0)
    def _():
        for segment in range(2):
            start = segment * (devices // 2) + z * 4
            rows = ids_of(pieces_ref, (start + devices - 1) % devices)
            column = column_of(rows[2:])
            column = jnp.concatenate([column[2 * LANES - lead :, 0:1], column[:, 1:2]], axis=0)
            lead_ref[segment * lead : (segment + 1) * lead, :] = one_hot(column, vocab)

    for block in range(half):
        index = step * half + block
        source = index // 4 * (devices // 2) + z * 4 + index % 4
        column = column_of(ids_of(pieces_ref, source))
        for j in range(tokens // LANES):
            out_ref[block, j * LANES : (j + 1) * LANES, :] = one_hot(column[:, j : j + 1], vocab)


def hot_rows(spot, pieces, blocks, tokens, vocab):
    half = 2
    return pl.pallas_call(
        hot_kernel,
        out_shape=(
            jax.ShapeDtypeStruct((blocks, tokens, vocab), BF),
            jax.ShapeDtypeStruct((2 * HALO, vocab), BF),
        ),
        grid=(blocks // half,),
        in_specs=[
            pl.BlockSpec(memory_space=pltpu.SMEM),
            pl.BlockSpec(pieces.shape, lambda i: (0, 0, 0)),
        ],
        out_specs=(
            pl.BlockSpec((half, tokens, vocab), lambda i: (i, 0, 0)),
            pl.BlockSpec((2 * HALO, vocab), lambda i: (0, 0)),
        ),
        compiler_params=pltpu.CompilerParams(vmem_limit_bytes=GRANT),
        cost_estimate=cost(5000000, 4500000),
        name="hot_rows",
    )(spot, pieces)


def mix_kernel(spot_ref, hot_ref, lead_hot_ref, *refs):
    tables = refs[:8]
    filt_ref, toep_ref, out_ref = refs[8:11]
    table_ref, lead_ref, head_ref, edge_ref = refs[11:15]
    next_ref, proj_ref, fresh_ref, inner_ref, fresh_gate_ref, gate_ref, conv_ref, flat_ref = refs[15:]
    step = pl.program_id(0)
    tokens = out_ref.shape[1]
    groups = LANES // GROUP
    margin = proj_ref.shape[1] - tokens
    lead = lead_hot_ref.shape[0] // 2
    chunk = 64

    def short(source, p, start, count):
        total = None
        for k in range(SHORT_TAPS):
            tap = filt_ref[p, k : k + 1, :]
            term = tap * source[p, start - k : start - k + count, :]
            total = term if total is None else total + term
        return total

    @pl.when(step == 0)
    def _():
        for j, piece in enumerate(tables):
            at = (spot_ref[0] + len(tables) - j) % len(tables) * GROUP
            for p in range(STREAMS):
                flat_ref[p, pl.ds(pl.multiple_of(at, GROUP), GROUP), :] = piece[
                    p * GROUP : (p + 1) * GROUP, :
                ]
        for p in range(STREAMS):
            table_ref[:, p * LANES : (p + 1) * LANES] = jnp.transpose(
                flat_ref[p].astype(F32)
            ).astype(BF)
        proj = jnp.dot(lead_hot_ref[...], table_ref[...], preferred_element_type=F32)
        for p in range(STREAMS):
            lead_ref[p] = proj[:, p * LANES : (p + 1) * LANES]
        for segment in range(2):
            for p in range(STREAMS):
                head_ref[segment, p] = lead_ref[
                    p, (segment + 1) * lead - margin : (segment + 1) * lead, :
                ]
            for at in range(0, LONG_TAPS, chunk):
                start = (segment + 1) * lead - LONG_TAPS + at
                fresh_ref[at : at + chunk, :] = short(lead_ref, 1, start, chunk) * short(
                    lead_ref, 2, start, chunk
                )
            edge_ref[segment] = jnp.transpose(fresh_ref[:LONG_TAPS, :]).astype(BF)

    count = tokens // LONG_TAPS

    def select(begin, end):
        proj = jnp.dot(hot_ref[0, begin:end, :], table_ref[...], preferred_element_type=F32)
        for p in range(STREAMS):
            next_ref[p, begin:end, :] = proj[:, p * LANES : (p + 1) * LANES]

    def filtered(at):
        left = short(proj_ref, 1, margin + at, chunk)
        right = short(proj_ref, 2, margin + at, chunk)
        fresh_ref[at : at + chunk, :] = left * right
        fresh_gate_ref[at : at + chunk, :] = short(proj_ref, 0, margin + at, chunk)

    def convolved(g):
        rows = slice(g * GROUP, (g + 1) * GROUP)
        windows = jnp.concatenate(
            [inner_ref[rows, j * LONG_TAPS : (j + 2) * LONG_TAPS] for j in range(count)], axis=0
        )
        full = jnp.dot(windows, toep_ref[g], preferred_element_type=F32)
        for j in range(count):
            conv_ref[j, rows, :] = full[j * GROUP : (j + 1) * GROUP]

    select(0, tokens)
    for g in range(groups):
        convolved(g)
        filtered(g * chunk)

    @pl.when(step >= 0)
    def _():
        for j in range(count):
            at = j * LONG_TAPS
            conv = jnp.transpose(conv_ref[j])
            out_ref[0, at : at + LONG_TAPS, :] = (gate_ref[at : at + LONG_TAPS, :] * conv).astype(BF)

        starts = step % 4 == 0
        segment = jnp.minimum(step // 4, 1)
        for p in range(STREAMS):
            proj_ref[p, :margin, :] = jnp.where(
                starts, head_ref[segment, p], proj_ref[p, tokens:, :]
            )
            proj_ref[p, margin:, :] = next_ref[p]
        starts = (step + 3) % 4 == 0
        segment = jnp.minimum((step + 3) // 4 - 1, 1)
        segment = jnp.maximum(segment, 0)
        inner_ref[:, :LONG_TAPS] = jnp.where(starts, edge_ref[segment], inner_ref[:, tokens:])
        for j in range(count):
            at = j * LONG_TAPS
            inner_ref[:, LONG_TAPS + at : 2 * LONG_TAPS + at] = jnp.transpose(
                fresh_ref[at : at + LONG_TAPS, :]
            ).astype(BF)
        gate_ref[...] = fresh_gate_ref[...]


def mixed_blocks(spot, hot, lead_hot, tables, filt, toep):
    blocks, tokens, vocab = hot.shape
    width = STREAMS * LANES

    def whole(value):
        return pl.BlockSpec(value.shape, lambda i: (0,) * value.ndim)

    return pl.pallas_call(
        mix_kernel,
        out_shape=jax.ShapeDtypeStruct((blocks, tokens, LANES), BF),
        grid=(blocks + 2,),
        in_specs=[
            pl.BlockSpec(memory_space=pltpu.SMEM),
            pl.BlockSpec((1, tokens, vocab), lambda i: (jnp.minimum(i, blocks - 1), 0, 0)),
            whole(lead_hot),
        ]
        + [whole(table) for table in tables]
        + [whole(filt), whole(toep)],
        out_specs=pl.BlockSpec((1, tokens, LANES), lambda i: (jnp.maximum(i - 2, 0), 0, 0)),
        scratch_shapes=[
            pltpu.VMEM((vocab, width), BF),
            pltpu.VMEM((STREAMS, 2 * HALO, LANES), F32),
            pltpu.VMEM((2, STREAMS, 8, LANES), F32),
            pltpu.VMEM((2, LONG_TAPS, LANES), BF),
            pltpu.VMEM((STREAMS, tokens, LANES), F32),
            pltpu.VMEM((STREAMS, tokens + 8, LANES), F32),
            pltpu.VMEM((tokens, LANES), F32),
            pltpu.VMEM((LANES, tokens + LONG_TAPS), BF),
            pltpu.VMEM((tokens, LANES), F32),
            pltpu.VMEM((tokens, LANES), F32),
            pltpu.VMEM((tokens // LONG_TAPS, LANES, LONG_TAPS), F32),
            pltpu.VMEM((STREAMS, LANES, vocab), BF),
        ],
        compiler_params=pltpu.CompilerParams(vmem_limit_bytes=GRANT),
        cost_estimate=cost(5000000000, 6000000),
        name="mixed_blocks",
    )(spot, hot, lead_hot, *tables, filt, toep)


def place_kernel(blocks_ref, out_ref, sems):
    copies = [
        pltpu.make_async_copy(
            blocks_ref.at[j], out_ref.at[:, pl.ds(j * LANES, LANES)], sems.at[j]
        )
        for j in range(blocks_ref.shape[0])
    ]
    for copy in copies:
        copy.start()
    for copy in copies:
        copy.wait()


def placed_columns(blocks):
    count, tokens, lanes = blocks.shape
    return pl.pallas_call(
        place_kernel,
        out_shape=jax.ShapeDtypeStruct((tokens, count * lanes), BF),
        in_specs=in_vmem(1),
        out_specs=pl.BlockSpec(memory_space=pl.ANY),
        scratch_shapes=[pltpu.SemaphoreType.DMA((count,))],
        compiler_params=pltpu.CompilerParams(vmem_limit_bytes=GRANT),
        cost_estimate=cost(0, 2000000),
        name="placed_columns",
    )(blocks)


def per_device(ids, embed_table, norm_gain, in_weight, in_scale, short_filter, long_filter, decay):
    tokens = ids.shape[0]
    vocab, width_local = embed_table.shape
    yh = lax.axis_index("yh")
    z = lax.axis_index("z")
    x = lax.axis_index("x")
    yl = lax.axis_index("yl")
    core = lax.axis_index("core")
    x_count = lax.axis_size("x")
    z_count = lax.axis_size("z")
    ctx = ("yh", "z", "x")
    tile = yh * x_count + x
    tiles = width_local // LANES

    load, upper, lower = payload(in_weight, ids.reshape(-1, LANES), embed_table, tiles * z_count)
    got_up = shifted(upper, ("yh", "yl"), -1)
    got_down = shifted(lower, ("yh", "yl"), 1)
    got_core = shifted(embed_table, "core", 1)
    pieces = lax.all_to_all(load, ctx, 0, 0, tiled=True)

    groups = LANES // GROUP
    steps = jnp.arange(LONG_TAPS, dtype=F32)
    filt = lax.dynamic_slice_in_dim(long_filter, tile * groups, groups, 1)
    rate = lax.dynamic_slice_in_dim(decay, tile * groups, groups, 0)
    filt, rate, load = lax.optimization_barrier((filt, rate, load))
    taps = (filt * jnp.exp(-rate[None, :] * steps[:, None])).astype(BF).astype(F32)
    toep = toeplitz(jnp.pad(taps[::-1].T, ((0, 0), (1, LONG_TAPS - 1))))
    near_filter = lax.dynamic_slice_in_dim(short_filter, tile * LANES, LANES, 2)
    scale = lax.dynamic_slice_in_dim(in_scale, tile * LANES + z * GROUP, GROUP, 1)
    scale = scale.reshape(STREAMS * GROUP, 1)

    far_up = shifted(got_up, "core", 1)
    far_down = shifted(got_down, "core", 1)
    mine = yl * 2 + core
    order = jnp.stack([mine, mine ^ 1, mine ^ 2, mine ^ 3]).astype(jnp.int32)
    normed, token = normed_rows(
        order, [embed_table, got_core, got_up, got_down, far_up, far_down], norm_gain.reshape(1, -1)
    )
    pieces, toep, near_filter, token = lax.optimization_barrier(
        (pieces, toep, near_filter, token)
    )
    piece = table_piece(normed, pieces, scale, token)
    ups, downs, last = [piece], [], piece
    for step in range(4):
        ups.append(shifted(ups[-1], "z", 1))
        if step < 3:
            last = shifted(last, "z", -1)
            downs.append(last)

    spot = z.reshape(1).astype(jnp.int32)
    hot, lead_hot = hot_rows(spot, pieces, tiles, tokens, vocab)
    blocks = mixed_blocks(spot, hot, lead_hot, ups + downs[::-1], near_filter, toep)
    result = lax.all_to_all(blocks, ("yh", "x"), 0, 0, tiled=True)
    return placed_columns(result)


def solution(mesh):
    fine = Mesh(mesh.devices.reshape(2, 8, 4, 2, 2), ("yh", "z", "x", "yl", "core"))
    ctx = ("yh", "z", "x")
    tp = ("yl", "core")
    placed = (
        P(ctx),
        P(None, tp),
        P(),
        P(None, ctx, tp),
        P(None, tp),
        P(None, None, tp),
        P(None, tp),
        P(tp),
    )
    return jax.shard_map(
        per_device, mesh=fine, in_specs=placed, out_specs=P(ctx, tp), check_vma=False
    )
```

```python
import jax
import jax.numpy as jnp
import numpy as np
from jax import lax
from jax.experimental import pallas as pl
from jax.experimental.pallas import tpu as pltpu
from jax.sharding import Mesh, PartitionSpec as P

GROUP = 16
SHORT_TAPS = 7
LONG_TAPS = 128
LANES = 128
HALO = 144
GRANT = 24 * 1024 * 1024
STREAMS = 3
BF = jnp.bfloat16
F32 = jnp.float32


def shifted(value, axis, steps):
    count = lax.axis_size(axis)
    pairs = [(source, (source + steps) % count) for source in range(count)]
    return lax.ppermute(value, axis, pairs)


def payload_kernel(
    far_weight_ref, far_ids_ref, table_ref, out_ref, upper_ref, lower_ref, weight_ref, ids_ref, sems
):
    half = upper_ref.shape[0]
    moves = [
        (far_weight_ref.at[0], weight_ref.at[0]),
        (far_weight_ref.at[1], weight_ref.at[1]),
        (far_weight_ref.at[2], weight_ref.at[2]),
        (far_ids_ref, ids_ref),
        (table_ref.at[pl.ds(0, half), :], upper_ref),
        (table_ref.at[pl.ds(half, half), :], lower_ref),
    ]
    copies = [
        pltpu.make_async_copy(source, target, sems.at[j])
        for j, (source, target) in enumerate(moves)
    ]
    for copy in copies:
        copy.start()
    for copy in copies[:4]:
        copy.wait()
    streams, rows, width = weight_ref.shape
    tiles = width // LANES
    columns = out_ref.shape[0] // tiles
    values = ids_ref[...]
    coded = jnp.where(values < 256, values, 255 - values).astype(F32)
    coded = jnp.concatenate([coded, jnp.zeros_like(coded)], axis=0)
    for tile in range(tiles):
        lanes = slice(tile * LANES, (tile + 1) * LANES)
        pair = jnp.concatenate([weight_ref[0, :, lanes], weight_ref[1, :, lanes]], axis=0)
        third = weight_ref[2, :, lanes].astype(F32)
        third = jnp.concatenate([third, pltpu.roll(third, LANES - 8, 1)], axis=0)
        pair = jnp.transpose(pair.astype(F32))
        third = jnp.transpose(third)
        for part in range(columns):
            to = (tile // 4 * columns + part) * 4 + tile % 4
            at = part * GROUP
            out_ref[to, :GROUP, :] = pair[at : at + GROUP].astype(BF)
            out_ref[to, GROUP:, :] = jnp.concatenate([third[at : at + 8], coded], axis=0).astype(
                BF
            )
    for copy in copies[4:]:
        copy.wait()


def in_vmem(count):
    return [pl.BlockSpec(memory_space=pltpu.VMEM)] * count


def cost(flops, moved):
    return pl.CostEstimate(flops=flops, bytes_accessed=moved, transcendentals=0)


def payload(in_weight, ids_rows, embed_table, parts):
    vocab, width = embed_table.shape
    half = jax.ShapeDtypeStruct((vocab // 2, width), BF)
    return pl.pallas_call(
        payload_kernel,
        out_shape=(jax.ShapeDtypeStruct((parts, 2 * GROUP, LANES), BF), half, half),
        in_specs=[pl.BlockSpec(memory_space=pl.ANY)] * 3,
        out_specs=tuple(in_vmem(3)),
        scratch_shapes=[
            pltpu.VMEM(in_weight.shape, BF),
            pltpu.VMEM(ids_rows.shape, jnp.int32),
            pltpu.SemaphoreType.DMA((6,)),
        ],
        compiler_params=pltpu.CompilerParams(vmem_limit_bytes=66800000),
        cost_estimate=cost(0, 2900000),
        name="payload",
    )(in_weight, ids_rows, embed_table)


def norm_kernel(spot_ref, *refs):
    shards, gain_ref, out_ref, token_ref = refs[:6], refs[6], refs[7], refs[8]
    token_ref[...] = jnp.zeros_like(token_ref)
    vocab, width = shards[0].shape
    quarter = [spot_ref[j] for j in range(4)]
    chunk = 16

    for half in range(2):
        read = (shards[0], shards[1], shards[2 + half], shards[4 + half])

        def step(i, _, half=half, read=read):
            near = pl.ds(pl.multiple_of(i * chunk, chunk), chunk)
            at = pl.ds(pl.multiple_of(half * (vocab // 2) + i * chunk, chunk), chunk)
            rows = (at, at, near, near)
            squares = 0.0
            for shard, row in zip(read, rows):
                part = shard[row, :].astype(F32)
                squares = squares + jnp.sum(part * part, axis=1, keepdims=True)
            factor = lax.rsqrt(squares / (4 * width) + 1e-06)
            for j, (shard, row) in enumerate(zip(read, rows)):
                gain = gain_ref[:, pl.ds(pl.multiple_of(quarter[j] * width, LANES), width)]
                out_ref[quarter[j], at, :] = (shard[row, :].astype(F32) * factor * gain).astype(BF)
            return 0

        lax.fori_loop(0, vocab // 2 // chunk, step, 0, unroll=2)


def normed_rows(spot, shards, gain):
    vocab, width = shards[0].shape
    return pl.pallas_call(
        norm_kernel,
        out_shape=(
            jax.ShapeDtypeStruct((4, vocab, width), BF),
            jax.ShapeDtypeStruct((8, LANES), F32),
        ),
        in_specs=[pl.BlockSpec(memory_space=pltpu.SMEM)] + in_vmem(7),
        out_specs=tuple(in_vmem(2)),
        compiler_params=pltpu.CompilerParams(vmem_limit_bytes=GRANT),
        cost_estimate=cost(20 * vocab * width, 8 * 2 * vocab * width),
        name="normed_rows",
    )(spot, *shards, gain)


def table_kernel(far_ref, pieces_ref, scale_ref, _, out_ref, weight_ref, normed_ref, sems):
    quarters, _, width = normed_ref.shape
    copies = [
        pltpu.make_async_copy(far_ref.at[q], normed_ref.at[q], sems.at[q]) for q in range(quarters)
    ]
    for copy in copies:
        copy.start()
    low = lax.broadcasted_iota(jnp.int32, (GROUP, LANES), 1) < LANES // 2
    for m in range(pieces_ref.shape[0] // 2):
        lanes = slice(m * LANES, (m + 1) * LANES)
        first = pieces_ref[2 * m, :GROUP, :].astype(F32)
        second = pieces_ref[2 * m + 1, :GROUP, :].astype(F32)
        weight_ref[:GROUP, lanes] = jnp.where(low, first, pltpu.roll(second, 64, 1)).astype(BF)
        weight_ref[GROUP : 2 * GROUP, lanes] = jnp.where(
            low, pltpu.roll(first, 64, 1), second
        ).astype(BF)
        first = pieces_ref[2 * m, GROUP:, :].astype(F32)[:8]
        second = pieces_ref[2 * m + 1, GROUP:, :].astype(F32)[:8]
        third = jnp.concatenate(
            [
                jnp.where(low[:8], first, pltpu.roll(second, 64, 1)),
                jnp.where(low[:8], pltpu.roll(first, 64, 1), second),
            ],
            axis=0,
        )
        weight_ref[2 * GROUP :, lanes] = third.astype(BF)
    total = None
    for q in range(quarters):
        copies[q].wait()
        term = lax.dot_general(
            weight_ref[:, q * width : (q + 1) * width],
            normed_ref[q],
            (((1,), (1,)), ((), ())),
            preferred_element_type=F32,
        )
        total = term if total is None else total + term
    out_ref[...] = (total * scale_ref[...]).astype(BF)


def table_piece(normed, pieces, scale, token):
    quarters, vocab, width = normed.shape
    rows = STREAMS * GROUP
    return pl.pallas_call(
        table_kernel,
        out_shape=jax.ShapeDtypeStruct((rows, vocab), BF),
        in_specs=[pl.BlockSpec(memory_space=pl.ANY)] + in_vmem(3),
        out_specs=pl.BlockSpec(memory_space=pltpu.VMEM),
        scratch_shapes=[
            pltpu.VMEM((rows, quarters * width), BF),
            pltpu.VMEM(normed.shape, BF),
            pltpu.SemaphoreType.DMA((quarters,)),
        ],
        compiler_params=pltpu.CompilerParams(vmem_limit_bytes=GRANT),
        cost_estimate=cost(2 * rows * vocab * quarters * width, 5000000),
        name="table_piece",
    )(normed, pieces, scale, token)


def toeplitz_kernel(taps_ref, out_ref):
    for g in range(taps_ref.shape[0]):
        row = jnp.broadcast_to(taps_ref[g : g + 1, :], (LONG_TAPS, 2 * LONG_TAPS))
        block = pltpu.roll(row, 0, 1, stride=1, stride_axis=0)
        out_ref[g] = jnp.transpose(block).astype(BF)


def toeplitz(taps_row):
    groups = taps_row.shape[0]
    return pl.pallas_call(
        toeplitz_kernel,
        out_shape=jax.ShapeDtypeStruct((groups, 2 * LONG_TAPS, LONG_TAPS), BF),
        in_specs=in_vmem(1),
        out_specs=pl.BlockSpec(memory_space=pltpu.VMEM),
        compiler_params=pltpu.CompilerParams(vmem_limit_bytes=GRANT),
        cost_estimate=cost(2000000, 1060000),
        name="toeplitz",
    )(taps_row)


def column_of(coded):
    known = jnp.where(coded < 0.0, 255.0 - coded, coded)
    rows = known.shape[0]
    padded = jnp.concatenate([known, jnp.zeros((8 - rows, LANES), F32)], axis=0)
    return jnp.transpose(padded).astype(jnp.int32)


def one_hot(column, vocab):
    hit = column == lax.broadcasted_iota(jnp.int32, (column.shape[0], vocab), 1)
    return jnp.where(hit, 1.0, 0.0).astype(BF)


def ids_of(pieces_ref, index):
    return pieces_ref[index, GROUP:, :].astype(F32)[8:12]


def hot_kernel(spot_ref, pieces_ref, out_ref, lead_ref):
    z = spot_ref[0]
    step = pl.program_id(0)
    devices = pieces_ref.shape[0]
    half, tokens, vocab = out_ref.shape
    lead = lead_ref.shape[0] // 2

    @pl.when(step == 0)
    def _():
        for segment in range(2):
            start = segment * (devices // 2) + z * 4
            rows = ids_of(pieces_ref, (start + devices - 1) % devices)
            column = column_of(rows[2:])
            column = jnp.concatenate([column[2 * LANES - lead :, 0:1], column[:, 1:2]], axis=0)
            lead_ref[segment * lead : (segment + 1) * lead, :] = one_hot(column, vocab)

    for block in range(half):
        index = step * half + block
        source = index // 4 * (devices // 2) + z * 4 + index % 4
        column = column_of(ids_of(pieces_ref, source))
        for j in range(tokens // LANES):
            out_ref[block, j * LANES : (j + 1) * LANES, :] = one_hot(column[:, j : j + 1], vocab)


def hot_rows(spot, pieces, blocks, tokens, vocab):
    half = 2
    return pl.pallas_call(
        hot_kernel,
        out_shape=(
            jax.ShapeDtypeStruct((blocks, tokens, vocab), BF),
            jax.ShapeDtypeStruct((2 * HALO, vocab), BF),
        ),
        grid=(blocks // half,),
        in_specs=[
            pl.BlockSpec(memory_space=pltpu.SMEM),
            pl.BlockSpec(pieces.shape, lambda i: (0, 0, 0)),
        ],
        out_specs=(
            pl.BlockSpec((half, tokens, vocab), lambda i: (i, 0, 0)),
            pl.BlockSpec((2 * HALO, vocab), lambda i: (0, 0)),
        ),
        compiler_params=pltpu.CompilerParams(vmem_limit_bytes=GRANT),
        cost_estimate=cost(5000000, 4500000),
        name="hot_rows",
    )(spot, pieces)


def mix_kernel(spot_ref, hot_ref, lead_hot_ref, *refs):
    tables = refs[:8]
    filt_ref, toep_ref, out_ref = refs[8:11]
    table_ref, lead_ref, head_ref, edge_ref = refs[11:15]
    next_ref, proj_ref, fresh_ref, inner_ref, fresh_gate_ref, gate_ref, conv_ref, flat_ref = refs[15:]
    step = pl.program_id(0)
    tokens = out_ref.shape[1]
    groups = LANES // GROUP
    margin = proj_ref.shape[1] - tokens
    lead = lead_hot_ref.shape[0] // 2
    chunk = 64

    def short(source, p, start, count):
        total = None
        for k in range(SHORT_TAPS):
            tap = filt_ref[p, k : k + 1, :]
            term = tap * source[p, start - k : start - k + count, :]
            total = term if total is None else total + term
        return total

    @pl.when(step == 0)
    def _():
        for j, piece in enumerate(tables):
            at = (spot_ref[0] + len(tables) - j) % len(tables) * GROUP
            for p in range(STREAMS):
                flat_ref[p, pl.ds(pl.multiple_of(at, GROUP), GROUP), :] = piece[
                    p * GROUP : (p + 1) * GROUP, :
                ]
        for p in range(STREAMS):
            table_ref[:, p * LANES : (p + 1) * LANES] = jnp.transpose(
                flat_ref[p].astype(F32)
            ).astype(BF)
        proj = jnp.dot(lead_hot_ref[...], table_ref[...], preferred_element_type=F32)
        for p in range(STREAMS):
            lead_ref[p] = proj[:, p * LANES : (p + 1) * LANES]
        for segment in range(2):
            for p in range(STREAMS):
                head_ref[segment, p] = lead_ref[
                    p, (segment + 1) * lead - margin : (segment + 1) * lead, :
                ]
            for at in range(0, LONG_TAPS, chunk):
                start = (segment + 1) * lead - LONG_TAPS + at
                fresh_ref[at : at + chunk, :] = short(lead_ref, 1, start, chunk) * short(
                    lead_ref, 2, start, chunk
                )
            edge_ref[segment] = jnp.transpose(fresh_ref[:LONG_TAPS, :]).astype(BF)

    count = tokens // LONG_TAPS

    def select(begin, end):
        proj = jnp.dot(hot_ref[0, begin:end, :], table_ref[...], preferred_element_type=F32)
        for p in range(STREAMS):
            next_ref[p, begin:end, :] = proj[:, p * LANES : (p + 1) * LANES]

    def filtered(at):
        left = short(proj_ref, 1, margin + at, chunk)
        right = short(proj_ref, 2, margin + at, chunk)
        fresh_ref[at : at + chunk, :] = left * right
        fresh_gate_ref[at : at + chunk, :] = short(proj_ref, 0, margin + at, chunk)

    def convolved(g):
        rows = slice(g * GROUP, (g + 1) * GROUP)
        windows = jnp.concatenate(
            [inner_ref[rows, j * LONG_TAPS : (j + 2) * LONG_TAPS] for j in range(count)], axis=0
        )
        full = jnp.dot(windows, toep_ref[g], preferred_element_type=F32)
        for j in range(count):
            conv_ref[j, rows, :] = full[j * GROUP : (j + 1) * GROUP]

    select(0, tokens)
    for g in range(groups):
        convolved(g)
        filtered(g * chunk)

    @pl.when(step >= 0)
    def _():
        for j in range(count):
            at = j * LONG_TAPS
            conv = jnp.transpose(conv_ref[j])
            out_ref[0, at : at + LONG_TAPS, :] = (gate_ref[at : at + LONG_TAPS, :] * conv).astype(BF)

        starts = step % 4 == 0
        segment = jnp.minimum(step // 4, 1)
        for p in range(STREAMS):
            proj_ref[p, :margin, :] = jnp.where(
                starts, head_ref[segment, p], proj_ref[p, tokens:, :]
            )
            proj_ref[p, margin:, :] = next_ref[p]
        starts = (step + 3) % 4 == 0
        segment = jnp.minimum((step + 3) // 4 - 1, 1)
        segment = jnp.maximum(segment, 0)
        inner_ref[:, :LONG_TAPS] = jnp.where(starts, edge_ref[segment], inner_ref[:, tokens:])
        for j in range(count):
            at = j * LONG_TAPS
            inner_ref[:, LONG_TAPS + at : 2 * LONG_TAPS + at] = jnp.transpose(
                fresh_ref[at : at + LONG_TAPS, :]
            ).astype(BF)
        gate_ref[...] = fresh_gate_ref[...]


def mixed_blocks(spot, hot, lead_hot, tables, filt, toep):
    blocks, tokens, vocab = hot.shape
    width = STREAMS * LANES

    def whole(value):
        return pl.BlockSpec(value.shape, lambda i: (0,) * value.ndim)

    return pl.pallas_call(
        mix_kernel,
        out_shape=jax.ShapeDtypeStruct((blocks, tokens, LANES), BF),
        grid=(blocks + 2,),
        in_specs=[
            pl.BlockSpec(memory_space=pltpu.SMEM),
            pl.BlockSpec((1, tokens, vocab), lambda i: (jnp.minimum(i, blocks - 1), 0, 0)),
            whole(lead_hot),
        ]
        + [whole(table) for table in tables]
        + [whole(filt), whole(toep)],
        out_specs=pl.BlockSpec((1, tokens, LANES), lambda i: (jnp.maximum(i - 2, 0), 0, 0)),
        scratch_shapes=[
            pltpu.VMEM((vocab, width), BF),
            pltpu.VMEM((STREAMS, 2 * HALO, LANES), F32),
            pltpu.VMEM((2, STREAMS, 8, LANES), F32),
            pltpu.VMEM((2, LONG_TAPS, LANES), BF),
            pltpu.VMEM((STREAMS, tokens, LANES), F32),
            pltpu.VMEM((STREAMS, tokens + 8, LANES), F32),
            pltpu.VMEM((tokens, LANES), F32),
            pltpu.VMEM((LANES, tokens + LONG_TAPS), BF),
            pltpu.VMEM((tokens, LANES), F32),
            pltpu.VMEM((tokens, LANES), F32),
            pltpu.VMEM((tokens // LONG_TAPS, LANES, LONG_TAPS), F32),
            pltpu.VMEM((STREAMS, LANES, vocab), BF),
        ],
        compiler_params=pltpu.CompilerParams(vmem_limit_bytes=GRANT),
        cost_estimate=cost(5000000000, 6000000),
        name="mixed_blocks",
    )(spot, hot, lead_hot, *tables, filt, toep)


def place_kernel(blocks_ref, out_ref, sems):
    copies = [
        pltpu.make_async_copy(
            blocks_ref.at[j], out_ref.at[:, pl.ds(j * LANES, LANES)], sems.at[j]
        )
        for j in range(blocks_ref.shape[0])
    ]
    for copy in copies:
        copy.start()
    for copy in copies:
        copy.wait()


def placed_columns(blocks):
    count, tokens, lanes = blocks.shape
    return pl.pallas_call(
        place_kernel,
        out_shape=jax.ShapeDtypeStruct((tokens, count * lanes), BF),
        in_specs=in_vmem(1),
        out_specs=pl.BlockSpec(memory_space=pl.ANY),
        scratch_shapes=[pltpu.SemaphoreType.DMA((count,))],
        compiler_params=pltpu.CompilerParams(vmem_limit_bytes=GRANT),
        cost_estimate=cost(0, 2000000),
        name="placed_columns",
    )(blocks)


def per_device(ids, embed_table, norm_gain, in_weight, in_scale, short_filter, long_filter, decay):
    tokens = ids.shape[0]
    vocab, width_local = embed_table.shape
    yh = lax.axis_index("yh")
    z = lax.axis_index("z")
    x = lax.axis_index("x")
    yl = lax.axis_index("yl")
    core = lax.axis_index("core")
    x_count = lax.axis_size("x")
    z_count = lax.axis_size("z")
    ctx = ("yh", "z", "x")
    tile = yh * x_count + x
    tiles = width_local // LANES

    load, upper, lower = payload(in_weight, ids.reshape(-1, LANES), embed_table, tiles * z_count)
    got_up = shifted(upper, ("yh", "yl"), -1)
    got_down = shifted(lower, ("yh", "yl"), 1)
    pieces = lax.all_to_all(load, ctx, 0, 0, tiled=True)

    groups = LANES // GROUP
    steps = jnp.arange(LONG_TAPS, dtype=F32)
    filt = lax.dynamic_slice_in_dim(long_filter, tile * groups, groups, 1)
    rate = lax.dynamic_slice_in_dim(decay, tile * groups, groups, 0)
    filt, rate, load = lax.optimization_barrier((filt, rate, load))
    taps = (filt * jnp.exp(-rate[None, :] * steps[:, None])).astype(BF).astype(F32)
    toep = toeplitz(jnp.pad(taps[::-1].T, ((0, 0), (1, LONG_TAPS - 1))))
    near_filter = lax.dynamic_slice_in_dim(short_filter, tile * LANES, LANES, 2)
    scale = lax.dynamic_slice_in_dim(in_scale, tile * LANES + z * GROUP, GROUP, 1)
    scale = scale.reshape(STREAMS * GROUP, 1)

    swapped, near_filter = lax.optimization_barrier((embed_table, near_filter))
    got_core = shifted(swapped, "core", 1)
    far_up = shifted(got_up, "core", 1)
    far_down = shifted(got_down, "core", 1)
    mine = yl * 2 + core
    order = jnp.stack([mine, mine ^ 1, mine ^ 2, mine ^ 3]).astype(jnp.int32)
    normed, token = normed_rows(
        order, [embed_table, got_core, got_up, got_down, far_up, far_down], norm_gain.reshape(1, -1)
    )
    pieces, toep, near_filter, token = lax.optimization_barrier(
        (pieces, toep, near_filter, token)
    )
    normed = pltpu.with_memory_space_constraint(normed, pltpu.HBM)
    piece = table_piece(normed, pieces, scale, token)
    ups, downs, last = [piece], [], piece
    for step in range(4):
        ups.append(shifted(ups[-1], "z", 1))
        if step < 3:
            last = shifted(last, "z", -1)
            downs.append(last)

    spot = z.reshape(1).astype(jnp.int32)
    hot, lead_hot = hot_rows(spot, pieces, tiles, tokens, vocab)
    blocks = mixed_blocks(spot, hot, lead_hot, ups + downs[::-1], near_filter, toep)
    result = lax.all_to_all(blocks, ("yh", "x"), 0, 0, tiled=True)
    return placed_columns(result)


def solution(mesh):
    fine = Mesh(mesh.devices.reshape(2, 8, 4, 2, 2), ("yh", "z", "x", "yl", "core"))
    ctx = ("yh", "z", "x")
    tp = ("yl", "core")
    placed = (
        P(ctx),
        P(None, tp),
        P(),
        P(None, ctx, tp),
        P(None, tp),
        P(None, None, tp),
        P(None, tp),
        P(tp),
    )
    return jax.shard_map(
        per_device, mesh=fine, in_specs=placed, out_specs=P(ctx, tp), check_vma=False
    )
```

```python
import jax
import jax.numpy as jnp
import numpy as np
from jax import lax
from jax.experimental import pallas as pl
from jax.experimental.pallas import tpu as pltpu
from jax.sharding import Mesh, PartitionSpec as P

GROUP = 16
SHORT_TAPS = 7
LONG_TAPS = 128
LANES = 128
HALO = 144
GRANT = 24 * 1024 * 1024
STREAMS = 3
BF = jnp.bfloat16
F32 = jnp.float32


def shifted(value, axis, steps):
    count = lax.axis_size(axis)
    pairs = [(source, (source + steps) % count) for source in range(count)]
    return lax.ppermute(value, axis, pairs)


def payload_kernel(
    far_weight_ref, table_ref, out_ref, upper_ref, lower_ref, weight_ref, sems
):
    half = upper_ref.shape[0]
    moves = [
        (far_weight_ref.at[0], weight_ref.at[0]),
        (far_weight_ref.at[1], weight_ref.at[1]),
        (far_weight_ref.at[2], weight_ref.at[2]),
        (table_ref.at[pl.ds(0, half), :], upper_ref),
        (table_ref.at[pl.ds(half, half), :], lower_ref),
    ]
    copies = [
        pltpu.make_async_copy(source, target, sems.at[j])
        for j, (source, target) in enumerate(moves)
    ]
    for copy in copies:
        copy.start()
    for copy in copies[:3]:
        copy.wait()
    streams, rows, width = weight_ref.shape
    tiles = width // LANES
    columns = out_ref.shape[0] // tiles
    for tile in range(tiles):
        lanes = slice(tile * LANES, (tile + 1) * LANES)
        pair = jnp.concatenate([weight_ref[0, :, lanes], weight_ref[1, :, lanes]], axis=0)
        third = weight_ref[2, :, lanes].astype(F32)
        third = jnp.concatenate([third, pltpu.roll(third, LANES - 8, 1)], axis=0)
        pair = jnp.transpose(pair.astype(F32))
        third = jnp.transpose(third)
        for part in range(columns):
            to = (tile // 4 * columns + part) * 4 + tile % 4
            at = part * GROUP
            out_ref[to, :GROUP, :] = pair[at : at + GROUP].astype(BF)
            out_ref[to, GROUP:, :] = third[at : at + 8].astype(BF)
    for copy in copies[3:]:
        copy.wait()


def in_vmem(count):
    return [pl.BlockSpec(memory_space=pltpu.VMEM)] * count


def cost(flops, moved):
    return pl.CostEstimate(flops=flops, bytes_accessed=moved, transcendentals=0)


def payload(in_weight, embed_table, parts):
    vocab, width = embed_table.shape
    half = jax.ShapeDtypeStruct((vocab // 2, width), BF)
    return pl.pallas_call(
        payload_kernel,
        out_shape=(jax.ShapeDtypeStruct((parts, GROUP + 8, LANES), BF), half, half),
        in_specs=[pl.BlockSpec(memory_space=pl.ANY)] * 2,
        out_specs=tuple(in_vmem(3)),
        scratch_shapes=[
            pltpu.VMEM(in_weight.shape, BF),
            pltpu.SemaphoreType.DMA((5,)),
        ],
        compiler_params=pltpu.CompilerParams(vmem_limit_bytes=66800000),
        cost_estimate=cost(0, 2900000),
        name="payload",
    )(in_weight, embed_table)


def norm_kernel(spot_ref, *refs):
    shards, gain_ref, out_ref, token_ref = refs[:6], refs[6], refs[7], refs[8]
    token_ref[...] = jnp.zeros_like(token_ref)
    vocab, width = shards[0].shape
    quarter = [spot_ref[j] for j in range(4)]
    chunk = 16

    for half in range(2):
        read = (shards[0], shards[1], shards[2 + half], shards[4 + half])

        def step(i, _, half=half, read=read):
            near = pl.ds(pl.multiple_of(i * chunk, chunk), chunk)
            at = pl.ds(pl.multiple_of(half * (vocab // 2) + i * chunk, chunk), chunk)
            rows = (at, at, near, near)
            squares = 0.0
            for shard, row in zip(read, rows):
                part = shard[row, :].astype(F32)
                squares = squares + jnp.sum(part * part, axis=1, keepdims=True)
            factor = lax.rsqrt(squares / (4 * width) + 1e-06)
            for j, (shard, row) in enumerate(zip(read, rows)):
                gain = gain_ref[:, pl.ds(pl.multiple_of(quarter[j] * width, LANES), width)]
                out_ref[quarter[j], at, :] = (shard[row, :].astype(F32) * factor * gain).astype(BF)
            return 0

        lax.fori_loop(0, vocab // 2 // chunk, step, 0, unroll=2)


def normed_rows(spot, shards, gain):
    vocab, width = shards[0].shape
    return pl.pallas_call(
        norm_kernel,
        out_shape=(
            jax.ShapeDtypeStruct((4, vocab, width), BF),
            jax.ShapeDtypeStruct((8, LANES), F32),
        ),
        in_specs=[pl.BlockSpec(memory_space=pltpu.SMEM)] + in_vmem(7),
        out_specs=tuple(in_vmem(2)),
        compiler_params=pltpu.CompilerParams(vmem_limit_bytes=GRANT),
        cost_estimate=cost(20 * vocab * width, 8 * 2 * vocab * width),
        name="normed_rows",
    )(spot, *shards, gain)


def table_kernel(far_ref, pieces_ref, scale_ref, _, out_ref, weight_ref, normed_ref, sems):
    quarters, _, width = normed_ref.shape
    copies = [
        pltpu.make_async_copy(far_ref.at[q], normed_ref.at[q], sems.at[q]) for q in range(quarters)
    ]
    for copy in copies:
        copy.start()
    low = lax.broadcasted_iota(jnp.int32, (GROUP, LANES), 1) < LANES // 2
    for m in range(pieces_ref.shape[0] // 2):
        lanes = slice(m * LANES, (m + 1) * LANES)
        first = pieces_ref[2 * m, :GROUP, :].astype(F32)
        second = pieces_ref[2 * m + 1, :GROUP, :].astype(F32)
        weight_ref[:GROUP, lanes] = jnp.where(low, first, pltpu.roll(second, 64, 1)).astype(BF)
        weight_ref[GROUP : 2 * GROUP, lanes] = jnp.where(
            low, pltpu.roll(first, 64, 1), second
        ).astype(BF)
        first = pieces_ref[2 * m, GROUP:, :].astype(F32)
        second = pieces_ref[2 * m + 1, GROUP:, :].astype(F32)
        third = jnp.concatenate(
            [
                jnp.where(low[:8], first, pltpu.roll(second, 64, 1)),
                jnp.where(low[:8], pltpu.roll(first, 64, 1), second),
            ],
            axis=0,
        )
        weight_ref[2 * GROUP :, lanes] = third.astype(BF)
    total = None
    for q in range(quarters):
        copies[q].wait()
        term = lax.dot_general(
            weight_ref[:, q * width : (q + 1) * width],
            normed_ref[q],
            (((1,), (1,)), ((), ())),
            preferred_element_type=F32,
        )
        total = term if total is None else total + term
    out_ref[...] = (total * scale_ref[...]).astype(BF)


def table_piece(normed, pieces, scale, token):
    quarters, vocab, width = normed.shape
    rows = STREAMS * GROUP
    return pl.pallas_call(
        table_kernel,
        out_shape=jax.ShapeDtypeStruct((rows, vocab), BF),
        in_specs=[pl.BlockSpec(memory_space=pl.ANY)] + in_vmem(3),
        out_specs=pl.BlockSpec(memory_space=pltpu.VMEM),
        scratch_shapes=[
            pltpu.VMEM((rows, quarters * width), BF),
            pltpu.VMEM(normed.shape, BF),
            pltpu.SemaphoreType.DMA((quarters,)),
        ],
        compiler_params=pltpu.CompilerParams(vmem_limit_bytes=GRANT),
        cost_estimate=cost(2 * rows * vocab * quarters * width, 5000000),
        name="table_piece",
    )(normed, pieces, scale, token)


def toeplitz_kernel(taps_ref, out_ref):
    for g in range(taps_ref.shape[0]):
        row = jnp.broadcast_to(taps_ref[g : g + 1, :], (LONG_TAPS, 2 * LONG_TAPS))
        block = pltpu.roll(row, 0, 1, stride=1, stride_axis=0)
        out_ref[g] = jnp.transpose(block).astype(BF)


def toeplitz(taps_row):
    groups = taps_row.shape[0]
    return pl.pallas_call(
        toeplitz_kernel,
        out_shape=jax.ShapeDtypeStruct((groups, 2 * LONG_TAPS, LONG_TAPS), BF),
        in_specs=in_vmem(1),
        out_specs=pl.BlockSpec(memory_space=pltpu.VMEM),
        compiler_params=pltpu.CompilerParams(vmem_limit_bytes=GRANT),
        cost_estimate=cost(2000000, 1060000),
        name="toeplitz",
    )(taps_row)


def column_of(known):
    rows = known.shape[0]
    padded = jnp.concatenate(
        [known.astype(F32), jnp.zeros((8 - rows, LANES), F32)], axis=0
    )
    return jnp.transpose(padded).astype(jnp.int32)


def one_hot(column, vocab):
    hit = column == lax.broadcasted_iota(jnp.int32, (column.shape[0], vocab), 1)
    return jnp.where(hit, 1.0, 0.0).astype(BF)


def hot_kernel(spot_ref, mine_ref, other_ref, tail_ref, far_tail_ref, out_ref, lead_ref):
    z, yh, x = spot_ref[0], spot_ref[1], spot_ref[2]
    segment = pl.program_id(0) // 2
    half, tokens, vocab = out_ref.shape
    lead = lead_ref.shape[0] // 2
    own = segment == yh

    @pl.when(pl.program_id(0) % 2 == 0)
    def _():
        near = own != (z == 0)
        rows = jnp.where(near, tail_ref[...], far_tail_ref[...])
        column = column_of(rows)
        column = jnp.concatenate([column[2 * LANES - lead :, 0:1], column[:, 1:2]], axis=0)
        at = pl.multiple_of(segment * lead, lead)
        lead_ref[pl.ds(at, lead), :] = one_hot(column, vocab)

    for block in range(half):
        place = (x - (pl.program_id(0) % 2 * half + block) + 4) % 4
        rows = jnp.where(own, mine_ref[place], other_ref[place])
        column = column_of(rows)
        for j in range(tokens // LANES):
            out_ref[block, j * LANES : (j + 1) * LANES, :] = one_hot(column[:, j : j + 1], vocab)


def hot_rows(spot, mine, other, tail, far_tail, tokens, vocab):
    half = 2
    blocks = 2 * mine.shape[0]

    def whole(value):
        return pl.BlockSpec(value.shape, lambda i: (0,) * value.ndim)

    return pl.pallas_call(
        hot_kernel,
        out_shape=(
            jax.ShapeDtypeStruct((blocks, tokens, vocab), BF),
            jax.ShapeDtypeStruct((2 * HALO, vocab), BF),
        ),
        grid=(blocks // half,),
        in_specs=[pl.BlockSpec(memory_space=pltpu.SMEM)]
        + [whole(value) for value in (mine, other, tail, far_tail)],
        out_specs=(
            pl.BlockSpec((half, tokens, vocab), lambda i: (i, 0, 0)),
            pl.BlockSpec((2 * HALO, vocab), lambda i: (0, 0)),
        ),
        compiler_params=pltpu.CompilerParams(vmem_limit_bytes=GRANT),
        cost_estimate=cost(5000000, 4500000),
        name="hot_rows",
    )(spot, mine, other, tail, far_tail)


def mix_kernel(spot_ref, hot_ref, lead_hot_ref, *refs):
    tables = refs[:8]
    filt_ref, toep_ref, out_ref = refs[8:11]
    table_ref, lead_ref, head_ref, edge_ref = refs[11:15]
    next_ref, proj_ref, fresh_ref, inner_ref, fresh_gate_ref, gate_ref, conv_ref, flat_ref = refs[15:]
    step = pl.program_id(0)
    tokens = out_ref.shape[1]
    groups = LANES // GROUP
    margin = proj_ref.shape[1] - tokens
    lead = lead_hot_ref.shape[0] // 2
    chunk = 64

    def short(source, p, start, count):
        total = None
        for k in range(SHORT_TAPS):
            tap = filt_ref[p, k : k + 1, :]
            term = tap * source[p, start - k : start - k + count, :]
            total = term if total is None else total + term
        return total

    @pl.when(step == 0)
    def _():
        for j, piece in enumerate(tables):
            at = (spot_ref[0] + len(tables) - j) % len(tables) * GROUP
            for p in range(STREAMS):
                flat_ref[p, pl.ds(pl.multiple_of(at, GROUP), GROUP), :] = piece[
                    p * GROUP : (p + 1) * GROUP, :
                ]
        for p in range(STREAMS):
            table_ref[:, p * LANES : (p + 1) * LANES] = jnp.transpose(
                flat_ref[p].astype(F32)
            ).astype(BF)
        proj = jnp.dot(lead_hot_ref[...], table_ref[...], preferred_element_type=F32)
        for p in range(STREAMS):
            lead_ref[p] = proj[:, p * LANES : (p + 1) * LANES]
        for segment in range(2):
            for p in range(STREAMS):
                head_ref[segment, p] = lead_ref[
                    p, (segment + 1) * lead - margin : (segment + 1) * lead, :
                ]
            for at in range(0, LONG_TAPS, chunk):
                start = (segment + 1) * lead - LONG_TAPS + at
                fresh_ref[at : at + chunk, :] = short(lead_ref, 1, start, chunk) * short(
                    lead_ref, 2, start, chunk
                )
            edge_ref[segment] = jnp.transpose(fresh_ref[:LONG_TAPS, :]).astype(BF)

    count = tokens // LONG_TAPS

    def select(begin, end):
        proj = jnp.dot(hot_ref[0, begin:end, :], table_ref[...], preferred_element_type=F32)
        for p in range(STREAMS):
            next_ref[p, begin:end, :] = proj[:, p * LANES : (p + 1) * LANES]

    def filtered(at):
        left = short(proj_ref, 1, margin + at, chunk)
        right = short(proj_ref, 2, margin + at, chunk)
        fresh_ref[at : at + chunk, :] = left * right
        fresh_gate_ref[at : at + chunk, :] = short(proj_ref, 0, margin + at, chunk)

    def convolved(g):
        rows = slice(g * GROUP, (g + 1) * GROUP)
        windows = jnp.concatenate(
            [inner_ref[rows, j * LONG_TAPS : (j + 2) * LONG_TAPS] for j in range(count)], axis=0
        )
        full = jnp.dot(windows, toep_ref[g], preferred_element_type=F32)
        for j in range(count):
            conv_ref[j, rows, :] = full[j * GROUP : (j + 1) * GROUP]

    select(0, tokens)
    for g in range(groups):
        convolved(g)
        filtered(g * chunk)

    @pl.when(step >= 0)
    def _():
        for j in range(count):
            at = j * LONG_TAPS
            conv = jnp.transpose(conv_ref[j])
            out_ref[0, at : at + LONG_TAPS, :] = (gate_ref[at : at + LONG_TAPS, :] * conv).astype(BF)

        starts = step % 4 == 0
        segment = jnp.minimum(step // 4, 1)
        for p in range(STREAMS):
            proj_ref[p, :margin, :] = jnp.where(
                starts, head_ref[segment, p], proj_ref[p, tokens:, :]
            )
            proj_ref[p, margin:, :] = next_ref[p]
        starts = (step + 3) % 4 == 0
        segment = jnp.minimum((step + 3) // 4 - 1, 1)
        segment = jnp.maximum(segment, 0)
        inner_ref[:, :LONG_TAPS] = jnp.where(starts, edge_ref[segment], inner_ref[:, tokens:])
        for j in range(count):
            at = j * LONG_TAPS
            inner_ref[:, LONG_TAPS + at : 2 * LONG_TAPS + at] = jnp.transpose(
                fresh_ref[at : at + LONG_TAPS, :]
            ).astype(BF)
        gate_ref[...] = fresh_gate_ref[...]


def mixed_blocks(spot, hot, lead_hot, tables, filt, toep):
    blocks, tokens, vocab = hot.shape
    width = STREAMS * LANES

    def whole(value):
        return pl.BlockSpec(value.shape, lambda i: (0,) * value.ndim)

    return pl.pallas_call(
        mix_kernel,
        out_shape=jax.ShapeDtypeStruct((blocks, tokens, LANES), BF),
        grid=(blocks + 2,),
        in_specs=[
            pl.BlockSpec(memory_space=pltpu.SMEM),
            pl.BlockSpec((1, tokens, vocab), lambda i: (jnp.minimum(i, blocks - 1), 0, 0)),
            whole(lead_hot),
        ]
        + [whole(table) for table in tables]
        + [whole(filt), whole(toep)],
        out_specs=pl.BlockSpec((1, tokens, LANES), lambda i: (jnp.maximum(i - 2, 0), 0, 0)),
        scratch_shapes=[
            pltpu.VMEM((vocab, width), BF),
            pltpu.VMEM((STREAMS, 2 * HALO, LANES), F32),
            pltpu.VMEM((2, STREAMS, 8, LANES), F32),
            pltpu.VMEM((2, LONG_TAPS, LANES), BF),
            pltpu.VMEM((STREAMS, tokens, LANES), F32),
            pltpu.VMEM((STREAMS, tokens + 8, LANES), F32),
            pltpu.VMEM((tokens, LANES), F32),
            pltpu.VMEM((LANES, tokens + LONG_TAPS), BF),
            pltpu.VMEM((tokens, LANES), F32),
            pltpu.VMEM((tokens, LANES), F32),
            pltpu.VMEM((tokens // LONG_TAPS, LANES, LONG_TAPS), F32),
            pltpu.VMEM((STREAMS, LANES, vocab), BF),
        ],
        compiler_params=pltpu.CompilerParams(vmem_limit_bytes=GRANT),
        cost_estimate=cost(5000000000, 6000000),
        name="mixed_blocks",
    )(spot, hot, lead_hot, *tables, filt, toep)


def place_kernel(blocks_ref, out_ref, sems):
    copies = [
        pltpu.make_async_copy(
            blocks_ref.at[j], out_ref.at[:, pl.ds(j * LANES, LANES)], sems.at[j]
        )
        for j in range(blocks_ref.shape[0])
    ]
    for copy in copies:
        copy.start()
    for copy in copies:
        copy.wait()


def placed_columns(blocks):
    count, tokens, lanes = blocks.shape
    return pl.pallas_call(
        place_kernel,
        out_shape=jax.ShapeDtypeStruct((tokens, count * lanes), BF),
        in_specs=in_vmem(1),
        out_specs=pl.BlockSpec(memory_space=pl.ANY),
        scratch_shapes=[pltpu.SemaphoreType.DMA((count,))],
        compiler_params=pltpu.CompilerParams(vmem_limit_bytes=GRANT),
        cost_estimate=cost(0, 2000000),
        name="placed_columns",
    )(blocks)


def per_device(ids, embed_table, norm_gain, in_weight, in_scale, short_filter, long_filter, decay):
    tokens = ids.shape[0]
    vocab, width_local = embed_table.shape
    yh = lax.axis_index("yh")
    z = lax.axis_index("z")
    x = lax.axis_index("x")
    yl = lax.axis_index("yl")
    core = lax.axis_index("core")
    x_count = lax.axis_size("x")
    z_count = lax.axis_size("z")
    ctx = ("yh", "z", "x")
    tile = yh * x_count + x
    tiles = width_local // LANES

    load, upper, lower = payload(in_weight, embed_table, tiles * z_count)
    got_up = shifted(upper, ("yh", "yl"), -1)
    got_down = shifted(lower, ("yh", "yl"), 1)
    pieces = lax.all_to_all(load, ctx, 0, 0, tiled=True)

    groups = LANES // GROUP
    steps = jnp.arange(LONG_TAPS, dtype=F32)
    filt = lax.dynamic_slice_in_dim(long_filter, tile * groups, groups, 1)
    rate = lax.dynamic_slice_in_dim(decay, tile * groups, groups, 0)
    filt, rate, load = lax.optimization_barrier((filt, rate, load))
    taps = (filt * jnp.exp(-rate[None, :] * steps[:, None])).astype(BF).astype(F32)
    toep = toeplitz(jnp.pad(taps[::-1].T, ((0, 0), (1, LONG_TAPS - 1))))
    near_filter = lax.dynamic_slice_in_dim(short_filter, tile * LANES, LANES, 2)
    scale = lax.dynamic_slice_in_dim(in_scale, tile * LANES + z * GROUP, GROUP, 1)
    scale = scale.reshape(STREAMS * GROUP, 1)

    swapped, local, got_up = lax.optimization_barrier(
        (embed_table, ids.reshape(-1, LANES), got_up)
    )
    got_core = shifted(swapped, "core", 1)
    far_up = shifted(got_up, "core", 1)
    far_down = shifted(got_down, "core", 1)
    mine_ids = jnp.stack([local] + [shifted(local, "x", step) for step in (1, 2, 3)])
    other_ids = shifted(mine_ids, "yh", 1)
    last = lax.dynamic_index_in_dim(mine_ids, (x + 1) % x_count, 0, keepdims=False)[2:]
    tail = shifted(last, "z", 1)
    pairs = [
        (a * z_count + b, (1 - a) * z_count + (b + 1) % z_count)
        for a in range(2)
        for b in range(z_count)
    ]
    far_tail = lax.ppermute(last, ("yh", "z"), pairs)
    mine = yl * 2 + core
    order = jnp.stack([mine, mine ^ 1, mine ^ 2, mine ^ 3]).astype(jnp.int32)
    normed, token = normed_rows(
        order, [embed_table, got_core, got_up, got_down, far_up, far_down], norm_gain.reshape(1, -1)
    )
    pieces, toep, near_filter, token, mine_ids, other_ids, tail, far_tail = (
        lax.optimization_barrier(
            (pieces, toep, near_filter, token, mine_ids, other_ids, tail, far_tail)
        )
    )
    normed = pltpu.with_memory_space_constraint(normed, pltpu.HBM)
    piece = table_piece(normed, pieces, scale, token)
    ups, downs, last = [piece], [], piece
    for step in range(4):
        ups.append(shifted(ups[-1], "z", 1))
        if step < 3:
            last = shifted(last, "z", -1)
            downs.append(last)

    spot = jnp.stack([z, yh, x]).astype(jnp.int32)
    hot, lead_hot = hot_rows(spot, mine_ids, other_ids, tail, far_tail, tokens, vocab)
    blocks = mixed_blocks(spot, hot, lead_hot, ups + downs[::-1], near_filter, toep)
    result = lax.all_to_all(blocks, ("yh", "x"), 0, 0, tiled=True)
    return placed_columns(result)


def solution(mesh):
    fine = Mesh(mesh.devices.reshape(2, 8, 4, 2, 2), ("yh", "z", "x", "yl", "core"))
    ctx = ("yh", "z", "x")
    tp = ("yl", "core")
    placed = (
        P(ctx),
        P(None, tp),
        P(),
        P(None, ctx, tp),
        P(None, tp),
        P(None, None, tp),
        P(None, tp),
        P(tp),
    )
    return jax.shard_map(
        per_device, mesh=fine, in_specs=placed, out_specs=P(ctx, tp), check_vma=False
    )
```

```python
import jax
import jax.numpy as jnp
import numpy as np
from jax import lax
from jax.experimental import pallas as pl
from jax.experimental.pallas import tpu as pltpu
from jax.sharding import Mesh, PartitionSpec as P

GROUP = 16
SHORT_TAPS = 7
LONG_TAPS = 128
LANES = 128
HALO = 144
GRANT = 24 * 1024 * 1024
STREAMS = 3
BF = jnp.bfloat16
F32 = jnp.float32


def shifted(value, axis, steps):
    count = lax.axis_size(axis)
    pairs = [(source, (source + steps) % count) for source in range(count)]
    return lax.ppermute(value, axis, pairs)


def payload_kernel(
    far_weight_ref, far_ids_ref, table_ref, out_ref, upper_ref, lower_ref, weight_ref, ids_ref, sems
):
    half = upper_ref.shape[0]
    moves = [
        (far_weight_ref.at[0], weight_ref.at[0]),
        (far_weight_ref.at[1], weight_ref.at[1]),
        (far_weight_ref.at[2], weight_ref.at[2]),
        (far_ids_ref, ids_ref),
        (table_ref.at[pl.ds(0, half), :], upper_ref),
        (table_ref.at[pl.ds(half, half), :], lower_ref),
    ]
    copies = [
        pltpu.make_async_copy(source, target, sems.at[j])
        for j, (source, target) in enumerate(moves)
    ]
    for copy in copies:
        copy.start()
    for copy in copies[:4]:
        copy.wait()
    streams, rows, width = weight_ref.shape
    tiles = width // LANES
    columns = out_ref.shape[0] // tiles
    values = ids_ref[...]
    coded = jnp.where(values < 256, values, 255 - values).astype(F32)
    coded = jnp.concatenate([coded, jnp.zeros_like(coded)], axis=0)
    for tile in range(tiles):
        lanes = slice(tile * LANES, (tile + 1) * LANES)
        pair = jnp.concatenate([weight_ref[0, :, lanes], weight_ref[1, :, lanes]], axis=0)
        third = weight_ref[2, :, lanes].astype(F32)
        third = jnp.concatenate([third, pltpu.roll(third, LANES - 8, 1)], axis=0)
        pair = jnp.transpose(pair.astype(F32))
        third = jnp.transpose(third)
        for part in range(columns):
            to = (tile // 4 * columns + part) * 4 + tile % 4
            at = part * GROUP
            out_ref[to, :GROUP, :] = pair[at : at + GROUP].astype(BF)
            out_ref[to, GROUP:, :] = jnp.concatenate([third[at : at + 8], coded], axis=0).astype(
                BF
            )
    for copy in copies[4:]:
        copy.wait()


def in_vmem(count):
    return [pl.BlockSpec(memory_space=pltpu.VMEM)] * count


def cost(flops, moved):
    return pl.CostEstimate(flops=flops, bytes_accessed=moved, transcendentals=0)


def payload(in_weight, ids_rows, embed_table, parts):
    vocab, width = embed_table.shape
    half = jax.ShapeDtypeStruct((vocab // 2, width), BF)
    return pl.pallas_call(
        payload_kernel,
        out_shape=(jax.ShapeDtypeStruct((parts, 2 * GROUP, LANES), BF), half, half),
        in_specs=[pl.BlockSpec(memory_space=pl.ANY)] * 3,
        out_specs=tuple(in_vmem(3)),
        scratch_shapes=[
            pltpu.VMEM(in_weight.shape, BF),
            pltpu.VMEM(ids_rows.shape, jnp.int32),
            pltpu.SemaphoreType.DMA((6,)),
        ],
        compiler_params=pltpu.CompilerParams(vmem_limit_bytes=66800000),
        cost_estimate=cost(0, 2900000),
        name="payload",
    )(in_weight, ids_rows, embed_table)


def norm_kernel(spot_ref, *refs):
    shards, gain_ref, out_ref, token_ref = refs[:6], refs[6], refs[7], refs[8]
    token_ref[...] = jnp.zeros_like(token_ref)
    vocab, width = shards[0].shape
    quarter = [spot_ref[j] for j in range(4)]
    chunk = 16

    for half in range(2):
        read = (shards[0], shards[1], shards[2 + half], shards[4 + half])

        def step(i, _, half=half, read=read):
            near = pl.ds(pl.multiple_of(i * chunk, chunk), chunk)
            at = pl.ds(pl.multiple_of(half * (vocab // 2) + i * chunk, chunk), chunk)
            rows = (at, at, near, near)
            squares = 0.0
            for shard, row in zip(read, rows):
                part = shard[row, :].astype(F32)
                squares = squares + jnp.sum(part * part, axis=1, keepdims=True)
            factor = lax.rsqrt(squares / (4 * width) + 1e-06)
            for j, (shard, row) in enumerate(zip(read, rows)):
                gain = gain_ref[:, pl.ds(pl.multiple_of(quarter[j] * width, LANES), width)]
                out_ref[quarter[j], at, :] = (shard[row, :].astype(F32) * factor * gain).astype(BF)
            return 0

        lax.fori_loop(0, vocab // 2 // chunk, step, 0, unroll=2)


def normed_rows(spot, shards, gain):
    vocab, width = shards[0].shape
    return pl.pallas_call(
        norm_kernel,
        out_shape=(
            jax.ShapeDtypeStruct((4, vocab, width), BF),
            jax.ShapeDtypeStruct((8, LANES), F32),
        ),
        in_specs=[pl.BlockSpec(memory_space=pltpu.SMEM)] + in_vmem(7),
        out_specs=tuple(in_vmem(2)),
        compiler_params=pltpu.CompilerParams(vmem_limit_bytes=GRANT),
        cost_estimate=cost(20 * vocab * width, 8 * 2 * vocab * width),
        name="normed_rows",
    )(spot, *shards, gain)


def table_kernel(far_ref, pieces_ref, scale_ref, _, out_ref, weight_ref, normed_ref, sems):
    quarters, _, width = normed_ref.shape
    copies = [
        pltpu.make_async_copy(far_ref.at[q], normed_ref.at[q], sems.at[q]) for q in range(quarters)
    ]
    for copy in copies:
        copy.start()
    low = lax.broadcasted_iota(jnp.int32, (GROUP, LANES), 1) < LANES // 2
    for m in range(pieces_ref.shape[0] // 2):
        lanes = slice(m * LANES, (m + 1) * LANES)
        first = pieces_ref[2 * m, :GROUP, :].astype(F32)
        second = pieces_ref[2 * m + 1, :GROUP, :].astype(F32)
        weight_ref[:GROUP, lanes] = jnp.where(low, first, pltpu.roll(second, 64, 1)).astype(BF)
        weight_ref[GROUP : 2 * GROUP, lanes] = jnp.where(
            low, pltpu.roll(first, 64, 1), second
        ).astype(BF)
        first = pieces_ref[2 * m, GROUP:, :].astype(F32)[:8]
        second = pieces_ref[2 * m + 1, GROUP:, :].astype(F32)[:8]
        third = jnp.concatenate(
            [
                jnp.where(low[:8], first, pltpu.roll(second, 64, 1)),
                jnp.where(low[:8], pltpu.roll(first, 64, 1), second),
            ],
            axis=0,
        )
        weight_ref[2 * GROUP :, lanes] = third.astype(BF)
    total = None
    for q in range(quarters):
        copies[q].wait()
        term = lax.dot_general(
            weight_ref[:, q * width : (q + 1) * width],
            normed_ref[q],
            (((1,), (1,)), ((), ())),
            preferred_element_type=F32,
        )
        total = term if total is None else total + term
    out_ref[...] = (total * scale_ref[...]).astype(BF)


def table_piece(normed, pieces, scale, token):
    quarters, vocab, width = normed.shape
    rows = STREAMS * GROUP
    return pl.pallas_call(
        table_kernel,
        out_shape=jax.ShapeDtypeStruct((rows, vocab), BF),
        in_specs=[pl.BlockSpec(memory_space=pl.ANY)] + in_vmem(3),
        out_specs=pl.BlockSpec(memory_space=pltpu.VMEM),
        scratch_shapes=[
            pltpu.VMEM((rows, quarters * width), BF),
            pltpu.VMEM(normed.shape, BF),
            pltpu.SemaphoreType.DMA((quarters,)),
        ],
        compiler_params=pltpu.CompilerParams(vmem_limit_bytes=GRANT),
        cost_estimate=cost(2 * rows * vocab * quarters * width, 5000000),
        name="table_piece",
    )(normed, pieces, scale, token)


def toeplitz_kernel(taps_ref, out_ref):
    for g in range(taps_ref.shape[0]):
        row = jnp.broadcast_to(taps_ref[g : g + 1, :], (LONG_TAPS, 2 * LONG_TAPS))
        block = pltpu.roll(row, 0, 1, stride=1, stride_axis=0)
        out_ref[g] = jnp.transpose(block).astype(BF)


def toeplitz(taps_row):
    groups = taps_row.shape[0]
    return pl.pallas_call(
        toeplitz_kernel,
        out_shape=jax.ShapeDtypeStruct((groups, 2 * LONG_TAPS, LONG_TAPS), BF),
        in_specs=in_vmem(1),
        out_specs=pl.BlockSpec(memory_space=pltpu.VMEM),
        compiler_params=pltpu.CompilerParams(vmem_limit_bytes=GRANT),
        cost_estimate=cost(2000000, 1060000),
        name="toeplitz",
    )(taps_row)


def column_of(coded):
    known = jnp.where(coded < 0.0, 255.0 - coded, coded)
    rows = known.shape[0]
    padded = jnp.concatenate([known, jnp.zeros((8 - rows, LANES), F32)], axis=0)
    return jnp.transpose(padded).astype(jnp.int32)


def one_hot(column, vocab):
    hit = column == lax.broadcasted_iota(jnp.int32, (column.shape[0], vocab), 1)
    return jnp.where(hit, 1.0, 0.0).astype(BF)


def ids_of(pieces_ref, index):
    return pieces_ref[index, GROUP:, :].astype(F32)[8:12]


def hot_kernel(spot_ref, pieces_ref, out_ref, lead_ref):
    z = spot_ref[0]
    step = pl.program_id(0)
    devices = pieces_ref.shape[0]
    half, tokens, vocab = out_ref.shape
    lead = lead_ref.shape[0] // 2

    @pl.when(step == 0)
    def _():
        for segment in range(2):
            start = segment * (devices // 2) + z * 4
            rows = ids_of(pieces_ref, (start + devices - 1) % devices)
            column = column_of(rows[2:])
            column = jnp.concatenate([column[2 * LANES - lead :, 0:1], column[:, 1:2]], axis=0)
            lead_ref[segment * lead : (segment + 1) * lead, :] = one_hot(column, vocab)

    for block in range(half):
        index = step * half + block
        source = index // 4 * (devices // 2) + z * 4 + index % 4
        column = column_of(ids_of(pieces_ref, source))
        for j in range(tokens // LANES):
            out_ref[block, j * LANES : (j + 1) * LANES, :] = one_hot(column[:, j : j + 1], vocab)


def hot_rows(spot, pieces, blocks, tokens, vocab):
    half = 2
    return pl.pallas_call(
        hot_kernel,
        out_shape=(
            jax.ShapeDtypeStruct((blocks, tokens, vocab), BF),
            jax.ShapeDtypeStruct((2 * HALO, vocab), BF),
        ),
        grid=(blocks // half,),
        in_specs=[
            pl.BlockSpec(memory_space=pltpu.SMEM),
            pl.BlockSpec(pieces.shape, lambda i: (0, 0, 0)),
        ],
        out_specs=(
            pl.BlockSpec((half, tokens, vocab), lambda i: (i, 0, 0)),
            pl.BlockSpec((2 * HALO, vocab), lambda i: (0, 0)),
        ),
        compiler_params=pltpu.CompilerParams(vmem_limit_bytes=GRANT),
        cost_estimate=cost(5000000, 4500000),
        name="hot_rows",
    )(spot, pieces)


def mix_kernel(spot_ref, hot_ref, lead_hot_ref, *refs):
    tables = refs[:8]
    filt_ref, toep_ref, out_ref = refs[8:11]
    table_ref, lead_ref, head_ref, edge_ref = refs[11:15]
    next_ref, proj_ref, fresh_ref, inner_ref, fresh_gate_ref, gate_ref, conv_ref, flat_ref = refs[15:]
    step = pl.program_id(0)
    tokens = out_ref.shape[1]
    groups = LANES // GROUP
    margin = proj_ref.shape[1] - tokens
    lead = lead_hot_ref.shape[0] // 2
    chunk = 64

    def short(source, p, start, count):
        total = None
        for k in range(SHORT_TAPS):
            tap = filt_ref[p, k : k + 1, :]
            term = tap * source[p, start - k : start - k + count, :]
            total = term if total is None else total + term
        return total

    @pl.when(step == 0)
    def _():
        for j, piece in enumerate(tables):
            at = (spot_ref[0] + len(tables) - j) % len(tables) * GROUP
            for p in range(STREAMS):
                flat_ref[p, pl.ds(pl.multiple_of(at, GROUP), GROUP), :] = piece[
                    p * GROUP : (p + 1) * GROUP, :
                ]
        for p in range(STREAMS):
            table_ref[:, p * LANES : (p + 1) * LANES] = jnp.transpose(
                flat_ref[p].astype(F32)
            ).astype(BF)
        proj = jnp.dot(lead_hot_ref[...], table_ref[...], preferred_element_type=F32)
        for p in range(STREAMS):
            lead_ref[p] = proj[:, p * LANES : (p + 1) * LANES]
        for segment in range(2):
            for p in range(STREAMS):
                head_ref[segment, p] = lead_ref[
                    p, (segment + 1) * lead - margin : (segment + 1) * lead, :
                ]
            for at in range(0, LONG_TAPS, chunk):
                start = (segment + 1) * lead - LONG_TAPS + at
                fresh_ref[at : at + chunk, :] = short(lead_ref, 1, start, chunk) * short(
                    lead_ref, 2, start, chunk
                )
            edge_ref[segment] = jnp.transpose(fresh_ref[:LONG_TAPS, :]).astype(BF)

    count = tokens // LONG_TAPS

    def select(begin, end):
        proj = jnp.dot(hot_ref[0, begin:end, :], table_ref[...], preferred_element_type=F32)
        for p in range(STREAMS):
            next_ref[p, begin:end, :] = proj[:, p * LANES : (p + 1) * LANES]

    def filtered(at):
        left = short(proj_ref, 1, margin + at, chunk)
        right = short(proj_ref, 2, margin + at, chunk)
        fresh_ref[at : at + chunk, :] = left * right
        fresh_gate_ref[at : at + chunk, :] = short(proj_ref, 0, margin + at, chunk)

    def convolved(g):
        rows = slice(g * GROUP, (g + 1) * GROUP)
        windows = jnp.concatenate(
            [inner_ref[rows, j * LONG_TAPS : (j + 2) * LONG_TAPS] for j in range(count)], axis=0
        )
        full = jnp.dot(windows, toep_ref[g], preferred_element_type=F32)
        for j in range(count):
            conv_ref[j, rows, :] = full[j * GROUP : (j + 1) * GROUP]

    final = pl.num_programs(0) - 1

    @pl.when(step == 0)
    def _():
        select(0, tokens)

    @pl.when((step > 0) & (step < final))
    def _():
        select(0, tokens)
        for g in range(groups):
            convolved(g)
            filtered(g * chunk)

    @pl.when(step == final)
    def _():
        for g in range(groups):
            convolved(g)

    @pl.when(step >= 0)
    def _():
        for j in range(count):
            at = j * LONG_TAPS
            conv = jnp.transpose(conv_ref[j])
            out_ref[0, at : at + LONG_TAPS, :] = (gate_ref[at : at + LONG_TAPS, :] * conv).astype(BF)

        starts = step % 4 == 0
        segment = jnp.minimum(step // 4, 1)
        for p in range(STREAMS):
            proj_ref[p, :margin, :] = jnp.where(
                starts, head_ref[segment, p], proj_ref[p, tokens:, :]
            )
            proj_ref[p, margin:, :] = next_ref[p]
        starts = (step + 3) % 4 == 0
        segment = jnp.minimum((step + 3) // 4 - 1, 1)
        segment = jnp.maximum(segment, 0)
        inner_ref[:, :LONG_TAPS] = jnp.where(starts, edge_ref[segment], inner_ref[:, tokens:])
        for j in range(count):
            at = j * LONG_TAPS
            inner_ref[:, LONG_TAPS + at : 2 * LONG_TAPS + at] = jnp.transpose(
                fresh_ref[at : at + LONG_TAPS, :]
            ).astype(BF)
        gate_ref[...] = fresh_gate_ref[...]


def mixed_blocks(spot, hot, lead_hot, tables, filt, toep):
    blocks, tokens, vocab = hot.shape
    width = STREAMS * LANES

    def whole(value):
        return pl.BlockSpec(value.shape, lambda i: (0,) * value.ndim)

    return pl.pallas_call(
        mix_kernel,
        out_shape=jax.ShapeDtypeStruct((blocks, tokens, LANES), BF),
        grid=(blocks + 2,),
        in_specs=[
            pl.BlockSpec(memory_space=pltpu.SMEM),
            pl.BlockSpec((1, tokens, vocab), lambda i: (jnp.minimum(i, blocks - 1), 0, 0)),
            whole(lead_hot),
        ]
        + [whole(table) for table in tables]
        + [whole(filt), whole(toep)],
        out_specs=pl.BlockSpec((1, tokens, LANES), lambda i: (jnp.maximum(i - 2, 0), 0, 0)),
        scratch_shapes=[
            pltpu.VMEM((vocab, width), BF),
            pltpu.VMEM((STREAMS, 2 * HALO, LANES), F32),
            pltpu.VMEM((2, STREAMS, 8, LANES), F32),
            pltpu.VMEM((2, LONG_TAPS, LANES), BF),
            pltpu.VMEM((STREAMS, tokens, LANES), F32),
            pltpu.VMEM((STREAMS, tokens + 8, LANES), F32),
            pltpu.VMEM((tokens, LANES), F32),
            pltpu.VMEM((LANES, tokens + LONG_TAPS), BF),
            pltpu.VMEM((tokens, LANES), F32),
            pltpu.VMEM((tokens, LANES), F32),
            pltpu.VMEM((tokens // LONG_TAPS, LANES, LONG_TAPS), F32),
            pltpu.VMEM((STREAMS, LANES, vocab), BF),
        ],
        compiler_params=pltpu.CompilerParams(vmem_limit_bytes=GRANT),
        cost_estimate=cost(5000000000, 6000000),
        name="mixed_blocks",
    )(spot, hot, lead_hot, *tables, filt, toep)


def place_kernel(blocks_ref, out_ref, sems):
    copies = [
        pltpu.make_async_copy(
            blocks_ref.at[j], out_ref.at[:, pl.ds(j * LANES, LANES)], sems.at[j]
        )
        for j in range(blocks_ref.shape[0])
    ]
    for copy in copies:
        copy.start()
    for copy in copies:
        copy.wait()


def placed_columns(blocks):
    count, tokens, lanes = blocks.shape
    return pl.pallas_call(
        place_kernel,
        out_shape=jax.ShapeDtypeStruct((tokens, count * lanes), BF),
        in_specs=in_vmem(1),
        out_specs=pl.BlockSpec(memory_space=pl.ANY),
        scratch_shapes=[pltpu.SemaphoreType.DMA((count,))],
        compiler_params=pltpu.CompilerParams(vmem_limit_bytes=GRANT),
        cost_estimate=cost(0, 2000000),
        name="placed_columns",
    )(blocks)


def per_device(ids, embed_table, norm_gain, in_weight, in_scale, short_filter, long_filter, decay):
    tokens = ids.shape[0]
    vocab, width_local = embed_table.shape
    yh = lax.axis_index("yh")
    z = lax.axis_index("z")
    x = lax.axis_index("x")
    yl = lax.axis_index("yl")
    core = lax.axis_index("core")
    x_count = lax.axis_size("x")
    z_count = lax.axis_size("z")
    ctx = ("yh", "z", "x")
    tile = yh * x_count + x
    tiles = width_local // LANES

    load, upper, lower = payload(in_weight, ids.reshape(-1, LANES), embed_table, tiles * z_count)
    got_up = shifted(upper, ("yh", "yl"), -1)
    got_down = shifted(lower, ("yh", "yl"), 1)
    pieces = lax.all_to_all(load, ctx, 0, 0, tiled=True)

    groups = LANES // GROUP
    steps = jnp.arange(LONG_TAPS, dtype=F32)
    filt = lax.dynamic_slice_in_dim(long_filter, tile * groups, groups, 1)
    rate = lax.dynamic_slice_in_dim(decay, tile * groups, groups, 0)
    filt, rate, load = lax.optimization_barrier((filt, rate, load))
    taps = (filt * jnp.exp(-rate[None, :] * steps[:, None])).astype(BF).astype(F32)
    toep = toeplitz(jnp.pad(taps[::-1].T, ((0, 0), (1, LONG_TAPS - 1))))
    near_filter = lax.dynamic_slice_in_dim(short_filter, tile * LANES, LANES, 2)
    scale = lax.dynamic_slice_in_dim(in_scale, tile * LANES + z * GROUP, GROUP, 1)
    scale = scale.reshape(STREAMS * GROUP, 1)

    swapped, near_filter = lax.optimization_barrier((embed_table, near_filter))
    got_core = shifted(swapped, "core", 1)
    far_up = shifted(got_up, "core", 1)
    far_down = shifted(got_down, "core", 1)
    mine = yl * 2 + core
    order = jnp.stack([mine, mine ^ 1, mine ^ 2, mine ^ 3]).astype(jnp.int32)
    normed, token = normed_rows(
        order, [embed_table, got_core, got_up, got_down, far_up, far_down], norm_gain.reshape(1, -1)
    )
    pieces, toep, near_filter, token = lax.optimization_barrier(
        (pieces, toep, near_filter, token)
    )
    normed = pltpu.with_memory_space_constraint(normed, pltpu.HBM)
    piece = table_piece(normed, pieces, scale, token)
    ups, downs, last = [piece], [], piece
    for step in range(4):
        ups.append(shifted(ups[-1], "z", 1))
        if step < 3:
            last = shifted(last, "z", -1)
            downs.append(last)

    spot = z.reshape(1).astype(jnp.int32)
    hot, lead_hot = hot_rows(spot, pieces, tiles, tokens, vocab)
    blocks = mixed_blocks(spot, hot, lead_hot, ups + downs[::-1], near_filter, toep)
    result = lax.all_to_all(blocks, ("yh", "x"), 0, 0, tiled=True)
    return placed_columns(result)


def solution(mesh):
    fine = Mesh(mesh.devices.reshape(2, 8, 4, 2, 2), ("yh", "z", "x", "yl", "core"))
    ctx = ("yh", "z", "x")
    tp = ("yl", "core")
    placed = (
        P(ctx),
        P(None, tp),
        P(),
        P(None, ctx, tp),
        P(None, tp),
        P(None, None, tp),
        P(None, tp),
        P(tp),
    )
    return jax.shard_map(
        per_device, mesh=fine, in_specs=placed, out_specs=P(ctx, tp), check_vma=False
    )
```

```python
import jax
import jax.numpy as jnp
import numpy as np
from jax import lax
from jax.experimental import pallas as pl
from jax.experimental.pallas import tpu as pltpu
from jax.sharding import Mesh, PartitionSpec as P

GROUP = 16
SHORT_TAPS = 7
LONG_TAPS = 128
LANES = 128
HALO = 144
GRANT = 24 * 1024 * 1024
STREAMS = 3
BF = jnp.bfloat16
F32 = jnp.float32


def shifted(value, axis, steps):
    count = lax.axis_size(axis)
    pairs = [(source, (source + steps) % count) for source in range(count)]
    return lax.ppermute(value, axis, pairs)


def payload_kernel(
    far_weight_ref, far_ids_ref, table_ref, out_ref, upper_ref, lower_ref, weight_ref, ids_ref, sems
):
    half = upper_ref.shape[0]
    moves = [
        (far_weight_ref.at[0], weight_ref.at[0]),
        (far_weight_ref.at[1], weight_ref.at[1]),
        (far_weight_ref.at[2], weight_ref.at[2]),
        (far_ids_ref, ids_ref),
        (table_ref.at[pl.ds(0, half), :], upper_ref),
        (table_ref.at[pl.ds(half, half), :], lower_ref),
    ]
    copies = [
        pltpu.make_async_copy(source, target, sems.at[j])
        for j, (source, target) in enumerate(moves)
    ]
    for copy in copies:
        copy.start()
    for copy in copies[:4]:
        copy.wait()
    streams, rows, width = weight_ref.shape
    tiles = width // LANES
    columns = out_ref.shape[0] // tiles
    values = ids_ref[...]
    coded = jnp.where(values < 256, values, 255 - values).astype(F32)
    coded = jnp.concatenate([coded, jnp.zeros_like(coded)], axis=0)
    for tile in range(tiles):
        lanes = slice(tile * LANES, (tile + 1) * LANES)
        pair = jnp.concatenate([weight_ref[0, :, lanes], weight_ref[1, :, lanes]], axis=0)
        third = weight_ref[2, :, lanes].astype(F32)
        third = jnp.concatenate([third, pltpu.roll(third, LANES - 8, 1)], axis=0)
        pair = jnp.transpose(pair.astype(F32))
        third = jnp.transpose(third)
        for part in range(columns):
            to = (tile // 4 * columns + part) * 4 + tile % 4
            at = part * GROUP
            out_ref[to, :GROUP, :] = pair[at : at + GROUP].astype(BF)
            out_ref[to, GROUP:, :] = jnp.concatenate([third[at : at + 8], coded], axis=0).astype(
                BF
            )
    for copy in copies[4:]:
        copy.wait()


def in_vmem(count):
    return [pl.BlockSpec(memory_space=pltpu.VMEM)] * count


def cost(flops, moved):
    return pl.CostEstimate(flops=flops, bytes_accessed=moved, transcendentals=0)


def payload(in_weight, ids_rows, embed_table, parts):
    vocab, width = embed_table.shape
    half = jax.ShapeDtypeStruct((vocab // 2, width), BF)
    return pl.pallas_call(
        payload_kernel,
        out_shape=(jax.ShapeDtypeStruct((parts, 2 * GROUP, LANES), BF), half, half),
        in_specs=[pl.BlockSpec(memory_space=pl.ANY)] * 3,
        out_specs=tuple(in_vmem(3)),
        scratch_shapes=[
            pltpu.VMEM(in_weight.shape, BF),
            pltpu.VMEM(ids_rows.shape, jnp.int32),
            pltpu.SemaphoreType.DMA((6,)),
        ],
        compiler_params=pltpu.CompilerParams(vmem_limit_bytes=66800000),
        cost_estimate=cost(0, 2900000),
        name="payload",
    )(in_weight, ids_rows, embed_table)


def norm_kernel(spot_ref, *refs):
    shards, gain_ref, out_ref, token_ref = refs[:6], refs[6], refs[7], refs[8]
    token_ref[...] = jnp.zeros_like(token_ref)
    vocab, width = shards[0].shape
    quarter = [spot_ref[j] for j in range(4)]
    chunk = 16

    for half in range(2):
        read = (shards[0], shards[1], shards[2 + half], shards[4 + half])

        def step(i, _, half=half, read=read):
            near = pl.ds(pl.multiple_of(i * chunk, chunk), chunk)
            at = pl.ds(pl.multiple_of(half * (vocab // 2) + i * chunk, chunk), chunk)
            rows = (at, at, near, near)
            squares = 0.0
            for shard, row in zip(read, rows):
                part = shard[row, :].astype(F32)
                squares = squares + jnp.sum(part * part, axis=1, keepdims=True)
            factor = lax.rsqrt(squares / (4 * width) + 1e-06)
            for j, (shard, row) in enumerate(zip(read, rows)):
                gain = gain_ref[:, pl.ds(pl.multiple_of(quarter[j] * width, LANES), width)]
                out_ref[quarter[j], at, :] = (shard[row, :].astype(F32) * factor * gain).astype(BF)
            return 0

        lax.fori_loop(0, vocab // 2 // chunk, step, 0, unroll=2)


def normed_rows(spot, shards, gain):
    vocab, width = shards[0].shape
    return pl.pallas_call(
        norm_kernel,
        out_shape=(
            jax.ShapeDtypeStruct((4, vocab, width), BF),
            jax.ShapeDtypeStruct((8, LANES), F32),
        ),
        in_specs=[pl.BlockSpec(memory_space=pltpu.SMEM)] + in_vmem(7),
        out_specs=tuple(in_vmem(2)),
        compiler_params=pltpu.CompilerParams(vmem_limit_bytes=GRANT),
        cost_estimate=cost(20 * vocab * width, 8 * 2 * vocab * width),
        name="normed_rows",
    )(spot, *shards, gain)


def table_kernel(far_ref, pieces_ref, scale_ref, _, out_ref, weight_ref, normed_ref, sems):
    quarters, _, width = normed_ref.shape
    copies = [
        pltpu.make_async_copy(far_ref.at[q], normed_ref.at[q], sems.at[q]) for q in range(quarters)
    ]
    for copy in copies:
        copy.start()
    low = lax.broadcasted_iota(jnp.int32, (GROUP, LANES), 1) < LANES // 2
    for m in range(pieces_ref.shape[0] // 2):
        lanes = slice(m * LANES, (m + 1) * LANES)
        first = pieces_ref[2 * m, :GROUP, :].astype(F32)
        second = pieces_ref[2 * m + 1, :GROUP, :].astype(F32)
        weight_ref[:GROUP, lanes] = jnp.where(low, first, pltpu.roll(second, 64, 1)).astype(BF)
        weight_ref[GROUP : 2 * GROUP, lanes] = jnp.where(
            low, pltpu.roll(first, 64, 1), second
        ).astype(BF)
        first = pieces_ref[2 * m, GROUP:, :].astype(F32)[:8]
        second = pieces_ref[2 * m + 1, GROUP:, :].astype(F32)[:8]
        third = jnp.concatenate(
            [
                jnp.where(low[:8], first, pltpu.roll(second, 64, 1)),
                jnp.where(low[:8], pltpu.roll(first, 64, 1), second),
            ],
            axis=0,
        )
        weight_ref[2 * GROUP :, lanes] = third.astype(BF)
    total = None
    for q in range(quarters):
        copies[q].wait()
        term = lax.dot_general(
            weight_ref[:, q * width : (q + 1) * width],
            normed_ref[q],
            (((1,), (1,)), ((), ())),
            preferred_element_type=F32,
        )
        total = term if total is None else total + term
    out_ref[...] = (total * scale_ref[...]).astype(BF)


def table_piece(normed, pieces, scale, token):
    quarters, vocab, width = normed.shape
    rows = STREAMS * GROUP
    return pl.pallas_call(
        table_kernel,
        out_shape=jax.ShapeDtypeStruct((rows, vocab), BF),
        in_specs=[pl.BlockSpec(memory_space=pl.ANY)] + in_vmem(3),
        out_specs=pl.BlockSpec(memory_space=pltpu.VMEM),
        scratch_shapes=[
            pltpu.VMEM((rows, quarters * width), BF),
            pltpu.VMEM(normed.shape, BF),
            pltpu.SemaphoreType.DMA((quarters,)),
        ],
        compiler_params=pltpu.CompilerParams(vmem_limit_bytes=GRANT),
        cost_estimate=cost(2 * rows * vocab * quarters * width, 5000000),
        name="table_piece",
    )(normed, pieces, scale, token)


def toeplitz_kernel(taps_ref, out_ref):
    for g in range(taps_ref.shape[0]):
        row = jnp.broadcast_to(taps_ref[g : g + 1, :], (LONG_TAPS, 2 * LONG_TAPS))
        block = pltpu.roll(row, 0, 1, stride=1, stride_axis=0)
        out_ref[g] = jnp.transpose(block).astype(BF)


def toeplitz(taps_row):
    groups = taps_row.shape[0]
    return pl.pallas_call(
        toeplitz_kernel,
        out_shape=jax.ShapeDtypeStruct((groups, 2 * LONG_TAPS, LONG_TAPS), BF),
        in_specs=in_vmem(1),
        out_specs=pl.BlockSpec(memory_space=pltpu.VMEM),
        compiler_params=pltpu.CompilerParams(vmem_limit_bytes=GRANT),
        cost_estimate=cost(2000000, 1060000),
        name="toeplitz",
    )(taps_row)


def column_of(coded):
    known = jnp.where(coded < 0.0, 255.0 - coded, coded)
    rows = known.shape[0]
    padded = jnp.concatenate([known, jnp.zeros((8 - rows, LANES), F32)], axis=0)
    return jnp.transpose(padded).astype(jnp.int32)


def one_hot(column, vocab):
    hit = column == lax.broadcasted_iota(jnp.int32, (column.shape[0], vocab), 1)
    return jnp.where(hit, 1.0, 0.0).astype(BF)


def ids_of(pieces_ref, index):
    return pieces_ref[index, GROUP:, :].astype(F32)[8:12]


def hot_kernel(spot_ref, pieces_ref, out_ref, lead_ref):
    z = spot_ref[0]
    step = pl.program_id(0)
    devices = pieces_ref.shape[0]
    half, tokens, vocab = out_ref.shape
    lead = lead_ref.shape[0] // 2

    @pl.when(step == 0)
    def _():
        for segment in range(2):
            start = segment * (devices // 2) + z * 4
            rows = ids_of(pieces_ref, (start + devices - 1) % devices)
            column = column_of(rows[2:])
            column = jnp.concatenate([column[2 * LANES - lead :, 0:1], column[:, 1:2]], axis=0)
            lead_ref[segment * lead : (segment + 1) * lead, :] = one_hot(column, vocab)

    for block in range(half):
        index = step * half + block
        source = index // 4 * (devices // 2) + z * 4 + index % 4
        column = column_of(ids_of(pieces_ref, source))
        for j in range(tokens // LANES):
            out_ref[block, j * LANES : (j + 1) * LANES, :] = one_hot(column[:, j : j + 1], vocab)


def hot_rows(spot, pieces, blocks, tokens, vocab):
    half = 2
    return pl.pallas_call(
        hot_kernel,
        out_shape=(
            jax.ShapeDtypeStruct((blocks, tokens, vocab), BF),
            jax.ShapeDtypeStruct((2 * HALO, vocab), BF),
        ),
        grid=(blocks // half,),
        in_specs=[
            pl.BlockSpec(memory_space=pltpu.SMEM),
            pl.BlockSpec(pieces.shape, lambda i: (0, 0, 0)),
        ],
        out_specs=(
            pl.BlockSpec((half, tokens, vocab), lambda i: (i, 0, 0)),
            pl.BlockSpec((2 * HALO, vocab), lambda i: (0, 0)),
        ),
        compiler_params=pltpu.CompilerParams(vmem_limit_bytes=GRANT),
        cost_estimate=cost(5000000, 4500000),
        name="hot_rows",
    )(spot, pieces)


def mix_kernel(spot_ref, hot_ref, lead_hot_ref, *refs):
    tables = refs[:8]
    filt_ref, toep_ref, out_ref = refs[8:11]
    table_ref, lead_ref, head_ref, edge_ref = refs[11:15]
    next_ref, proj_ref, fresh_ref, inner_ref, fresh_gate_ref, gate_ref, conv_ref, flat_ref = refs[15:]
    step = pl.program_id(0)
    tokens = out_ref.shape[1]
    groups = LANES // GROUP
    margin = proj_ref.shape[1] - tokens
    lead = lead_hot_ref.shape[0] // 2
    chunk = 64

    def short(source, p, start, count):
        total = None
        for k in range(SHORT_TAPS):
            tap = filt_ref[p, k : k + 1, :]
            term = tap * source[p, start - k : start - k + count, :]
            total = term if total is None else total + term
        return total

    @pl.when(step == 0)
    def _():
        for j, piece in enumerate(tables):
            at = (spot_ref[0] + len(tables) - j) % len(tables) * GROUP
            for p in range(STREAMS):
                flat_ref[p, pl.ds(pl.multiple_of(at, GROUP), GROUP), :] = piece[
                    p * GROUP : (p + 1) * GROUP, :
                ]
        for p in range(STREAMS):
            table_ref[:, p * LANES : (p + 1) * LANES] = jnp.transpose(
                flat_ref[p].astype(F32)
            ).astype(BF)
        proj = jnp.dot(lead_hot_ref[...], table_ref[...], preferred_element_type=F32)
        for p in range(STREAMS):
            lead_ref[p] = proj[:, p * LANES : (p + 1) * LANES]
        for segment in range(2):
            for p in range(STREAMS):
                head_ref[segment, p] = lead_ref[
                    p, (segment + 1) * lead - margin : (segment + 1) * lead, :
                ]
            for at in range(0, LONG_TAPS, chunk):
                start = (segment + 1) * lead - LONG_TAPS + at
                fresh_ref[at : at + chunk, :] = short(lead_ref, 1, start, chunk) * short(
                    lead_ref, 2, start, chunk
                )
            edge_ref[segment] = jnp.transpose(fresh_ref[:LONG_TAPS, :]).astype(BF)

    count = tokens // LONG_TAPS

    def select(begin, end):
        proj = jnp.dot(hot_ref[0, begin:end, :], table_ref[...], preferred_element_type=F32)
        for p in range(STREAMS):
            next_ref[p, begin:end, :] = proj[:, p * LANES : (p + 1) * LANES]

    def filtered(at):
        left = short(proj_ref, 1, margin + at, chunk)
        right = short(proj_ref, 2, margin + at, chunk)
        fresh_ref[at : at + chunk, :] = left * right
        fresh_gate_ref[at : at + chunk, :] = short(proj_ref, 0, margin + at, chunk)

    def convolved(g):
        rows = slice(g * GROUP, (g + 1) * GROUP)
        windows = jnp.concatenate(
            [inner_ref[rows, j * LONG_TAPS : (j + 2) * LONG_TAPS] for j in range(count)], axis=0
        )
        full = jnp.dot(windows, toep_ref[g], preferred_element_type=F32)
        for j in range(count):
            conv_ref[j, rows, :] = full[j * GROUP : (j + 1) * GROUP]

    final = pl.num_programs(0) - 1

    @pl.when(step == 0)
    def _():
        select(0, tokens)

    @pl.when((step > 0) & (step < final))
    def _():
        select(0, tokens)
        for g in range(groups):
            convolved(g)
            filtered(g * chunk)

    @pl.when(step == final)
    def _():
        for g in range(groups):
            convolved(g)

    @pl.when(step >= 0)
    def _():
        starts = step % 4 == 0
        segment = jnp.minimum(step // 4, 1)
        for p in range(STREAMS):
            proj_ref[p, :margin, :] = jnp.where(
                starts, head_ref[segment, p], proj_ref[p, tokens:, :]
            )
            proj_ref[p, margin:, :] = next_ref[p]
        for j in range(count):
            at = j * LONG_TAPS
            conv = jnp.transpose(conv_ref[j])
            out_ref[0, at : at + LONG_TAPS, :] = (gate_ref[at : at + LONG_TAPS, :] * conv).astype(BF)
        starts = (step + 3) % 4 == 0
        segment = jnp.minimum((step + 3) // 4 - 1, 1)
        segment = jnp.maximum(segment, 0)
        inner_ref[:, :LONG_TAPS] = jnp.where(starts, edge_ref[segment], inner_ref[:, tokens:])
        for j in range(count):
            at = j * LONG_TAPS
            inner_ref[:, LONG_TAPS + at : 2 * LONG_TAPS + at] = jnp.transpose(
                fresh_ref[at : at + LONG_TAPS, :]
            ).astype(BF)
        gate_ref[...] = fresh_gate_ref[...]


def mixed_blocks(spot, hot, lead_hot, tables, filt, toep):
    blocks, tokens, vocab = hot.shape
    width = STREAMS * LANES

    def whole(value):
        return pl.BlockSpec(value.shape, lambda i: (0,) * value.ndim)

    return pl.pallas_call(
        mix_kernel,
        out_shape=jax.ShapeDtypeStruct((blocks, tokens, LANES), BF),
        grid=(blocks + 2,),
        in_specs=[
            pl.BlockSpec(memory_space=pltpu.SMEM),
            pl.BlockSpec((1, tokens, vocab), lambda i: (jnp.minimum(i, blocks - 1), 0, 0)),
            whole(lead_hot),
        ]
        + [whole(table) for table in tables]
        + [whole(filt), whole(toep)],
        out_specs=pl.BlockSpec((1, tokens, LANES), lambda i: (jnp.maximum(i - 2, 0), 0, 0)),
        scratch_shapes=[
            pltpu.VMEM((vocab, width), BF),
            pltpu.VMEM((STREAMS, 2 * HALO, LANES), F32),
            pltpu.VMEM((2, STREAMS, 8, LANES), F32),
            pltpu.VMEM((2, LONG_TAPS, LANES), BF),
            pltpu.VMEM((STREAMS, tokens, LANES), F32),
            pltpu.VMEM((STREAMS, tokens + 8, LANES), F32),
            pltpu.VMEM((tokens, LANES), F32),
            pltpu.VMEM((LANES, tokens + LONG_TAPS), BF),
            pltpu.VMEM((tokens, LANES), F32),
            pltpu.VMEM((tokens, LANES), F32),
            pltpu.VMEM((tokens // LONG_TAPS, LANES, LONG_TAPS), F32),
            pltpu.VMEM((STREAMS, LANES, vocab), BF),
        ],
        compiler_params=pltpu.CompilerParams(vmem_limit_bytes=GRANT),
        cost_estimate=cost(5000000000, 6000000),
        name="mixed_blocks",
    )(spot, hot, lead_hot, *tables, filt, toep)


def place_kernel(blocks_ref, out_ref, sems):
    copies = [
        pltpu.make_async_copy(
            blocks_ref.at[j], out_ref.at[:, pl.ds(j * LANES, LANES)], sems.at[j]
        )
        for j in range(blocks_ref.shape[0])
    ]
    for copy in copies:
        copy.start()
    for copy in copies:
        copy.wait()


def placed_columns(blocks):
    count, tokens, lanes = blocks.shape
    return pl.pallas_call(
        place_kernel,
        out_shape=jax.ShapeDtypeStruct((tokens, count * lanes), BF),
        in_specs=in_vmem(1),
        out_specs=pl.BlockSpec(memory_space=pl.ANY),
        scratch_shapes=[pltpu.SemaphoreType.DMA((count,))],
        compiler_params=pltpu.CompilerParams(vmem_limit_bytes=GRANT),
        cost_estimate=cost(0, 2000000),
        name="placed_columns",
    )(blocks)


def per_device(ids, embed_table, norm_gain, in_weight, in_scale, short_filter, long_filter, decay):
    tokens = ids.shape[0]
    vocab, width_local = embed_table.shape
    yh = lax.axis_index("yh")
    z = lax.axis_index("z")
    x = lax.axis_index("x")
    yl = lax.axis_index("yl")
    core = lax.axis_index("core")
    x_count = lax.axis_size("x")
    z_count = lax.axis_size("z")
    ctx = ("yh", "z", "x")
    tile = yh * x_count + x
    tiles = width_local // LANES

    load, upper, lower = payload(in_weight, ids.reshape(-1, LANES), embed_table, tiles * z_count)
    got_up = shifted(upper, ("yh", "yl"), -1)
    got_down = shifted(lower, ("yh", "yl"), 1)
    pieces = lax.all_to_all(load, ctx, 0, 0, tiled=True)

    groups = LANES // GROUP
    steps = jnp.arange(LONG_TAPS, dtype=F32)
    filt = lax.dynamic_slice_in_dim(long_filter, tile * groups, groups, 1)
    rate = lax.dynamic_slice_in_dim(decay, tile * groups, groups, 0)
    filt, rate, load = lax.optimization_barrier((filt, rate, load))
    taps = (filt * jnp.exp(-rate[None, :] * steps[:, None])).astype(BF).astype(F32)
    toep = toeplitz(jnp.pad(taps[::-1].T, ((0, 0), (1, LONG_TAPS - 1))))
    near_filter = lax.dynamic_slice_in_dim(short_filter, tile * LANES, LANES, 2)
    scale = lax.dynamic_slice_in_dim(in_scale, tile * LANES + z * GROUP, GROUP, 1)
    scale = scale.reshape(STREAMS * GROUP, 1)

    swapped, near_filter = lax.optimization_barrier((embed_table, near_filter))
    got_core = shifted(swapped, "core", 1)
    far_up = shifted(got_up, "core", 1)
    far_down = shifted(got_down, "core", 1)
    mine = yl * 2 + core
    order = jnp.stack([mine, mine ^ 1, mine ^ 2, mine ^ 3]).astype(jnp.int32)
    normed, token = normed_rows(
        order, [embed_table, got_core, got_up, got_down, far_up, far_down], norm_gain.reshape(1, -1)
    )
    pieces, toep, near_filter, token = lax.optimization_barrier(
        (pieces, toep, near_filter, token)
    )
    normed = pltpu.with_memory_space_constraint(normed, pltpu.HBM)
    piece = table_piece(normed, pieces, scale, token)
    spot = z.reshape(1).astype(jnp.int32)
    hot, lead_hot = hot_rows(spot, pieces, tiles, tokens, vocab)
    ups, downs, last = [piece], [], piece
    for step in range(4):
        if step == 3:
            ups[-1], hot, lead_hot = lax.optimization_barrier((ups[-1], hot, lead_hot))
        ups.append(shifted(ups[-1], "z", 1))
        if step < 3:
            last = shifted(last, "z", -1)
            downs.append(last)

    blocks = mixed_blocks(spot, hot, lead_hot, ups + downs[::-1], near_filter, toep)
    result = lax.all_to_all(blocks, ("yh", "x"), 0, 0, tiled=True)
    return placed_columns(result)


def solution(mesh):
    fine = Mesh(mesh.devices.reshape(2, 8, 4, 2, 2), ("yh", "z", "x", "yl", "core"))
    ctx = ("yh", "z", "x")
    tp = ("yl", "core")
    placed = (
        P(ctx),
        P(None, tp),
        P(),
        P(None, ctx, tp),
        P(None, tp),
        P(None, None, tp),
        P(None, tp),
        P(tp),
    )
    return jax.shard_map(
        per_device, mesh=fine, in_specs=placed, out_specs=P(ctx, tp), check_vma=False
    )
```

```python
import jax
import jax.numpy as jnp
import numpy as np
from jax import lax
from jax.experimental import pallas as pl
from jax.experimental.pallas import tpu as pltpu
from jax.sharding import Mesh, PartitionSpec as P

GROUP = 16
SHORT_TAPS = 7
LONG_TAPS = 128
LANES = 128
HALO = 144
GRANT = 24 * 1024 * 1024
STREAMS = 3
BF = jnp.bfloat16
F32 = jnp.float32


def shifted(value, axis, steps):
    count = lax.axis_size(axis)
    pairs = [(source, (source + steps) % count) for source in range(count)]
    return lax.ppermute(value, axis, pairs)


def peer_of(index):
    return (index % 4 * 2 + index // 32) * 8 + index // 4 % 8


def payload_kernel(
    far_weight_ref, far_ids_ref, table_ref, out_ref, upper_ref, lower_ref, weight_ref, ids_ref, sems
):
    half = upper_ref.shape[0]
    moves = [
        (far_weight_ref.at[0], weight_ref.at[0]),
        (far_weight_ref.at[1], weight_ref.at[1]),
        (far_weight_ref.at[2], weight_ref.at[2]),
        (far_ids_ref, ids_ref),
        (table_ref.at[pl.ds(0, half), :], upper_ref),
        (table_ref.at[pl.ds(half, half), :], lower_ref),
    ]
    copies = [
        pltpu.make_async_copy(source, target, sems.at[j])
        for j, (source, target) in enumerate(moves)
    ]
    for copy in copies:
        copy.start()
    for copy in copies[:4]:
        copy.wait()
    streams, rows, width = weight_ref.shape
    tiles = width // LANES
    columns = out_ref.shape[0] // tiles
    values = ids_ref[...]
    coded = jnp.where(values < 256, values, 255 - values).astype(F32)
    coded = jnp.concatenate([coded, jnp.zeros_like(coded)], axis=0)
    for tile in range(tiles):
        lanes = slice(tile * LANES, (tile + 1) * LANES)
        pair = jnp.concatenate([weight_ref[0, :, lanes], weight_ref[1, :, lanes]], axis=0)
        third = weight_ref[2, :, lanes].astype(F32)
        third = jnp.concatenate([third, pltpu.roll(third, LANES - 8, 1)], axis=0)
        pair = jnp.transpose(pair.astype(F32))
        third = jnp.transpose(third)
        for part in range(columns):
            to = peer_of((tile // 4 * columns + part) * 4 + tile % 4)
            at = part * GROUP
            out_ref[to, :GROUP, :] = pair[at : at + GROUP].astype(BF)
            out_ref[to, GROUP:, :] = jnp.concatenate([third[at : at + 8], coded], axis=0).astype(
                BF
            )
    for copy in copies[4:]:
        copy.wait()


def in_vmem(count):
    return [pl.BlockSpec(memory_space=pltpu.VMEM)] * count


def cost(flops, moved):
    return pl.CostEstimate(flops=flops, bytes_accessed=moved, transcendentals=0)


def payload(in_weight, ids_rows, embed_table, parts):
    vocab, width = embed_table.shape
    half = jax.ShapeDtypeStruct((vocab // 2, width), BF)
    return pl.pallas_call(
        payload_kernel,
        out_shape=(jax.ShapeDtypeStruct((parts, 2 * GROUP, LANES), BF), half, half),
        in_specs=[pl.BlockSpec(memory_space=pl.ANY)] * 3,
        out_specs=tuple(in_vmem(3)),
        scratch_shapes=[
            pltpu.VMEM(in_weight.shape, BF),
            pltpu.VMEM(ids_rows.shape, jnp.int32),
            pltpu.SemaphoreType.DMA((6,)),
        ],
        compiler_params=pltpu.CompilerParams(vmem_limit_bytes=66800000),
        cost_estimate=cost(0, 2900000),
        name="payload",
    )(in_weight, ids_rows, embed_table)


def norm_kernel(spot_ref, *refs):
    shards, gain_ref, out_ref, token_ref = refs[:6], refs[6], refs[7], refs[8]
    token_ref[...] = jnp.zeros_like(token_ref)
    vocab, width = shards[0].shape
    quarter = [spot_ref[j] for j in range(4)]
    chunk = 16

    for half in range(2):
        read = (shards[0], shards[1], shards[2 + half], shards[4 + half])

        def step(i, _, half=half, read=read):
            near = pl.ds(pl.multiple_of(i * chunk, chunk), chunk)
            at = pl.ds(pl.multiple_of(half * (vocab // 2) + i * chunk, chunk), chunk)
            rows = (at, at, near, near)
            squares = 0.0
            for shard, row in zip(read, rows):
                part = shard[row, :].astype(F32)
                squares = squares + jnp.sum(part * part, axis=1, keepdims=True)
            factor = lax.rsqrt(squares / (4 * width) + 1e-06)
            for j, (shard, row) in enumerate(zip(read, rows)):
                gain = gain_ref[:, pl.ds(pl.multiple_of(quarter[j] * width, LANES), width)]
                out_ref[quarter[j], at, :] = (shard[row, :].astype(F32) * factor * gain).astype(BF)
            return 0

        lax.fori_loop(0, vocab // 2 // chunk, step, 0, unroll=2)


def normed_rows(spot, shards, gain):
    vocab, width = shards[0].shape
    return pl.pallas_call(
        norm_kernel,
        out_shape=(
            jax.ShapeDtypeStruct((4, vocab, width), BF),
            jax.ShapeDtypeStruct((8, LANES), F32),
        ),
        in_specs=[pl.BlockSpec(memory_space=pltpu.SMEM)] + in_vmem(7),
        out_specs=tuple(in_vmem(2)),
        compiler_params=pltpu.CompilerParams(vmem_limit_bytes=GRANT),
        cost_estimate=cost(20 * vocab * width, 8 * 2 * vocab * width),
        name="normed_rows",
    )(spot, *shards, gain)


def table_kernel(far_ref, pieces_ref, scale_ref, _, out_ref, weight_ref, normed_ref, sems):
    quarters, _, width = normed_ref.shape
    copies = [
        pltpu.make_async_copy(far_ref.at[q], normed_ref.at[q], sems.at[q]) for q in range(quarters)
    ]
    for copy in copies:
        copy.start()
    low = lax.broadcasted_iota(jnp.int32, (GROUP, LANES), 1) < LANES // 2
    for m in range(pieces_ref.shape[0] // 2):
        lanes = slice(m * LANES, (m + 1) * LANES)
        first = pieces_ref[peer_of(2 * m), :GROUP, :].astype(F32)
        second = pieces_ref[peer_of(2 * m + 1), :GROUP, :].astype(F32)
        weight_ref[:GROUP, lanes] = jnp.where(low, first, pltpu.roll(second, 64, 1)).astype(BF)
        weight_ref[GROUP : 2 * GROUP, lanes] = jnp.where(
            low, pltpu.roll(first, 64, 1), second
        ).astype(BF)
        first = pieces_ref[peer_of(2 * m), GROUP:, :].astype(F32)[:8]
        second = pieces_ref[peer_of(2 * m + 1), GROUP:, :].astype(F32)[:8]
        third = jnp.concatenate(
            [
                jnp.where(low[:8], first, pltpu.roll(second, 64, 1)),
                jnp.where(low[:8], pltpu.roll(first, 64, 1), second),
            ],
            axis=0,
        )
        weight_ref[2 * GROUP :, lanes] = third.astype(BF)
    total = None
    for q in range(quarters):
        copies[q].wait()
        term = lax.dot_general(
            weight_ref[:, q * width : (q + 1) * width],
            normed_ref[q],
            (((1,), (1,)), ((), ())),
            preferred_element_type=F32,
        )
        total = term if total is None else total + term
    out_ref[...] = (total * scale_ref[...]).astype(BF)


def table_piece(normed, pieces, scale, token):
    quarters, vocab, width = normed.shape
    rows = STREAMS * GROUP
    return pl.pallas_call(
        table_kernel,
        out_shape=jax.ShapeDtypeStruct((rows, vocab), BF),
        in_specs=[pl.BlockSpec(memory_space=pl.ANY)] + in_vmem(3),
        out_specs=pl.BlockSpec(memory_space=pltpu.VMEM),
        scratch_shapes=[
            pltpu.VMEM((rows, quarters * width), BF),
            pltpu.VMEM(normed.shape, BF),
            pltpu.SemaphoreType.DMA((quarters,)),
        ],
        compiler_params=pltpu.CompilerParams(vmem_limit_bytes=GRANT),
        cost_estimate=cost(2 * rows * vocab * quarters * width, 5000000),
        name="table_piece",
    )(normed, pieces, scale, token)


def toeplitz_kernel(taps_ref, out_ref):
    for g in range(taps_ref.shape[0]):
        row = jnp.broadcast_to(taps_ref[g : g + 1, :], (LONG_TAPS, 2 * LONG_TAPS))
        block = pltpu.roll(row, 0, 1, stride=1, stride_axis=0)
        out_ref[g] = jnp.transpose(block).astype(BF)


def toeplitz(taps_row):
    groups = taps_row.shape[0]
    return pl.pallas_call(
        toeplitz_kernel,
        out_shape=jax.ShapeDtypeStruct((groups, 2 * LONG_TAPS, LONG_TAPS), BF),
        in_specs=in_vmem(1),
        out_specs=pl.BlockSpec(memory_space=pltpu.VMEM),
        compiler_params=pltpu.CompilerParams(vmem_limit_bytes=GRANT),
        cost_estimate=cost(2000000, 1060000),
        name="toeplitz",
    )(taps_row)


def column_of(coded):
    known = jnp.where(coded < 0.0, 255.0 - coded, coded)
    rows = known.shape[0]
    padded = jnp.concatenate([known, jnp.zeros((8 - rows, LANES), F32)], axis=0)
    return jnp.transpose(padded).astype(jnp.int32)


def one_hot(column, vocab):
    hit = column == lax.broadcasted_iota(jnp.int32, (column.shape[0], vocab), 1)
    return jnp.where(hit, 1.0, 0.0).astype(BF)


def ids_of(pieces_ref, index):
    return pieces_ref[peer_of(index), GROUP:, :].astype(F32)[8:12]


def hot_kernel(spot_ref, pieces_ref, out_ref, lead_ref):
    z = spot_ref[0]
    step = pl.program_id(0)
    devices = pieces_ref.shape[0]
    half, tokens, vocab = out_ref.shape
    lead = lead_ref.shape[0] // 2

    @pl.when(step == 0)
    def _():
        for segment in range(2):
            start = segment * (devices // 2) + z * 4
            rows = ids_of(pieces_ref, (start + devices - 1) % devices)
            column = column_of(rows[2:])
            column = jnp.concatenate([column[2 * LANES - lead :, 0:1], column[:, 1:2]], axis=0)
            lead_ref[segment * lead : (segment + 1) * lead, :] = one_hot(column, vocab)

    for block in range(half):
        index = step * half + block
        source = index // 4 * (devices // 2) + z * 4 + index % 4
        column = column_of(ids_of(pieces_ref, source))
        for j in range(tokens // LANES):
            out_ref[block, j * LANES : (j + 1) * LANES, :] = one_hot(column[:, j : j + 1], vocab)


def hot_rows(spot, pieces, blocks, tokens, vocab):
    half = 2
    return pl.pallas_call(
        hot_kernel,
        out_shape=(
            jax.ShapeDtypeStruct((blocks, tokens, vocab), BF),
            jax.ShapeDtypeStruct((2 * HALO, vocab), BF),
        ),
        grid=(blocks // half,),
        in_specs=[
            pl.BlockSpec(memory_space=pltpu.SMEM),
            pl.BlockSpec(pieces.shape, lambda i: (0, 0, 0)),
        ],
        out_specs=(
            pl.BlockSpec((half, tokens, vocab), lambda i: (i, 0, 0)),
            pl.BlockSpec((2 * HALO, vocab), lambda i: (0, 0)),
        ),
        compiler_params=pltpu.CompilerParams(vmem_limit_bytes=GRANT),
        cost_estimate=cost(5000000, 4500000),
        name="hot_rows",
    )(spot, pieces)


def mix_kernel(spot_ref, hot_ref, lead_hot_ref, *refs):
    tables = refs[:8]
    filt_ref, toep_ref, out_ref = refs[8:11]
    table_ref, lead_ref, head_ref, edge_ref = refs[11:15]
    next_ref, proj_ref, fresh_ref, inner_ref, fresh_gate_ref, gate_ref, conv_ref, flat_ref = refs[15:]
    step = pl.program_id(0)
    tokens = out_ref.shape[1]
    groups = LANES // GROUP
    margin = proj_ref.shape[1] - tokens
    lead = lead_hot_ref.shape[0] // 2
    chunk = 64

    def short(source, p, start, count):
        total = None
        for k in range(SHORT_TAPS):
            tap = filt_ref[p, k : k + 1, :]
            term = tap * source[p, start - k : start - k + count, :]
            total = term if total is None else total + term
        return total

    @pl.when(step == 0)
    def _():
        for j, piece in enumerate(tables):
            at = (spot_ref[0] + len(tables) - j) % len(tables) * GROUP
            for p in range(STREAMS):
                flat_ref[p, pl.ds(pl.multiple_of(at, GROUP), GROUP), :] = piece[
                    p * GROUP : (p + 1) * GROUP, :
                ]
        for p in range(STREAMS):
            table_ref[:, p * LANES : (p + 1) * LANES] = jnp.transpose(
                flat_ref[p].astype(F32)
            ).astype(BF)
        proj = jnp.dot(lead_hot_ref[...], table_ref[...], preferred_element_type=F32)
        for p in range(STREAMS):
            lead_ref[p] = proj[:, p * LANES : (p + 1) * LANES]
        for segment in range(2):
            for p in range(STREAMS):
                head_ref[segment, p] = lead_ref[
                    p, (segment + 1) * lead - margin : (segment + 1) * lead, :
                ]
            for at in range(0, LONG_TAPS, chunk):
                start = (segment + 1) * lead - LONG_TAPS + at
                fresh_ref[at : at + chunk, :] = short(lead_ref, 1, start, chunk) * short(
                    lead_ref, 2, start, chunk
                )
            edge_ref[segment] = jnp.transpose(fresh_ref[:LONG_TAPS, :]).astype(BF)

    count = tokens // LONG_TAPS

    def select(begin, end):
        proj = jnp.dot(hot_ref[0, begin:end, :], table_ref[...], preferred_element_type=F32)
        for p in range(STREAMS):
            next_ref[p, begin:end, :] = proj[:, p * LANES : (p + 1) * LANES]

    def filtered(at):
        left = short(proj_ref, 1, margin + at, chunk)
        right = short(proj_ref, 2, margin + at, chunk)
        fresh_ref[at : at + chunk, :] = left * right
        fresh_gate_ref[at : at + chunk, :] = short(proj_ref, 0, margin + at, chunk)

    def convolved(g):
        rows = slice(g * GROUP, (g + 1) * GROUP)
        windows = jnp.concatenate(
            [inner_ref[rows, j * LONG_TAPS : (j + 2) * LONG_TAPS] for j in range(count)], axis=0
        )
        full = jnp.dot(windows, toep_ref[g], preferred_element_type=F32)
        for j in range(count):
            conv_ref[j, rows, :] = full[j * GROUP : (j + 1) * GROUP]

    final = pl.num_programs(0) - 1

    @pl.when(step == 0)
    def _():
        select(0, tokens)

    @pl.when((step > 0) & (step < final))
    def _():
        select(0, tokens)
        for g in range(groups):
            convolved(g)
            filtered(g * chunk)

    @pl.when(step == final)
    def _():
        for g in range(groups):
            convolved(g)

    @pl.when(step >= 0)
    def _():
        starts = step % 4 == 0
        segment = jnp.minimum(step // 4, 1)
        for p in range(STREAMS):
            proj_ref[p, :margin, :] = jnp.where(
                starts, head_ref[segment, p], proj_ref[p, tokens:, :]
            )
            proj_ref[p, margin:, :] = next_ref[p]
        for j in range(count):
            at = j * LONG_TAPS
            conv = jnp.transpose(conv_ref[j])
            out_ref[0, at : at + LONG_TAPS, :] = (gate_ref[at : at + LONG_TAPS, :] * conv).astype(BF)
        starts = (step + 3) % 4 == 0
        segment = jnp.minimum((step + 3) // 4 - 1, 1)
        segment = jnp.maximum(segment, 0)
        inner_ref[:, :LONG_TAPS] = jnp.where(starts, edge_ref[segment], inner_ref[:, tokens:])
        for j in range(count):
            at = j * LONG_TAPS
            inner_ref[:, LONG_TAPS + at : 2 * LONG_TAPS + at] = jnp.transpose(
                fresh_ref[at : at + LONG_TAPS, :]
            ).astype(BF)
        gate_ref[...] = fresh_gate_ref[...]


def mixed_blocks(spot, hot, lead_hot, tables, filt, toep):
    blocks, tokens, vocab = hot.shape
    width = STREAMS * LANES

    def whole(value):
        return pl.BlockSpec(value.shape, lambda i: (0,) * value.ndim)

    return pl.pallas_call(
        mix_kernel,
        out_shape=jax.ShapeDtypeStruct((blocks, tokens, LANES), BF),
        grid=(blocks + 2,),
        in_specs=[
            pl.BlockSpec(memory_space=pltpu.SMEM),
            pl.BlockSpec((1, tokens, vocab), lambda i: (jnp.minimum(i, blocks - 1), 0, 0)),
            whole(lead_hot),
        ]
        + [whole(table) for table in tables]
        + [whole(filt), whole(toep)],
        out_specs=pl.BlockSpec((1, tokens, LANES), lambda i: (jnp.maximum(i - 2, 0), 0, 0)),
        scratch_shapes=[
            pltpu.VMEM((vocab, width), BF),
            pltpu.VMEM((STREAMS, 2 * HALO, LANES), F32),
            pltpu.VMEM((2, STREAMS, 8, LANES), F32),
            pltpu.VMEM((2, LONG_TAPS, LANES), BF),
            pltpu.VMEM((STREAMS, tokens, LANES), F32),
            pltpu.VMEM((STREAMS, tokens + 8, LANES), F32),
            pltpu.VMEM((tokens, LANES), F32),
            pltpu.VMEM((LANES, tokens + LONG_TAPS), BF),
            pltpu.VMEM((tokens, LANES), F32),
            pltpu.VMEM((tokens, LANES), F32),
            pltpu.VMEM((tokens // LONG_TAPS, LANES, LONG_TAPS), F32),
            pltpu.VMEM((STREAMS, LANES, vocab), BF),
        ],
        compiler_params=pltpu.CompilerParams(vmem_limit_bytes=GRANT),
        cost_estimate=cost(5000000000, 6000000),
        name="mixed_blocks",
    )(spot, hot, lead_hot, *tables, filt, toep)


def place_kernel(blocks_ref, out_ref, sems):
    copies = [
        pltpu.make_async_copy(
            blocks_ref.at[j], out_ref.at[:, pl.ds(j * LANES, LANES)], sems.at[j]
        )
        for j in range(blocks_ref.shape[0])
    ]
    for copy in copies:
        copy.start()
    for copy in copies:
        copy.wait()


def placed_columns(blocks):
    count, tokens, lanes = blocks.shape
    return pl.pallas_call(
        place_kernel,
        out_shape=jax.ShapeDtypeStruct((tokens, count * lanes), BF),
        in_specs=in_vmem(1),
        out_specs=pl.BlockSpec(memory_space=pl.ANY),
        scratch_shapes=[pltpu.SemaphoreType.DMA((count,))],
        compiler_params=pltpu.CompilerParams(vmem_limit_bytes=GRANT),
        cost_estimate=cost(0, 2000000),
        name="placed_columns",
    )(blocks)


def per_device(ids, embed_table, norm_gain, in_weight, in_scale, short_filter, long_filter, decay):
    tokens = ids.shape[0]
    vocab, width_local = embed_table.shape
    yh = lax.axis_index("yh")
    z = lax.axis_index("z")
    x = lax.axis_index("x")
    yl = lax.axis_index("yl")
    core = lax.axis_index("core")
    x_count = lax.axis_size("x")
    z_count = lax.axis_size("z")
    tile = yh * x_count + x
    tiles = width_local // LANES

    load, upper, lower = payload(in_weight, ids.reshape(-1, LANES), embed_table, tiles * z_count)
    got_up = shifted(upper, ("yh", "yl"), -1)
    got_down = shifted(lower, ("yh", "yl"), 1)
    pieces = lax.all_to_all(load, ("x", "yh", "z"), 0, 0, tiled=True)

    groups = LANES // GROUP
    steps = jnp.arange(LONG_TAPS, dtype=F32)
    filt = lax.dynamic_slice_in_dim(long_filter, tile * groups, groups, 1)
    rate = lax.dynamic_slice_in_dim(decay, tile * groups, groups, 0)
    filt, rate, load = lax.optimization_barrier((filt, rate, load))
    taps = (filt * jnp.exp(-rate[None, :] * steps[:, None])).astype(BF).astype(F32)
    toep = toeplitz(jnp.pad(taps[::-1].T, ((0, 0), (1, LONG_TAPS - 1))))
    near_filter = lax.dynamic_slice_in_dim(short_filter, tile * LANES, LANES, 2)
    scale = lax.dynamic_slice_in_dim(in_scale, tile * LANES + z * GROUP, GROUP, 1)
    scale = scale.reshape(STREAMS * GROUP, 1)

    swapped, near_filter = lax.optimization_barrier((embed_table, near_filter))
    got_core = shifted(swapped, "core", 1)
    far_up = shifted(got_up, "core", 1)
    far_down = shifted(got_down, "core", 1)
    mine = yl * 2 + core
    order = jnp.stack([mine, mine ^ 1, mine ^ 2, mine ^ 3]).astype(jnp.int32)
    normed, token = normed_rows(
        order, [embed_table, got_core, got_up, got_down, far_up, far_down], norm_gain.reshape(1, -1)
    )
    pieces, toep, near_filter, token = lax.optimization_barrier(
        (pieces, toep, near_filter, token)
    )
    normed = pltpu.with_memory_space_constraint(normed, pltpu.HBM)
    piece = table_piece(normed, pieces, scale, token)
    spot = z.reshape(1).astype(jnp.int32)
    hot, lead_hot = hot_rows(spot, pieces, tiles, tokens, vocab)
    ups, downs, last = [piece], [], piece
    for step in range(4):
        if step == 3:
            ups[-1], hot, lead_hot = lax.optimization_barrier((ups[-1], hot, lead_hot))
        ups.append(shifted(ups[-1], "z", 1))
        if step < 3:
            last = shifted(last, "z", -1)
            downs.append(last)

    blocks = mixed_blocks(spot, hot, lead_hot, ups + downs[::-1], near_filter, toep)
    result = lax.all_to_all(blocks, ("yh", "x"), 0, 0, tiled=True)
    return placed_columns(result)


def solution(mesh):
    fine = Mesh(mesh.devices.reshape(2, 8, 4, 2, 2), ("yh", "z", "x", "yl", "core"))
    ctx = ("yh", "z", "x")
    tp = ("yl", "core")
    placed = (
        P(ctx),
        P(None, tp),
        P(),
        P(None, ctx, tp),
        P(None, tp),
        P(None, None, tp),
        P(None, tp),
        P(tp),
    )
    return jax.shard_map(
        per_device, mesh=fine, in_specs=placed, out_specs=P(ctx, tp), check_vma=False
    )
```

```python
import jax
import jax.numpy as jnp
import numpy as np
from jax import lax
from jax.experimental import pallas as pl
from jax.experimental.pallas import tpu as pltpu
from jax.sharding import Mesh, PartitionSpec as P

GROUP = 16
SHORT_TAPS = 7
LONG_TAPS = 128
LANES = 128
HALO = 144
GRANT = 24 * 1024 * 1024
STREAMS = 3
BF = jnp.bfloat16
F32 = jnp.float32


def shifted(value, axis, steps):
    count = lax.axis_size(axis)
    pairs = [(source, (source + steps) % count) for source in range(count)]
    return lax.ppermute(value, axis, pairs)


def payload_kernel(
    far_weight_ref, far_ids_ref, table_ref, out_ref, upper_ref, lower_ref, weight_ref, ids_ref, sems
):
    half = upper_ref.shape[0]
    moves = [
        (far_weight_ref.at[0], weight_ref.at[0]),
        (far_weight_ref.at[1], weight_ref.at[1]),
        (far_weight_ref.at[2], weight_ref.at[2]),
        (far_ids_ref, ids_ref),
        (table_ref.at[pl.ds(0, half), :], upper_ref),
        (table_ref.at[pl.ds(half, half), :], lower_ref),
    ]
    copies = [
        pltpu.make_async_copy(source, target, sems.at[j])
        for j, (source, target) in enumerate(moves)
    ]
    for copy in copies:
        copy.start()
    for copy in copies[:4]:
        copy.wait()
    streams, rows, width = weight_ref.shape
    tiles = width // LANES
    columns = out_ref.shape[0] // tiles
    values = ids_ref[...]
    coded = jnp.where(values < 256, values, 255 - values).astype(F32)
    coded = jnp.concatenate([coded, jnp.zeros_like(coded)], axis=0)
    for tile in range(tiles):
        lanes = slice(tile * LANES, (tile + 1) * LANES)
        pair = jnp.concatenate([weight_ref[0, :, lanes], weight_ref[1, :, lanes]], axis=0)
        third = weight_ref[2, :, lanes].astype(F32)
        third = jnp.concatenate([third, pltpu.roll(third, LANES - 8, 1)], axis=0)
        pair = jnp.transpose(pair.astype(F32))
        third = jnp.transpose(third)
        for part in range(columns):
            to = (tile // 4 * columns + part) * 4 + tile % 4
            at = part * GROUP
            out_ref[to, :GROUP, :] = pair[at : at + GROUP].astype(BF)
            out_ref[to, GROUP:, :] = jnp.concatenate([third[at : at + 8], coded], axis=0).astype(
                BF
            )
    for copy in copies[4:]:
        copy.wait()


def in_vmem(count):
    return [pl.BlockSpec(memory_space=pltpu.VMEM)] * count


def cost(flops, moved):
    return pl.CostEstimate(flops=flops, bytes_accessed=moved, transcendentals=0)


def payload(in_weight, ids_rows, embed_table, parts):
    vocab, width = embed_table.shape
    half = jax.ShapeDtypeStruct((vocab // 2, width), BF)
    return pl.pallas_call(
        payload_kernel,
        out_shape=(jax.ShapeDtypeStruct((parts, 2 * GROUP, LANES), BF), half, half),
        in_specs=[pl.BlockSpec(memory_space=pl.ANY)] * 3,
        out_specs=tuple(in_vmem(3)),
        scratch_shapes=[
            pltpu.VMEM(in_weight.shape, BF),
            pltpu.VMEM(ids_rows.shape, jnp.int32),
            pltpu.SemaphoreType.DMA((6,)),
        ],
        compiler_params=pltpu.CompilerParams(vmem_limit_bytes=GRANT),
        cost_estimate=cost(0, 2900000),
        name="payload",
    )(in_weight, ids_rows, embed_table)


def norm_kernel(spot_ref, *refs):
    shards, gain_ref, out_ref, token_ref = refs[:6], refs[6], refs[7], refs[8]
    token_ref[...] = jnp.zeros_like(token_ref)
    vocab, width = shards[0].shape
    quarter = [spot_ref[j] for j in range(4)]
    chunk = 16

    for half in range(2):
        read = (shards[0], shards[1], shards[2 + half], shards[4 + half])

        def step(i, _, half=half, read=read):
            near = pl.ds(pl.multiple_of(i * chunk, chunk), chunk)
            at = pl.ds(pl.multiple_of(half * (vocab // 2) + i * chunk, chunk), chunk)
            rows = (at, at, near, near)
            squares = 0.0
            for shard, row in zip(read, rows):
                part = shard[row, :].astype(F32)
                squares = squares + jnp.sum(part * part, axis=1, keepdims=True)
            factor = lax.rsqrt(squares / (4 * width) + 1e-06)
            for j, (shard, row) in enumerate(zip(read, rows)):
                gain = gain_ref[:, pl.ds(pl.multiple_of(quarter[j] * width, LANES), width)]
                out_ref[quarter[j], at, :] = (shard[row, :].astype(F32) * factor * gain).astype(BF)
            return 0

        lax.fori_loop(0, vocab // 2 // chunk, step, 0, unroll=2)


def normed_rows(spot, shards, gain):
    vocab, width = shards[0].shape
    return pl.pallas_call(
        norm_kernel,
        out_shape=(
            jax.ShapeDtypeStruct((4, vocab, width), BF),
            jax.ShapeDtypeStruct((8, LANES), F32),
        ),
        in_specs=[pl.BlockSpec(memory_space=pltpu.SMEM)] + in_vmem(7),
        out_specs=tuple(in_vmem(2)),
        compiler_params=pltpu.CompilerParams(vmem_limit_bytes=GRANT),
        cost_estimate=cost(20 * vocab * width, 8 * 2 * vocab * width),
        name="normed_rows",
    )(spot, *shards, gain)


def table_kernel(far_ref, pieces_ref, scale_ref, _, out_ref, weight_ref, normed_ref, sems):
    quarters, _, width = normed_ref.shape
    copies = [
        pltpu.make_async_copy(far_ref.at[q], normed_ref.at[q], sems.at[q]) for q in range(quarters)
    ]
    for copy in copies:
        copy.start()
    low = lax.broadcasted_iota(jnp.int32, (GROUP, LANES), 1) < LANES // 2
    for m in range(pieces_ref.shape[0] // 2):
        lanes = slice(m * LANES, (m + 1) * LANES)
        first = pieces_ref[2 * m, :GROUP, :].astype(F32)
        second = pieces_ref[2 * m + 1, :GROUP, :].astype(F32)
        weight_ref[:GROUP, lanes] = jnp.where(low, first, pltpu.roll(second, 64, 1)).astype(BF)
        weight_ref[GROUP : 2 * GROUP, lanes] = jnp.where(
            low, pltpu.roll(first, 64, 1), second
        ).astype(BF)
        first = pieces_ref[2 * m, GROUP:, :].astype(F32)[:8]
        second = pieces_ref[2 * m + 1, GROUP:, :].astype(F32)[:8]
        third = jnp.concatenate(
            [
                jnp.where(low[:8], first, pltpu.roll(second, 64, 1)),
                jnp.where(low[:8], pltpu.roll(first, 64, 1), second),
            ],
            axis=0,
        )
        weight_ref[2 * GROUP :, lanes] = third.astype(BF)
    total = None
    for q in range(quarters):
        copies[q].wait()
        term = lax.dot_general(
            weight_ref[:, q * width : (q + 1) * width],
            normed_ref[q],
            (((1,), (1,)), ((), ())),
            preferred_element_type=F32,
        )
        total = term if total is None else total + term
    out_ref[...] = (total * scale_ref[...]).astype(BF)


def table_piece(normed, pieces, scale, token):
    quarters, vocab, width = normed.shape
    rows = STREAMS * GROUP
    return pl.pallas_call(
        table_kernel,
        out_shape=jax.ShapeDtypeStruct((rows, vocab), BF),
        in_specs=[pl.BlockSpec(memory_space=pl.ANY)] + in_vmem(3),
        out_specs=pl.BlockSpec(memory_space=pltpu.VMEM),
        scratch_shapes=[
            pltpu.VMEM((rows, quarters * width), BF),
            pltpu.VMEM(normed.shape, BF),
            pltpu.SemaphoreType.DMA((quarters,)),
        ],
        compiler_params=pltpu.CompilerParams(vmem_limit_bytes=GRANT),
        cost_estimate=cost(2 * rows * vocab * quarters * width, 5000000),
        name="table_piece",
    )(normed, pieces, scale, token)


def toeplitz_kernel(taps_ref, out_ref):
    for g in range(taps_ref.shape[0]):
        row = jnp.broadcast_to(taps_ref[g : g + 1, :], (LONG_TAPS, 2 * LONG_TAPS))
        block = pltpu.roll(row, 0, 1, stride=1, stride_axis=0)
        out_ref[g] = jnp.transpose(block).astype(BF)


def toeplitz(taps_row):
    groups = taps_row.shape[0]
    return pl.pallas_call(
        toeplitz_kernel,
        out_shape=jax.ShapeDtypeStruct((groups, 2 * LONG_TAPS, LONG_TAPS), BF),
        in_specs=in_vmem(1),
        out_specs=pl.BlockSpec(memory_space=pltpu.VMEM),
        compiler_params=pltpu.CompilerParams(vmem_limit_bytes=GRANT),
        cost_estimate=cost(2000000, 1060000),
        name="toeplitz",
    )(taps_row)


def column_of(coded):
    known = jnp.where(coded < 0.0, 255.0 - coded, coded)
    rows = known.shape[0]
    padded = jnp.concatenate([known, jnp.zeros((8 - rows, LANES), F32)], axis=0)
    return jnp.transpose(padded).astype(jnp.int32)


def one_hot(column, vocab):
    hit = column == lax.broadcasted_iota(jnp.int32, (column.shape[0], vocab), 1)
    return jnp.where(hit, 1.0, 0.0).astype(BF)


def ids_of(pieces_ref, index):
    return pieces_ref[index, GROUP:, :].astype(F32)[8:12]


def hot_kernel(spot_ref, pieces_ref, out_ref, lead_ref):
    z = spot_ref[0]
    step = pl.program_id(0)
    devices = pieces_ref.shape[0]
    half, tokens, vocab = out_ref.shape
    lead = lead_ref.shape[0] // 2

    @pl.when(step == 0)
    def _():
        for segment in range(2):
            start = segment * (devices // 2) + z * 4
            rows = ids_of(pieces_ref, (start + devices - 1) % devices)
            column = column_of(rows[2:])
            column = jnp.concatenate([column[2 * LANES - lead :, 0:1], column[:, 1:2]], axis=0)
            lead_ref[segment * lead : (segment + 1) * lead, :] = one_hot(column, vocab)

    for block in range(half):
        index = step * half + block
        source = index // 4 * (devices // 2) + z * 4 + index % 4
        column = column_of(ids_of(pieces_ref, source))
        for j in range(tokens // LANES):
            out_ref[block, j * LANES : (j + 1) * LANES, :] = one_hot(column[:, j : j + 1], vocab)


def hot_rows(spot, pieces, blocks, tokens, vocab):
    half = 2
    return pl.pallas_call(
        hot_kernel,
        out_shape=(
            jax.ShapeDtypeStruct((blocks, tokens, vocab), BF),
            jax.ShapeDtypeStruct((2 * HALO, vocab), BF),
        ),
        grid=(blocks // half,),
        in_specs=[
            pl.BlockSpec(memory_space=pltpu.SMEM),
            pl.BlockSpec(pieces.shape, lambda i: (0, 0, 0)),
        ],
        out_specs=(
            pl.BlockSpec((half, tokens, vocab), lambda i: (i, 0, 0)),
            pl.BlockSpec((2 * HALO, vocab), lambda i: (0, 0)),
        ),
        compiler_params=pltpu.CompilerParams(vmem_limit_bytes=GRANT),
        cost_estimate=cost(5000000, 4500000),
        name="hot_rows",
    )(spot, pieces)


def mix_kernel(spot_ref, hot_ref, lead_hot_ref, *refs):
    tables = refs[:8]
    filt_ref, toep_ref, out_ref = refs[8:11]
    table_ref, lead_ref, head_ref, edge_ref = refs[11:15]
    next_ref, proj_ref, fresh_ref, inner_ref, fresh_gate_ref, gate_ref, conv_ref, flat_ref = refs[15:]
    step = pl.program_id(0)
    tokens = out_ref.shape[1]
    groups = LANES // GROUP
    margin = proj_ref.shape[1] - tokens
    lead = lead_hot_ref.shape[0] // 2
    chunk = 64

    def short(source, p, start, count):
        total = None
        for k in range(SHORT_TAPS):
            tap = filt_ref[p, k : k + 1, :]
            term = tap * source[p, start - k : start - k + count, :]
            total = term if total is None else total + term
        return total

    @pl.when(step == 0)
    def _():
        for j, piece in enumerate(tables):
            at = (spot_ref[0] + len(tables) - j) % len(tables) * GROUP
            for p in range(STREAMS):
                flat_ref[p, pl.ds(pl.multiple_of(at, GROUP), GROUP), :] = piece[
                    p * GROUP : (p + 1) * GROUP, :
                ]
        for p in range(STREAMS):
            table_ref[:, p * LANES : (p + 1) * LANES] = jnp.transpose(
                flat_ref[p].astype(F32)
            ).astype(BF)
        proj = jnp.dot(lead_hot_ref[...], table_ref[...], preferred_element_type=F32)
        for p in range(STREAMS):
            lead_ref[p] = proj[:, p * LANES : (p + 1) * LANES]
        for segment in range(2):
            for p in range(STREAMS):
                head_ref[segment, p] = lead_ref[
                    p, (segment + 1) * lead - margin : (segment + 1) * lead, :
                ]
            for at in range(0, LONG_TAPS, chunk):
                start = (segment + 1) * lead - LONG_TAPS + at
                fresh_ref[at : at + chunk, :] = short(lead_ref, 1, start, chunk) * short(
                    lead_ref, 2, start, chunk
                )
            edge_ref[segment] = jnp.transpose(fresh_ref[:LONG_TAPS, :]).astype(BF)

    count = tokens // LONG_TAPS

    def select(begin, end):
        proj = jnp.dot(hot_ref[0, begin:end, :], table_ref[...], preferred_element_type=F32)
        for p in range(STREAMS):
            next_ref[p, begin:end, :] = proj[:, p * LANES : (p + 1) * LANES]

    def filtered(at):
        left = short(proj_ref, 1, margin + at, chunk)
        right = short(proj_ref, 2, margin + at, chunk)
        fresh_ref[at : at + chunk, :] = left * right
        fresh_gate_ref[at : at + chunk, :] = short(proj_ref, 0, margin + at, chunk)

    def convolved(g):
        rows = slice(g * GROUP, (g + 1) * GROUP)
        windows = jnp.concatenate(
            [inner_ref[rows, j * LONG_TAPS : (j + 2) * LONG_TAPS] for j in range(count)], axis=0
        )
        full = jnp.dot(windows, toep_ref[g], preferred_element_type=F32)
        for j in range(count):
            conv_ref[j, rows, :] = full[j * GROUP : (j + 1) * GROUP]

    final = pl.num_programs(0) - 1

    @pl.when(step == 0)
    def _():
        select(0, tokens)

    @pl.when((step > 0) & (step < final))
    def _():
        select(0, tokens)
        for g in range(groups):
            convolved(g)
            filtered(g * chunk)

    @pl.when(step == final)
    def _():
        for g in range(groups):
            convolved(g)

    @pl.when(step >= 0)
    def _():
        starts = step % 4 == 0
        segment = jnp.minimum(step // 4, 1)
        for p in range(STREAMS):
            proj_ref[p, :margin, :] = jnp.where(
                starts, head_ref[segment, p], proj_ref[p, tokens:, :]
            )
            proj_ref[p, margin:, :] = next_ref[p]
        for j in range(count):
            at = j * LONG_TAPS
            conv = jnp.transpose(conv_ref[j])
            out_ref[0, at : at + LONG_TAPS, :] = (gate_ref[at : at + LONG_TAPS, :] * conv).astype(BF)
        starts = (step + 3) % 4 == 0
        segment = jnp.minimum((step + 3) // 4 - 1, 1)
        segment = jnp.maximum(segment, 0)
        inner_ref[:, :LONG_TAPS] = jnp.where(starts, edge_ref[segment], inner_ref[:, tokens:])
        for j in range(count):
            at = j * LONG_TAPS
            inner_ref[:, LONG_TAPS + at : 2 * LONG_TAPS + at] = jnp.transpose(
                fresh_ref[at : at + LONG_TAPS, :]
            ).astype(BF)
        gate_ref[...] = fresh_gate_ref[...]


def mixed_blocks(spot, hot, lead_hot, tables, filt, toep):
    blocks, tokens, vocab = hot.shape
    width = STREAMS * LANES

    def whole(value):
        return pl.BlockSpec(value.shape, lambda i: (0,) * value.ndim)

    return pl.pallas_call(
        mix_kernel,
        out_shape=jax.ShapeDtypeStruct((blocks, tokens, LANES), BF),
        grid=(blocks + 2,),
        in_specs=[
            pl.BlockSpec(memory_space=pltpu.SMEM),
            pl.BlockSpec((1, tokens, vocab), lambda i: (jnp.minimum(i, blocks - 1), 0, 0)),
            whole(lead_hot),
        ]
        + [whole(table) for table in tables]
        + [whole(filt), whole(toep)],
        out_specs=pl.BlockSpec((1, tokens, LANES), lambda i: (jnp.maximum(i - 2, 0), 0, 0)),
        scratch_shapes=[
            pltpu.VMEM((vocab, width), BF),
            pltpu.VMEM((STREAMS, 2 * HALO, LANES), F32),
            pltpu.VMEM((2, STREAMS, 8, LANES), F32),
            pltpu.VMEM((2, LONG_TAPS, LANES), BF),
            pltpu.VMEM((STREAMS, tokens, LANES), F32),
            pltpu.VMEM((STREAMS, tokens + 8, LANES), F32),
            pltpu.VMEM((tokens, LANES), F32),
            pltpu.VMEM((LANES, tokens + LONG_TAPS), BF),
            pltpu.VMEM((tokens, LANES), F32),
            pltpu.VMEM((tokens, LANES), F32),
            pltpu.VMEM((tokens // LONG_TAPS, LANES, LONG_TAPS), F32),
            pltpu.VMEM((STREAMS, LANES, vocab), BF),
        ],
        compiler_params=pltpu.CompilerParams(vmem_limit_bytes=GRANT),
        cost_estimate=cost(5000000000, 6000000),
        name="mixed_blocks",
    )(spot, hot, lead_hot, *tables, filt, toep)


def place_kernel(blocks_ref, out_ref, sems):
    copies = [
        pltpu.make_async_copy(
            blocks_ref.at[j], out_ref.at[:, pl.ds(j * LANES, LANES)], sems.at[j]
        )
        for j in range(blocks_ref.shape[0])
    ]
    for copy in copies:
        copy.start()
    for copy in copies:
        copy.wait()


def placed_columns(blocks):
    count, tokens, lanes = blocks.shape
    return pl.pallas_call(
        place_kernel,
        out_shape=jax.ShapeDtypeStruct((tokens, count * lanes), BF),
        in_specs=in_vmem(1),
        out_specs=pl.BlockSpec(memory_space=pl.ANY),
        scratch_shapes=[pltpu.SemaphoreType.DMA((count,))],
        compiler_params=pltpu.CompilerParams(vmem_limit_bytes=GRANT),
        cost_estimate=cost(0, 2000000),
        name="placed_columns",
    )(blocks)


def per_device(ids, embed_table, norm_gain, in_weight, in_scale, short_filter, long_filter, decay):
    tokens = ids.shape[0]
    vocab, width_local = embed_table.shape
    yh = lax.axis_index("yh")
    z = lax.axis_index("z")
    x = lax.axis_index("x")
    yl = lax.axis_index("yl")
    core = lax.axis_index("core")
    x_count = lax.axis_size("x")
    z_count = lax.axis_size("z")
    ctx = ("yh", "z", "x")
    tile = yh * x_count + x
    tiles = width_local // LANES

    load, upper, lower = payload(
        pltpu.with_memory_space_constraint(in_weight, pltpu.HBM),
        pltpu.with_memory_space_constraint(ids.reshape(-1, LANES), pltpu.HBM),
        pltpu.with_memory_space_constraint(embed_table, pltpu.HBM),
        tiles * z_count,
    )
    got_up = shifted(upper, ("yh", "yl"), -1)
    got_down = shifted(lower, ("yh", "yl"), 1)
    pieces = lax.all_to_all(load, ctx, 0, 0, tiled=True)

    groups = LANES // GROUP
    steps = jnp.arange(LONG_TAPS, dtype=F32)
    filt = lax.dynamic_slice_in_dim(long_filter, tile * groups, groups, 1)
    rate = lax.dynamic_slice_in_dim(decay, tile * groups, groups, 0)
    filt, rate, load = lax.optimization_barrier((filt, rate, load))
    taps = (filt * jnp.exp(-rate[None, :] * steps[:, None])).astype(BF).astype(F32)
    toep = toeplitz(jnp.pad(taps[::-1].T, ((0, 0), (1, LONG_TAPS - 1))))
    near_filter = lax.dynamic_slice_in_dim(short_filter, tile * LANES, LANES, 2)
    scale = lax.dynamic_slice_in_dim(in_scale, tile * LANES + z * GROUP, GROUP, 1)
    scale = scale.reshape(STREAMS * GROUP, 1)

    swapped, near_filter = lax.optimization_barrier((embed_table, near_filter))
    got_core = shifted(swapped, "core", 1)
    far_up = shifted(got_up, "core", 1)
    far_down = shifted(got_down, "core", 1)
    mine = yl * 2 + core
    order = jnp.stack([mine, mine ^ 1, mine ^ 2, mine ^ 3]).astype(jnp.int32)
    normed, token = normed_rows(
        order, [embed_table, got_core, got_up, got_down, far_up, far_down], norm_gain.reshape(1, -1)
    )
    pieces, toep, near_filter, token = lax.optimization_barrier(
        (pieces, toep, near_filter, token)
    )
    normed = pltpu.with_memory_space_constraint(normed, pltpu.HBM)
    piece = table_piece(normed, pieces, scale, token)
    spot = z.reshape(1).astype(jnp.int32)
    hot, lead_hot = hot_rows(spot, pieces, tiles, tokens, vocab)
    ups, downs, last = [piece], [], piece
    for step in range(4):
        if step == 3:
            ups[-1], hot, lead_hot = lax.optimization_barrier((ups[-1], hot, lead_hot))
        ups.append(shifted(ups[-1], "z", 1))
        if step < 3:
            last = shifted(last, "z", -1)
            downs.append(last)

    blocks = mixed_blocks(spot, hot, lead_hot, ups + downs[::-1], near_filter, toep)
    result = lax.all_to_all(blocks, ("yh", "x"), 0, 0, tiled=True)
    return placed_columns(result)


def solution(mesh):
    fine = Mesh(mesh.devices.reshape(2, 8, 4, 2, 2), ("yh", "z", "x", "yl", "core"))
    ctx = ("yh", "z", "x")
    tp = ("yl", "core")
    placed = (
        P(ctx),
        P(None, tp),
        P(),
        P(None, ctx, tp),
        P(None, tp),
        P(None, None, tp),
        P(None, tp),
        P(tp),
    )
    return jax.shard_map(
        per_device, mesh=fine, in_specs=placed, out_specs=P(ctx, tp), check_vma=False
    )
```
